512 devices in a mesh: tm: 16 (over x, y), space: 32 (over z, core).
Axes of the slice: x: 4, y: 4, z: 16, core: 2. Of those that a mesh axis runs over, the one named last changes fastest.
Arguments:
- start_values: float32 [16, 256, 128, 128], P('tm', 'space'), may hold values from -6 to 6
- regions: int32 [256, 128, 128], P('space'), may hold values from 0 to 3
- resistivity: float32 [4], replicated, may hold values from 0.1 to 1
Outputs:
- slice_ends: float32 [16, 256, 128, 128], P('tm', 'space')
The draws below stay inside these ranges and needn't reach their ends.
All inputs are finite; a program needn't handle non-finite values.
Results may differ from the reference program's by a relative error of at most 0.0003.
Values sent between devices are 32-bit elements; how exact they have to be, the bound alone decides.
No kernel may reach another device: no remote copies, remote signals or barrier semaphores. Data moves between devices by JAX's collectives and lax.ppermute only.
A program may use at most 64 MiB of HBM per device.

```python
import math
import jax
import jax.numpy as jnp
from jax import lax

NY = 128
NZ = 128
STEPS = 8
REGIONS = 4
SLICES = 16
NX = 256


def plant(drawn, own_key, least, top_value):
    shape = drawn.shape
    spot = [jax.random.randint(jax.random.fold_in(own_key, axis), (), 0, shape[axis]) for axis in range(len(shape))]
    drawn = drawn.at[tuple(spot)].set(least)
    longest = shape.index(max(shape))
    spot[longest] = (spot[longest] + 1) % shape[longest]
    return drawn.at[tuple(spot)].set(top_value)


def levels(rng, dims, cuts, smallest, top_value):
    def one(axis_at, blocks):
        steps = jax.random.uniform(jax.random.fold_in(jax.random.fold_in(rng, 6), axis_at), (blocks,), jnp.float32, smallest / len(cuts), top_value / len(cuts))
        return jnp.repeat(jnp.exp(steps), dims[axis_at] // blocks).reshape((-1,) + (1,) * (len(dims) - axis_at - 1))

    loudness = one(*cuts[0])
    for cut in cuts[1:]:
        loudness = loudness * one(*cut)
    return loudness


def noise(rng, extent, spread, limit, split=(), kind=jnp.bfloat16):
    drawn = spread * jax.random.normal(rng, extent, jnp.float32)
    if split:
        drawn = drawn * levels(rng, extent, split, -0.22, 0.18)
    return jnp.clip(drawn, -limit, limit).astype(kind)


def setup_inputs(seed: int = 0) -> dict:
    arg_keys = jax.random.split(jax.random.key(seed), 4)
    return {
        "start_values": noise(arg_keys[0], (SLICES, NX, NY, NZ), 1.0, 6.0, ((0, 16), (1, 32)), jnp.float32),
        "regions": plant(jax.random.randint(arg_keys[1], (NX, NY, NZ), 0, REGIONS), jax.random.fold_in(arg_keys[1], 1), 0, REGIONS - 1).astype(jnp.int32),
        "resistivity": jnp.clip(jnp.exp(jax.random.uniform(arg_keys[2], (REGIONS,), jnp.float32, math.log(0.1), math.log(1.0))), 0.1, 1.0),
    }


fine_step = 0.008


def lookup(regions, resistivity):
    result = jnp.zeros(regions.shape, jnp.float32)
    for region in range(resistivity.shape[0]):
        result = result + jnp.where(regions == region, resistivity[region], jnp.float32(0.0))
    return result


def conduct(field_pad, resist_pad, step_size):
    squared = field_pad * field_pad
    coeff = resist_pad * (1.0 + squared / (1.0 + squared))
    center = field_pad[1:-1, 1:-1, 1:-1]
    coeff_mid = coeff[1:-1, 1:-1, 1:-1]
    flux_sum = jnp.zeros_like(center)
    for axis_dim in range(3):
        for offset in (0, 2):
            index_list = [slice(1, -1)] * 3
            index_list[axis_dim] = slice(offset, offset + center.shape[axis_dim])
            neighbor = field_pad[tuple(index_list)]
            neighbor_coeff = coeff[tuple(index_list)]
            flux_sum = flux_sum + 0.5 * (coeff_mid + neighbor_coeff) * (neighbor - center)
    return center + step_size * flux_sum


def reference(start_values, regions, resistivity):
    resist_pad = jnp.pad(lookup(regions, resistivity), 1)
    coarse_step = fine_step * STEPS

    def relax(pair):
        start, slot = pair
        field = start
        for repeat in range(STEPS):
            field = conduct(jnp.pad(field, 1), resist_pad, fine_step)
        guess = conduct(jnp.pad(start, 1), resist_pad, coarse_step)
        return jnp.where(slot == 0, field, field - guess)

    sent = lax.map(relax, (start_values, jnp.arange(SLICES, dtype=jnp.int32)))

    def chain_turn(carry, source):
        advanced = conduct(jnp.pad(carry, 1), resist_pad, coarse_step) + source
        return advanced, advanced

    final, later = lax.scan(chain_turn, sent[0], sent[1:])
    return jnp.concatenate([sent[:1], later], 0)
```

```python
import jax
import jax.numpy as jnp
from jax import lax
from jax.experimental import pallas as pl
from jax.experimental.pallas import tpu as pltpu
from jax.sharding import PartitionSpec as P

STEPS = 8
fine_step = 0.008

BX = 8
NY = 128
NZ = 128
SLICES = 16
ROWS = 8
EXT = 3 * ROWS
FIRST = 7
VMEM = pl.BlockSpec(memory_space=pltpu.VMEM)


def halo_depth(i):
    return FIRST - i if i <= FIRST else SLICES - 1 - i


def packed_tiles():
    tiles = []
    for i in range(SLICES):
        depth = halo_depth(i)
        for d in range(1, depth + 1):
            tiles.append((i, d, "mid"))
            beyond = depth - d
            if 1 <= beyond <= 4:
                tiles.append((i, d, "both"))
            elif beyond > 4:
                tiles.append((i, d, "low"))
                tiles.append((i, d, "high"))
    return tiles


TILES = packed_tiles()


def coeff(eta, u):
    return eta * (2.0 - 1.0 / (1.0 + u * u))


def z_flux(u0, k0, lane):
    up = pltpu.roll(u0, NZ - 1, 1)
    kp = pltpu.roll(k0, NZ - 1, 1)
    edge = k0 * u0
    upper = jnp.where(lane == NZ - 1, -edge, (k0 + kp) * (up - u0))
    lower = jnp.where(lane == 0, edge, pltpu.roll(upper, 1, 1))
    return upper - lower


def fine_kernel(low, own, high, out, u_ref, k_ref, e_ref, g_ref, f_ref, s_ref):
    space = lax.axis_index("space")
    lo = jnp.where(space == 0, BX, 0)
    hi = jnp.where(space == lax.axis_size("space") - 1, 2 * BX - 1, 3 * BX - 1)
    later = jnp.where(lax.axis_index("tm") == 0, 0.0, 1.0).astype(jnp.float32)
    lane = lax.broadcasted_iota(jnp.int32, (8, NZ), 1)
    sub = lax.broadcasted_iota(jnp.int32, (8, NZ), 0)
    parts = NY // 8

    for b, ref in enumerate((low, own, high)):

        def stage(x, _, b=b, ref=ref):
            for r in range(parts):
                u = ref[x, pl.ds(r, 8, stride=parts), :]
                e = ref[BX + x, pl.ds(r, 8, stride=parts), :]
                u_ref[b * BX + x, r] = u
                e_ref[b * BX + x, r] = e
                k_ref[b * BX + x, r] = coeff(e, u)
            return 0

        lax.fori_loop(0, BX, stage, 0)

    def step(first, last, emit):
        for r in range(parts):
            a = f_ref
            a[r] = (k_ref[first - 1, r] + k_ref[first, r]) * (
                u_ref[first, r] - u_ref[first - 1, r]
            )

        def plane(x, _):
            u0, k0 = u_ref[x, 0], k_ref[x, 0]
            u_end, k_end = u_ref[x, parts - 1], k_ref[x, parts - 1]
            wrap_u = jnp.where(sub == 7, 0.0, pltpu.roll(u0, 7, 0))
            wrap_k = jnp.where(sub == 7, 0.0, pltpu.roll(k0, 7, 0))
            top = (k_end + wrap_k) * (wrap_u - u_end)
            y_low = jnp.where(sub == 0, k0 * u0, pltpu.roll(top, 1, 0))
            for r in range(parts):
                if r < parts - 1:
                    u1, k1 = u_ref[x, r + 1], k_ref[x, r + 1]
                    y_up = (k0 + k1) * (u1 - u0)
                else:
                    u1 = k1 = None
                    y_up = top
                x_up = (k0 + k_ref[x + 1, r]) * (u_ref[x + 1, r] - u0)
                x_low = f_ref[r]
                f_ref[r] = x_up
                total = (x_up - x_low) + (y_up - y_low) + z_flux(u0, k0, lane)
                emit(x, r, u0, total)
                u0, k0, y_low = u1, k1, y_up
            return 0

        lax.fori_loop(first, last + 1, plane, 0)

    def keep(x, r, u0, total):
        new = u0 + total
        u_ref[x, r] = new
        k_ref[x, r] = coeff(e_ref[x, r], new)

    def keep_first(x, r, u0, total):
        g_ref[x, r] = later * (u0 + STEPS * total)
        keep(x, r, u0, total)

    def keep_last(x, r, u0, total):
        s_ref[x - BX, pl.ds(r, 8, stride=parts), :] = (u0 + total) - g_ref[x, r]

    step(jnp.maximum(1, lo), jnp.minimum(3 * BX - 2, hi), keep_first)

    def middle(t, _):
        step(jnp.maximum(t, lo), jnp.minimum(3 * BX - 1 - t, hi), keep)
        return 0

    lax.fori_loop(2, STEPS, middle, 0)
    step(BX, 2 * BX - 1, keep_last)

    def spread(x, _):
        for j in range(SLICES):
            for c in range(3):
                strip = j + c - 1
                if 0 <= strip < SLICES:
                    tile = s_ref[x, strip * ROWS : (strip + 1) * ROWS, :]
                else:
                    tile = jnp.zeros((ROWS, NZ), jnp.float32)
                out[j, x, c * ROWS : (c + 1) * ROWS, :] = tile
        return 0

    lax.fori_loop(0, BX, spread, 0)


def fine(low, own, high):
    f32 = jnp.float32
    grid = (3 * BX + 1, NY // 8, 8, NZ)
    return pl.pallas_call(
        fine_kernel,
        out_shape=jax.ShapeDtypeStruct((SLICES, BX, EXT, NZ), f32),
        in_specs=[VMEM] * 3,
        out_specs=VMEM,
        scratch_shapes=[
            pltpu.VMEM(grid, f32),
            pltpu.VMEM(grid, f32),
            pltpu.VMEM(grid, f32),
            pltpu.VMEM(grid, f32),
            pltpu.VMEM(grid[1:], f32),
            pltpu.VMEM((BX, NY, NZ), f32),
        ],
        compiler_params=pltpu.CompilerParams(vmem_limit_bytes=24 << 20),
        name="fine",
    )(low, own, high)


def pack_kernel(sent, down, up):
    row = lax.broadcasted_iota(jnp.int32, (ROWS, NZ), 0)

    def tile(i, x, c):
        return sent[i, x, c * ROWS : (c + 1) * ROWS, :]

    for n, (i, d, kind) in enumerate(TILES):
        for ref, x in ((down, d - 1), (up, BX - d)):
            if kind == "mid":
                value = tile(i, x, 1)
            elif kind == "both":
                value = jnp.where(row < 4, tile(i, x, 2), tile(i, x, 0))
            else:
                value = tile(i, x, 0 if kind == "low" else 2)
            ref[n] = value


def pack(sent):
    shape = jax.ShapeDtypeStruct((len(TILES), ROWS, NZ), jnp.float32)
    return pl.pallas_call(
        pack_kernel,
        out_shape=(shape, shape),
        in_specs=[VMEM],
        out_specs=(VMEM, VMEM),
        compiler_params=pltpu.CompilerParams(vmem_limit_bytes=8 << 20),
        name="pack",
    )(sent)


def stage_coarse(slices, low_eta, own_eta, high_eta, sent, below, above, e_ref, n_ref):
    tm = lax.axis_index("tm")
    for c in range(3):
        strip = tm + (c - 1)
        inside = jnp.where((strip >= 0) & (strip < SLICES), float(STEPS), 0.0)
        start = pl.multiple_of(jnp.clip(strip, 0, SLICES - 1) * ROWS, ROWS)
        for b, ref in enumerate((low_eta, own_eta, high_eta)):

            def one(x, _, b=b, ref=ref):
                e_ref[b * BX + x, c * ROWS : (c + 1) * ROWS, :] = (
                    inside.astype(jnp.float32) * ref[BX + x, pl.ds(start, ROWS), :]
                )
                return 0

            lax.fori_loop(0, BX, one, 0, unroll=True)

    base = slices[0]

    def own_part(i, _):
        for x in range(BX):
            for c in range(3):
                n_ref[i, BX + x, c * ROWS : (c + 1) * ROWS, :] = sent[
                    base + i, x, c * ROWS : (c + 1) * ROWS, :
                ]
        return 0

    lax.fori_loop(0, len(slices), own_part, 0)
    for n, (i, d, kind) in enumerate(TILES):
        if i not in slices:
            continue
        where = {"mid": (1,), "both": (0, 2), "low": (0,), "high": (2,)}[kind]
        for c in where:
            n_ref[i - base, BX - d, c * ROWS : (c + 1) * ROWS, :] = below[n]
            n_ref[i - base, 2 * BX - 1 + d, c * ROWS : (c + 1) * ROWS, :] = above[n]


def coarse_steps(count, base, e_ref, n_ref, u_ref, k_ref, f_ref, s_ref, out):
    space, tm = lax.axis_index("space"), lax.axis_index("tm")
    lo = jnp.where(space == 0, BX, 0)
    hi = jnp.where(space == lax.axis_size("space") - 1, 2 * BX - 1, 3 * BX - 1)
    lane = lax.broadcasted_iota(jnp.int32, (8, NZ), 1)
    sub = lax.broadcasted_iota(jnp.int32, (8, NZ), 0)
    y_lo = jnp.where(tm == 0, ROWS, 0)
    y_hi = jnp.where(tm == SLICES - 1, 2 * ROWS, EXT)
    masks = []
    for r in range(3):
        y = 3 * sub + r
        masks.append(jnp.where((y >= y_lo) & (y < y_hi), 1.0, 0.0).astype(jnp.float32))

    def setup(x, _):
        for r in range(3):
            k_ref[x, r] = coeff(e_ref[x, pl.ds(r, 8, stride=3), :], u_ref[x, r])
        return 0

    lax.fori_loop(BX - count, 2 * BX + count, setup, 0)

    for n in range(1, count + 1):
        first = jnp.maximum(BX - count + n, lo)
        last = jnp.minimum(2 * BX - 1 + count - n, hi)
        for r in range(3):
            f_ref[r] = (k_ref[first - 1, r] + k_ref[first, r]) * (
                u_ref[first, r] - u_ref[first - 1, r]
            )

        def plane(x, _, n=n):
            us = [u_ref[x, r] for r in range(3)]
            ks = [k_ref[x, r] for r in range(3)]
            us.append(pltpu.roll(us[0], 7, 0))
            ks.append(pltpu.roll(ks[0], 7, 0))
            ups = [(ks[r] + ks[r + 1]) * (us[r + 1] - us[r]) for r in range(3)]
            lows = [pltpu.roll(ups[2], 1, 0), ups[0], ups[1]]
            for r in range(3):
                u0, k0 = us[r], ks[r]
                x_up = (k0 + k_ref[x + 1, r]) * (u_ref[x + 1, r] - u0)
                x_low = f_ref[r]
                f_ref[r] = x_up
                total = (x_up - x_low) + (ups[r] - lows[r]) + z_flux(u0, k0, lane)
                new = masks[r] * (u0 + total + n_ref[base + n, x, pl.ds(r, 8, stride=3), :])
                u_ref[x, r] = new
                k_ref[x, r] = coeff(e_ref[x, pl.ds(r, 8, stride=3), :], new)
            return 0

        lax.fori_loop(first, last + 1, plane, 0)

        def emit(x, _, n=n):
            for r in range(3):
                s_ref[x, pl.ds(r, 8, stride=3), :] = u_ref[BX + x, r]
            out(n, x, s_ref[x, ROWS : 2 * ROWS, :])
            return 0

        lax.fori_loop(0, BX, emit, 0, unroll=True)


def first_kernel(
    low_eta, own_eta, high_eta, sent, below, above, out, e_ref, n_ref, u_ref, k_ref, f_ref, s_ref
):
    slices = list(range(FIRST + 1))
    stage_coarse(slices, low_eta, own_eta, high_eta, sent, below, above, e_ref, n_ref)

    def load(x, _):
        for r in range(3):
            u_ref[x, r] = n_ref[0, x, pl.ds(r, 8, stride=3), :]
        return 0

    lax.fori_loop(BX - FIRST, 2 * BX + FIRST, load, 0)
    for x in range(BX):
        out[0, x] = sent[0, x, ROWS : 2 * ROWS, :]

    def put(n, x, value):
        out[n, x] = value

    coarse_steps(FIRST, 0, e_ref, n_ref, u_ref, k_ref, f_ref, s_ref, put)


def second_kernel(
    low_eta, own_eta, high_eta, sent, below, above, low_u, own_u, high_u, done, out,
    e_ref, n_ref, u_ref, k_ref, f_ref, s_ref,
):
    slices = list(range(FIRST + 1, SLICES))
    stage_coarse(slices, low_eta, own_eta, high_eta, sent, below, above, e_ref, n_ref)
    for b, ref in enumerate((low_u, own_u, high_u)):
        for x in range(BX):
            for r in range(3):
                u_ref[b * BX + x, r] = ref[x, pl.ds(r, 8, stride=3), :]
    for i in range(FIRST + 1):
        for x in range(BX):
            out[i, x] = done[i, x]

    def put(n, x, value):
        out[FIRST + n, x] = value

    coarse_steps(len(slices), -1, e_ref, n_ref, u_ref, k_ref, f_ref, s_ref, put)


def coarse_call(kernel, name, count, *operands):
    f32 = jnp.float32
    return pl.pallas_call(
        kernel,
        out_shape=jax.ShapeDtypeStruct((count, BX, ROWS, NZ), f32),
        in_specs=[VMEM] * len(operands),
        out_specs=VMEM,
        scratch_shapes=[
            pltpu.VMEM((3 * BX + 1, EXT, NZ), f32),
            pltpu.VMEM((FIRST + 1, 3 * BX + 1, EXT, NZ), f32),
            pltpu.VMEM((3 * BX + 1, 3, 8, NZ), f32),
            pltpu.VMEM((3 * BX + 1, 3, 8, NZ), f32),
            pltpu.VMEM((3, 8, NZ), f32),
            pltpu.VMEM((BX, EXT, NZ), f32),
        ],
        compiler_params=pltpu.CompilerParams(vmem_limit_bytes=16 << 20),
        name=name,
    )(*operands)


def lookup(regions, resistivity):
    result = jnp.zeros(regions.shape, jnp.float32)
    for region in range(resistivity.shape[0]):
        result = result + jnp.where(regions == region, resistivity[region], jnp.float32(0.0))
    return result


def both_ways(down, up, axis):
    count = lax.axis_size(axis)
    forward = [(i, i + 1) for i in range(count - 1)]
    backward = [(i + 1, i) for i in range(count - 1)]
    return lax.ppermute(up, axis, forward), lax.ppermute(down, axis, backward)


def per_device(start_values, regions, resistivity):
    half = lookup(regions, resistivity) * jnp.float32(0.5 * fine_step)
    own = jnp.concatenate([start_values[0], half], axis=0)
    low, high = both_ways(own, own, "space")
    spread = fine(low, own, high)
    sent = lax.all_to_all(spread, "tm", 0, 0)
    below, above = both_ways(*pack(sent), "space")
    done = coarse_call(first_kernel, "first", FIRST + 1, low, own, high, sent, below, above)
    state = done[FIRST]
    y_low, y_high = both_ways(state, state, "tm")
    strip = jnp.concatenate([y_low, state, y_high], axis=1)
    x_low, x_high = both_ways(strip, strip, "space")
    ends = coarse_call(
        second_kernel, "second", SLICES, low, own, high, sent, below, above,
        x_low, strip, x_high, done,
    )
    result = lax.all_to_all(ends, "tm", 0, 0)
    result = jnp.transpose(result, (1, 0, 2, 3)).reshape(BX, NY, NZ)
    return result[None]


def solution(mesh):
    in_specs = (P("tm", "space", None, None), P("space", None, None), P())
    out_specs = P("tm", "space", None, None)
    return jax.shard_map(
        per_device, mesh=mesh, in_specs=in_specs, out_specs=out_specs, check_vma=False
    )
```

```python
import jax
import jax.numpy as jnp
from jax import lax
from jax.experimental import pallas as pl
from jax.experimental.pallas import tpu as pltpu
from jax.sharding import PartitionSpec as P

STEPS = 8
fine_step = 0.008

BX = 8
NY = 128
NZ = 128
SLICES = 16
REGIONS = 4
ROWS = 8
EXT = 3 * ROWS
SMEM = pl.BlockSpec(memory_space=pltpu.SMEM)
FIRST = 7
VMEM = pl.BlockSpec(memory_space=pltpu.VMEM)


def halo_depth(i):
    return FIRST - i if i <= FIRST else SLICES - 1 - i


def packed_tiles():
    tiles = []
    for i in range(SLICES):
        depth = halo_depth(i)
        for d in range(1, depth + 1):
            tiles.append((i, d, "mid"))
            beyond = depth - d
            if 1 <= beyond <= 4:
                tiles.append((i, d, "both"))
            elif beyond > 4:
                tiles.append((i, d, "low"))
                tiles.append((i, d, "high"))
    return tiles


TILES = packed_tiles()
PLACE = {}
for _n, (_i, _d, _kind) in enumerate(TILES):
    for _c in {"mid": (1,), "both": (0, 2), "low": (0,), "high": (2,)}[_kind]:
        PLACE[_i, _d, _c] = _n
PARTS = NY // 8
GROUP = 40


def coeff(eta, u):
    return eta * (2.0 - 1.0 / (1.0 + u * u))


def z_flux(u0, k0, lane):
    up = pltpu.roll(u0, NZ - 1, 1)
    kp = pltpu.roll(k0, NZ - 1, 1)
    edge = k0 * u0
    upper = jnp.where(lane == NZ - 1, -edge, (k0 + kp) * (up - u0))
    lower = jnp.where(lane == 0, edge, pltpu.roll(upper, 1, 1))
    return upper - lower


def iotas():
    shape = (8, NZ)
    return lax.broadcasted_iota(jnp.int32, shape, 1), lax.broadcasted_iota(jnp.int32, shape, 0)


def has_neighbours(axis):
    index = lax.axis_index(axis)
    below = jnp.where(index == 0, 0.0, 1.0).astype(jnp.float32)
    above = jnp.where(index == lax.axis_size(axis) - 1, 0.0, 1.0).astype(jnp.float32)
    return below, above


def own_kernel(start, regions, resistivity, out):
    scaled = [resistivity[i] * jnp.float32(0.5 * fine_step) for i in range(REGIONS)]

    def plane(x, _):
        for r in range(PARTS):
            out[x, r] = start[x, pl.ds(r, 8, stride=PARTS), :]
            region = regions[x, pl.ds(r, 8, stride=PARTS), :]
            value = jnp.zeros((8, NZ), jnp.float32)
            for i in range(REGIONS):
                value = jnp.where(region == i, scaled[i], value)
            out[BX + x, r] = value
        return 0

    lax.fori_loop(0, BX, plane, 0)


def own_part(start, regions, resistivity):
    return pl.pallas_call(
        own_kernel,
        out_shape=jax.ShapeDtypeStruct((2 * BX, PARTS, 8, NZ), jnp.float32),
        in_specs=[VMEM, VMEM, SMEM],
        out_specs=VMEM,
        compiler_params=pltpu.CompilerParams(vmem_limit_bytes=8 << 20),
        name="own",
    )(start, regions, resistivity)


def fine_kernel(low, own, high, out, u_ref, k_ref, e_ref, g_ref, f_ref, s_ref):
    below, above = has_neighbours("space")
    later = jnp.where(lax.axis_index("tm") == 0, 0.0, 1.0).astype(jnp.float32)
    lane, sub = iotas()

    for b, ref in enumerate((low, own, high)):

        def stage(x, _, b=b, ref=ref):
            for r in range(PARTS):
                u, e = ref[x, r], ref[BX + x, r]
                u_ref[b * BX + x, r] = u
                e_ref[b * BX + x, r] = e
                k_ref[b * BX + x, r] = coeff(e, u)
            return 0

        lax.fori_loop(0, BX, stage, 0)

    def plane(x, emit):
        u0, k0 = u_ref[x, 0], k_ref[x, 0]
        u_end, k_end = u_ref[x, PARTS - 1], k_ref[x, PARTS - 1]
        wrap_u = jnp.where(sub == 7, 0.0, pltpu.roll(u0, 7, 0))
        wrap_k = jnp.where(sub == 7, 0.0, pltpu.roll(k0, 7, 0))
        top = (k_end + wrap_k) * (wrap_u - u_end)
        y_low = jnp.where(sub == 0, k0 * u0, pltpu.roll(top, 1, 0))
        for r in range(PARTS):
            if r < PARTS - 1:
                u1, k1 = u_ref[x, r + 1], k_ref[x, r + 1]
                y_up = (k0 + k1) * (u1 - u0)
            else:
                u1 = k1 = None
                y_up = top
            x_up = (k0 + k_ref[x + 1, r]) * (u_ref[x + 1, r] - u0)
            x_low = f_ref[r]
            f_ref[r] = x_up
            total = (x_up - x_low) + (y_up - y_low) + z_flux(u0, k0, lane)
            emit(x, r, u0, total)
            u0, k0, y_low = u1, k1, y_up

    def step(first, pairs, emit):
        for r in range(PARTS):
            f_ref[r] = (k_ref[first - 1, r] + k_ref[first, r]) * (
                u_ref[first, r] - u_ref[first - 1, r]
            )

        def pair(n, _):
            for q in range(2):
                plane(first + 2 * n + q, emit)
            return 0

        lax.fori_loop(0, pairs, pair, 0)

    def inside(x):
        return jnp.where(x < BX, below, jnp.where(x < 2 * BX, jnp.float32(1.0), above))

    def keep(x, r, u0, total):
        new = inside(x) * (u0 + total)
        u_ref[x, r] = new
        k_ref[x, r] = coeff(e_ref[x, r], new)

    def keep_first(x, r, u0, total):
        g_ref[x, r] = later * (u0 + STEPS * total)
        keep(x, r, u0, total)

    def keep_last(x, r, u0, total):
        s_ref[x - BX, pl.ds(r, 8, stride=PARTS), :] = (u0 + total) - g_ref[x, r]

    step(1, 3 * BX // 2 - 1, keep_first)

    def middle(t, _):
        step(t, 3 * BX // 2 - t, keep)
        return 0

    lax.fori_loop(2, STEPS, middle, 0)
    step(BX, BX // 2, keep_last)

    def spread(x, _):
        for j in range(SLICES):
            for c in range(3):
                strip = j + c - 1
                if 0 <= strip < SLICES:
                    tile = s_ref[x, strip * ROWS : (strip + 1) * ROWS, :]
                else:
                    tile = jnp.zeros((ROWS, NZ), jnp.float32)
                out[j, x, c * ROWS : (c + 1) * ROWS, :] = tile
        return 0

    lax.fori_loop(0, BX, spread, 0)


def fine(low, own, high):
    f32 = jnp.float32
    grid = (3 * BX + 1, PARTS, 8, NZ)
    return pl.pallas_call(
        fine_kernel,
        out_shape=jax.ShapeDtypeStruct((SLICES, BX, EXT, NZ), f32),
        in_specs=[VMEM] * 3,
        out_specs=VMEM,
        scratch_shapes=[
            pltpu.VMEM(grid, f32),
            pltpu.VMEM(grid, f32),
            pltpu.VMEM(grid, f32),
            pltpu.VMEM(grid, f32),
            pltpu.VMEM(grid[1:], f32),
            pltpu.VMEM((BX, NY, NZ), f32),
        ],
        compiler_params=pltpu.CompilerParams(vmem_limit_bytes=24 << 20),
        name="fine",
    )(low, own, high)


def pack_kernel(sent, down, up):
    row = lax.broadcasted_iota(jnp.int32, (ROWS, NZ), 0)

    def tile(i, x, c):
        return sent[i, x, c * ROWS : (c + 1) * ROWS, :]

    for n, (i, d, kind) in enumerate(TILES):
        for ref, x in ((down, d - 1), (up, BX - d)):
            if kind == "mid":
                value = tile(i, x, 1)
            elif kind == "both":
                value = jnp.where(row < 4, tile(i, x, 2), tile(i, x, 0))
            else:
                value = tile(i, x, 0 if kind == "low" else 2)
            ref[n] = value


def pack(sent):
    shape = jax.ShapeDtypeStruct((len(TILES), ROWS, NZ), jnp.float32)
    return pl.pallas_call(
        pack_kernel,
        out_shape=(shape, shape),
        in_specs=[VMEM],
        out_specs=(VMEM, VMEM),
        compiler_params=pltpu.CompilerParams(vmem_limit_bytes=8 << 20),
        name="pack",
    )(sent)


def strip_kernel(low, own, high, out):
    tm = lax.axis_index("tm")
    for c in range(3):
        strip = tm + (c - 1)
        scale = jnp.where((strip >= 0) & (strip < SLICES), float(STEPS), 0.0).astype(jnp.float32)
        strip = jnp.clip(strip, 0, SLICES - 1)
        start = lax.rem(strip, 2) * 64 + lax.div(strip, 2)
        for b, ref in enumerate((low, own, high)):
            for x in range(BX):
                out[b * BX + x, c] = scale * ref[BX + x, pl.ds(start, 8, stride=8), :]


def strip_part(low, own, high):
    flat = [a.reshape(2 * BX, NY, NZ) for a in (low, own, high)]
    return pl.pallas_call(
        strip_kernel,
        out_shape=jax.ShapeDtypeStruct((3 * BX, 3, 8, NZ), jnp.float32),
        in_specs=[VMEM] * 3,
        out_specs=VMEM,
        compiler_params=pltpu.CompilerParams(vmem_limit_bytes=8 << 20),
        cost_estimate=pl.CostEstimate(flops=10**6, bytes_accessed=10**6, transcendentals=0),
        name="strip",
    )(*flat)


def sent_tile(refs, i, x, c):
    sent, below, above = refs
    if x < BX:
        return below[PLACE[i, BX - x, c]]
    if x >= 2 * BX:
        return above[PLACE[i, x - 2 * BX + 1, c]]
    return sent[i, x - BX, c * ROWS : (c + 1) * ROWS, :]


def coarse_steps(count, base, eta, refs, u_ref, k_ref, f_ref, out):
    lane, row = iotas()
    x_below, x_above = has_neighbours("space")
    y_below, y_above = has_neighbours("tm")
    once = jnp.where(lax.axis_index("space") < 0, 2, 1)

    def mask(x, c):
        factors = []
        if not BX <= x < 2 * BX:
            factors.append(x_below if x < BX else x_above)
        if c != 1:
            factors.append(y_below if c == 0 else y_above)
        return factors[0] * factors[1] if len(factors) == 2 else (factors or [None])[0]

    def begin(x, _):
        for c in range(3):
            k_ref[x, c] = coeff(eta[x, c], u_ref[x, c])
        return 0

    lax.fori_loop(BX - count, 2 * BX + count, begin, 0, unroll=4)

    def stretch(n, left, planes):
        def body(_, carry):
            flux = [None] * 3
            for x in planes:
                far = max(BX - x, x - (2 * BX - 1), 0)
                tiles = (0, 1, 2) if left - far >= 1 else (1,)
                us = [u_ref[x, c] for c in range(3)]
                ks = [k_ref[x, c] for c in range(3)]
                ru = [pltpu.roll(u, 7, 0) for u in us]
                rk = [pltpu.roll(k, 7, 0) for k in ks]
                ups = []
                for c in range(max(tiles) + 1):
                    un, kn = ru[c], rk[c]
                    if c < 2:
                        un = jnp.where(row == 7, ru[c + 1], un)
                        kn = jnp.where(row == 7, rk[c + 1], kn)
                    ups.append((ks[c] + kn) * (un - us[c]))
                rolled = [pltpu.roll(v, 1, 0) for v in ups]
                for c in tiles:
                    low = rolled[c]
                    if c > 0:
                        low = jnp.where(row == 0, rolled[c - 1], low)
                    u0, k0 = us[c], ks[c]
                    x_up = (k0 + k_ref[x + 1, c]) * (u_ref[x + 1, c] - u0)
                    x_low = flux[c]
                    if x_low is None:
                        if x == BX - (left if c == 1 else left - 1):
                            x_low = (k0 + k_ref[x - 1, c]) * (u0 - u_ref[x - 1, c])
                        else:
                            x_low = f_ref[c]
                    flux[c] = x_up
                    new = (u0 + (x_up - x_low) + (ups[c] - low) + z_flux(u0, k0, lane)) + (
                        sent_tile(refs, base + n, x, c)
                    )
                    m = mask(x, c)
                    if m is not None:
                        new = m * new
                    if left > 0:
                        u_ref[x, c] = new
                        k_ref[x, c] = coeff(eta[x, c], new)
                    if c == 1 and far == 0:
                        out[base + n, x - BX] = new
            for c in range(3):
                if flux[c] is not None:
                    f_ref[c] = flux[c]
            return carry

        lax.fori_loop(0, once, body, 0)

    for n in range(1, count + 1):
        left = count - n
        planes = list(range(BX - left, 2 * BX + left))
        parts = -(-len(planes) * (3 if left else 1) // GROUP)
        size = -(-len(planes) // parts)
        for a in range(0, len(planes), size):
            stretch(n, left, planes[a : a + size])


def first_kernel(eta, sent, below, above, out, u_ref, k_ref, f_ref):
    refs = (sent, below, above)
    for x in range(BX - FIRST, 2 * BX + FIRST):
        for c in range(3):
            if BX <= x < 2 * BX or c == 1 or max(BX - x, x - 2 * BX + 1) < FIRST:
                u_ref[x, c] = sent_tile(refs, 0, x, c)
            else:
                u_ref[x, c] = jnp.zeros((8, NZ), jnp.float32)
    for x in range(BX):
        out[0, x] = sent[0, x, ROWS : 2 * ROWS, :]
    coarse_steps(FIRST, 0, eta, refs, u_ref, k_ref, f_ref, out)


def second_kernel(eta, sent, below, above, low_u, own_u, high_u, done, out, u_ref, k_ref, f_ref):
    for b, ref in enumerate((low_u, own_u, high_u)):
        for x in range(BX):
            for c in range(3):
                u_ref[b * BX + x, c] = ref[x, c * ROWS : (c + 1) * ROWS, :]
    for i in range(FIRST + 1):
        for x in range(BX):
            out[i, x] = done[i, x]
    refs = (sent, below, above)
    coarse_steps(SLICES - 1 - FIRST, FIRST, eta, refs, u_ref, k_ref, f_ref, out)


def coarse_call(kernel, name, count, *operands):
    f32 = jnp.float32
    return pl.pallas_call(
        kernel,
        out_shape=jax.ShapeDtypeStruct((count, BX, ROWS, NZ), f32),
        in_specs=[VMEM] * len(operands),
        out_specs=VMEM,
        scratch_shapes=[
            pltpu.VMEM((3 * BX, 3, 8, NZ), f32),
            pltpu.VMEM((3 * BX, 3, 8, NZ), f32),
            pltpu.VMEM((3, 8, NZ), f32),
        ],
        compiler_params=pltpu.CompilerParams(vmem_limit_bytes=8 << 20),
        name=name,
    )(*operands)


def both_ways(down, up, axis):
    count = lax.axis_size(axis)
    forward = [(i, i + 1) for i in range(count - 1)]
    backward = [(i + 1, i) for i in range(count - 1)]
    return lax.ppermute(up, axis, forward), lax.ppermute(down, axis, backward)


def per_device(start_values, regions, resistivity):
    own = own_part(start_values[0], regions, resistivity)
    low, high = both_ways(own, own, "space")
    sent = lax.all_to_all(fine(low, own, high), "tm", 0, 0)
    below, above = both_ways(*pack(sent), "space")
    eta = strip_part(low, own, high)
    done = coarse_call(first_kernel, "first", FIRST + 1, eta, sent, below, above)
    state = done[FIRST]
    y_low, y_high = both_ways(state, state, "tm")
    strip = jnp.concatenate([y_low, state, y_high], axis=1)
    x_low, x_high = both_ways(strip, strip, "space")
    ends = coarse_call(
        second_kernel, "second", SLICES, eta, sent, below, above, x_low, strip, x_high, done
    )
    result = lax.all_to_all(ends, "tm", 0, 0)
    result = jnp.transpose(result, (1, 0, 2, 3)).reshape(BX, NY, NZ)
    return result[None]


def solution(mesh):
    in_specs = (P("tm", "space", None, None), P("space", None, None), P())
    out_specs = P("tm", "space", None, None)
    return jax.shard_map(
        per_device, mesh=mesh, in_specs=in_specs, out_specs=out_specs, check_vma=False
    )
```

```python
import jax
import jax.numpy as jnp
from jax import lax
from jax.experimental import pallas as pl
from jax.experimental.pallas import tpu as pltpu
from jax.sharding import PartitionSpec as P

STEPS = 8
fine_step = 0.008

BX = 8
HALF = BX // 2
NY = 128
NZ = 128
SLICES = 16
REGIONS = 4
ROWS = 8
EXT = 3 * ROWS
SMEM = pl.BlockSpec(memory_space=pltpu.SMEM)
FIRST = 7
VMEM = pl.BlockSpec(memory_space=pltpu.VMEM)


def halo_depth(i):
    return FIRST - i if i <= FIRST else SLICES - 1 - i


def packed_tiles():
    tiles = []
    for i in range(SLICES):
        depth = halo_depth(i)
        for d in range(1, depth + 1):
            tiles.append((i, d, "mid"))
            beyond = depth - d
            if 1 <= beyond <= 4:
                tiles.append((i, d, "both"))
            elif beyond > 4:
                tiles.append((i, d, "low"))
                tiles.append((i, d, "high"))
    return tiles


TILES = packed_tiles()
PLACE = {}
for _n, (_i, _d, _kind) in enumerate(TILES):
    for _c in {"mid": (1,), "both": (0, 2), "low": (0,), "high": (2,)}[_kind]:
        PLACE[_i, _d, _c] = _n
PARTS = NY // 8
GROUP = 40


def coeff(eta, u):
    return eta * (2.0 - 1.0 / (1.0 + u * u))


def z_flux(u0, k0, lane):
    up = pltpu.roll(u0, NZ - 1, 1)
    kp = pltpu.roll(k0, NZ - 1, 1)
    edge = k0 * u0
    upper = jnp.where(lane == NZ - 1, -edge, (k0 + kp) * (up - u0))
    lower = jnp.where(lane == 0, edge, pltpu.roll(upper, 1, 1))
    return upper - lower


def iotas():
    shape = (8, NZ)
    return lax.broadcasted_iota(jnp.int32, shape, 1), lax.broadcasted_iota(jnp.int32, shape, 0)


def has_neighbours(axis):
    index = lax.axis_index(axis)
    below = jnp.where(index == 0, 0.0, 1.0).astype(jnp.float32)
    above = jnp.where(index == lax.axis_size(axis) - 1, 0.0, 1.0).astype(jnp.float32)
    return below, above


def own_kernel(start, regions, resistivity, *refs):
    outs, (start_v, regions_v, resistivity_s, sems) = refs[:2], refs[2:]
    small = pltpu.make_async_copy(resistivity, resistivity_s, sems.at[4])
    small.start()
    copies = []
    for h in range(2):
        part = pl.ds(h * HALF, HALF)
        pair = (
            pltpu.make_async_copy(start.at[part], start_v.at[part], sems.at[2 * h]),
            pltpu.make_async_copy(regions.at[part], regions_v.at[part], sems.at[2 * h + 1]),
        )
        for copy in pair:
            copy.start()
        copies.append(pair)
    small.wait()
    scaled = [resistivity_s[i] * jnp.float32(0.5 * fine_step) for i in range(REGIONS)]
    for h in range(2):
        for copy in copies[h]:
            copy.wait()

        def plane(x, _, h=h):
            for r in range(PARTS):
                outs[h][x, r] = start_v[h * HALF + x, pl.ds(r, 8, stride=PARTS), :]
                region = regions_v[h * HALF + x, pl.ds(r, 8, stride=PARTS), :]
                value = jnp.zeros((8, NZ), jnp.float32)
                for i in range(REGIONS):
                    value = jnp.where(region == i, scaled[i], value)
                outs[h][HALF + x, r] = value
            return 0

        lax.fori_loop(0, HALF, plane, 0)


def own_part(start, regions, resistivity):
    hbm = pl.BlockSpec(memory_space=pltpu.MemorySpace.HBM)
    shape = jax.ShapeDtypeStruct((2 * HALF, PARTS, 8, NZ), jnp.float32)
    return pl.pallas_call(
        own_kernel,
        out_shape=(shape, shape),
        in_specs=[hbm] * 3,
        out_specs=(VMEM, VMEM),
        scratch_shapes=[
            pltpu.VMEM((BX, NY, NZ), jnp.float32),
            pltpu.VMEM((BX, NY, NZ), jnp.int32),
            pltpu.SMEM((REGIONS,), jnp.float32),
            pltpu.SemaphoreType.DMA((5,)),
        ],
        compiler_params=pltpu.CompilerParams(vmem_limit_bytes=60 << 20),
        name="own",
    )(start, regions, resistivity)


class Fine:
    def __init__(self, u_ref, k_ref, e_ref, f_ref):
        self.u, self.k, self.e, self.f = u_ref, k_ref, e_ref, f_ref
        self.below, self.above = has_neighbours("space")
        self.lane, self.sub = iotas()

    def stage(self, ref, base):
        def one(x, _):
            for r in range(PARTS):
                u, e = ref[x, r], ref[HALF + x, r]
                self.u[base + x, r] = u
                self.e[base + x, r] = e
                self.k[base + x, r] = coeff(e, u)
            return 0

        lax.fori_loop(0, HALF, one, 0)

    def plane(self, x, emit, next_u=None, next_k=None):
        u_ref, k_ref, f_ref, sub = self.u, self.k, self.f, self.sub
        if next_u is None:
            next_u, next_k = u_ref.at[x + 1], k_ref.at[x + 1]
        u0, k0 = u_ref[x, 0], k_ref[x, 0]
        u_end, k_end = u_ref[x, PARTS - 1], k_ref[x, PARTS - 1]
        wrap_u = jnp.where(sub == 7, 0.0, pltpu.roll(u0, 7, 0))
        wrap_k = jnp.where(sub == 7, 0.0, pltpu.roll(k0, 7, 0))
        top = (k_end + wrap_k) * (wrap_u - u_end)
        y_low = jnp.where(sub == 0, k0 * u0, pltpu.roll(top, 1, 0))
        for r in range(PARTS):
            if r < PARTS - 1:
                u1, k1 = u_ref[x, r + 1], k_ref[x, r + 1]
                y_up = (k0 + k1) * (u1 - u0)
            else:
                u1 = k1 = None
                y_up = top
            x_up = (k0 + next_k[r]) * (next_u[r] - u0)
            x_low = f_ref[r]
            f_ref[r] = x_up
            total = (x_up - x_low) + (y_up - y_low) + z_flux(u0, k0, self.lane)
            emit(x, r, u0, total)
            u0, k0, y_low = u1, k1, y_up

    def begin(self, x, low_u, low_k):
        for r in range(PARTS):
            self.f[r] = (low_k[r] + self.k[x, r]) * (self.u[x, r] - low_u[r])

    def pairs(self, first, count, emit):
        def pair(n, _):
            for q in range(2):
                self.plane(first + 2 * n + q, emit)
            return 0

        lax.fori_loop(0, count, pair, 0)

    def step(self, first, count, emit):
        self.begin(first, self.u.at[first - 1], self.k.at[first - 1])
        self.pairs(first, count, emit)

    def keep(self, x, r, u0, total):
        inside = jnp.where(x < BX, self.below, jnp.where(x < 2 * BX, jnp.float32(1.0), self.above))
        new = inside * (u0 + total)
        self.u[x, r] = new
        self.k[x, r] = coeff(self.e[x, r], new)


def inner_kernel(low, own_a, own_b, high, u_ref, k_ref, e_ref, g_ref, save, f_ref):
    later = jnp.where(lax.axis_index("tm") == 0, 0.0, 1.0).astype(jnp.float32)
    fine = Fine(u_ref, k_ref, e_ref, f_ref)
    for n, ref in enumerate((low, own_a, own_b, high)):
        fine.stage(ref, (n + 1) * HALF)

    def keep_first(x, r, u0, total):
        g_ref[x - HALF, r] = later * (u0 + STEPS * total)
        fine.keep(x, r, u0, total)

    def stow(t):
        for r in range(PARTS):
            save[0, t, r] = u_ref[HALF + t, r]
            save[1, t, r] = k_ref[HALF + t, r]
            save[2, t, r] = u_ref[5 * HALF - 1 - t, r]
            save[3, t, r] = k_ref[5 * HALF - 1 - t, r]

    stow(1)
    fine.step(HALF + 1, 2 * HALF - 1, keep_first)

    def later_step(t, _):
        stow(t)
        fine.step(HALF + t, 2 * HALF - t, fine.keep)
        return 0

    lax.fori_loop(2, HALF + 1, later_step, 0)


def outer_kernel(low, high, u_in, k_in, e_in, g_ref, save, out, u_ref, k_ref, e_ref, f_ref, s_ref):
    fine = Fine(u_ref, k_ref, e_ref, f_ref)
    fine.stage(low, 0)
    fine.stage(high, 5 * HALF)

    def wedges(t, _):
        fine.begin(t, u_ref.at[t - 1], k_ref.at[t - 1])
        fine.pairs(t, 1, fine.keep)
        fine.plane(t + 2, fine.keep)
        fine.plane(t + 3, fine.keep, save.at[0, t], save.at[1, t])
        fine.begin(5 * HALF - t, save.at[2, t], save.at[3, t])
        fine.pairs(5 * HALF - t, 2, fine.keep)
        return 0

    lax.fori_loop(1, HALF + 1, wedges, 0)

    def later_step(t, _):
        fine.step(t, 3 * HALF - t, fine.keep)
        return 0

    lax.fori_loop(HALF + 1, STEPS, later_step, 0)

    def keep_last(x, r, u0, total):
        s_ref[x - BX, pl.ds(r, 8, stride=PARTS), :] = (u0 + total) - g_ref[x - HALF, r]

    fine.step(BX, HALF, keep_last)

    def spread(x, _):
        for j in range(SLICES):
            for c in range(3):
                strip = j + c - 1
                if 0 <= strip < SLICES:
                    tile = s_ref[x, strip * ROWS : (strip + 1) * ROWS, :]
                else:
                    tile = jnp.zeros((ROWS, NZ), jnp.float32)
                out[j, x, c * ROWS : (c + 1) * ROWS, :] = tile
        return 0

    lax.fori_loop(0, BX, spread, 0)


GRID = jax.ShapeDtypeStruct((3 * BX + 1, PARTS, 8, NZ), jnp.float32)


def inner(low, own_a, own_b, high):
    f32 = jnp.float32
    return pl.pallas_call(
        inner_kernel,
        out_shape=(
            GRID,
            GRID,
            GRID,
            jax.ShapeDtypeStruct((4 * HALF, PARTS, 8, NZ), f32),
            jax.ShapeDtypeStruct((4, HALF + 1, PARTS, 8, NZ), f32),
        ),
        in_specs=[VMEM] * 4,
        out_specs=(VMEM,) * 5,
        scratch_shapes=[pltpu.VMEM((PARTS, 8, NZ), f32)],
        compiler_params=pltpu.CompilerParams(vmem_limit_bytes=16 << 20),
        cost_estimate=pl.CostEstimate(flops=10**8, bytes_accessed=10**7, transcendentals=0),
        name="inner",
    )(low, own_a, own_b, high)


def outer(low, high, u, k, e, g, save):
    f32 = jnp.float32
    return pl.pallas_call(
        outer_kernel,
        out_shape=(jax.ShapeDtypeStruct((SLICES, BX, EXT, NZ), f32), GRID, GRID, GRID),
        in_specs=[VMEM] * 7,
        out_specs=(VMEM,) * 4,
        scratch_shapes=[pltpu.VMEM((PARTS, 8, NZ), f32), pltpu.VMEM((BX, NY, NZ), f32)],
        input_output_aliases={2: 1, 3: 2, 4: 3},
        compiler_params=pltpu.CompilerParams(vmem_limit_bytes=16 << 20),
        name="outer",
    )(low, high, u, k, e, g, save)[0]


def pack_kernel(sent, down, up):
    row = lax.broadcasted_iota(jnp.int32, (ROWS, NZ), 0)

    def tile(i, x, c):
        return sent[i, x, c * ROWS : (c + 1) * ROWS, :]

    for n, (i, d, kind) in enumerate(TILES):
        for ref, x in ((down, d - 1), (up, BX - d)):
            if kind == "mid":
                value = tile(i, x, 1)
            elif kind == "both":
                value = jnp.where(row < 4, tile(i, x, 2), tile(i, x, 0))
            else:
                value = tile(i, x, 0 if kind == "low" else 2)
            ref[n] = value


def pack(sent):
    shape = jax.ShapeDtypeStruct((len(TILES), ROWS, NZ), jnp.float32)
    return pl.pallas_call(
        pack_kernel,
        out_shape=(shape, shape),
        in_specs=[VMEM],
        out_specs=(VMEM, VMEM),
        compiler_params=pltpu.CompilerParams(vmem_limit_bytes=8 << 20),
        name="pack",
    )(sent)


def strip_kernel(*refs):
    tm = lax.axis_index("tm")
    parts, out = refs[:-1], refs[-1]
    for c in range(3):
        strip = tm + (c - 1)
        scale = jnp.where((strip >= 0) & (strip < SLICES), float(STEPS), 0.0).astype(jnp.float32)
        strip = jnp.clip(strip, 0, SLICES - 1)
        start = lax.rem(strip, 2) * 64 + lax.div(strip, 2)
        for n, ref in enumerate(parts):
            for x in range(HALF):
                out[n * HALF + x, c] = scale * ref[HALF + x, pl.ds(start, 8, stride=8), :]


def strip_part(*parts):
    flat = [a.reshape(2 * HALF, NY, NZ) for a in parts]
    return pl.pallas_call(
        strip_kernel,
        out_shape=jax.ShapeDtypeStruct((3 * BX, 3, 8, NZ), jnp.float32),
        in_specs=[VMEM] * len(parts),
        out_specs=VMEM,
        compiler_params=pltpu.CompilerParams(vmem_limit_bytes=8 << 20),
        cost_estimate=pl.CostEstimate(flops=10**6, bytes_accessed=10**6, transcendentals=0),
        name="strip",
    )(*flat)


def sent_tile(refs, i, x, c):
    sent, below, above = refs
    if x < BX:
        return below[PLACE[i, BX - x, c]]
    if x >= 2 * BX:
        return above[PLACE[i, x - 2 * BX + 1, c]]
    return sent[i, x - BX, c * ROWS : (c + 1) * ROWS, :]


def coarse_steps(count, base, eta, refs, u_ref, k_ref, f_ref, out):
    lane, row = iotas()
    x_below, x_above = has_neighbours("space")
    y_below, y_above = has_neighbours("tm")
    once = jnp.where(lax.axis_index("space") < 0, 2, 1)

    def mask(x, c):
        factors = []
        if not BX <= x < 2 * BX:
            factors.append(x_below if x < BX else x_above)
        if c != 1:
            factors.append(y_below if c == 0 else y_above)
        return factors[0] * factors[1] if len(factors) == 2 else (factors or [None])[0]

    def begin(x, _):
        for c in range(3):
            k_ref[x, c] = coeff(eta[x, c], u_ref[x, c])
        return 0

    lax.fori_loop(BX - count, 2 * BX + count, begin, 0, unroll=4)

    def stretch(n, left, planes):
        def body(_, carry):
            flux = [None] * 3
            for x in planes:
                far = max(BX - x, x - (2 * BX - 1), 0)
                tiles = (0, 1, 2) if left - far >= 1 else (1,)
                us = [u_ref[x, c] for c in range(3)]
                ks = [k_ref[x, c] for c in range(3)]
                ru = [pltpu.roll(u, 7, 0) for u in us]
                rk = [pltpu.roll(k, 7, 0) for k in ks]
                ups = []
                for c in range(max(tiles) + 1):
                    un, kn = ru[c], rk[c]
                    if c < 2:
                        un = jnp.where(row == 7, ru[c + 1], un)
                        kn = jnp.where(row == 7, rk[c + 1], kn)
                    ups.append((ks[c] + kn) * (un - us[c]))
                rolled = [pltpu.roll(v, 1, 0) for v in ups]
                for c in tiles:
                    low = rolled[c]
                    if c > 0:
                        low = jnp.where(row == 0, rolled[c - 1], low)
                    u0, k0 = us[c], ks[c]
                    x_up = (k0 + k_ref[x + 1, c]) * (u_ref[x + 1, c] - u0)
                    x_low = flux[c]
                    if x_low is None:
                        if x == BX - (left if c == 1 else left - 1):
                            x_low = (k0 + k_ref[x - 1, c]) * (u0 - u_ref[x - 1, c])
                        else:
                            x_low = f_ref[c]
                    flux[c] = x_up
                    new = (u0 + (x_up - x_low) + (ups[c] - low) + z_flux(u0, k0, lane)) + (
                        sent_tile(refs, base + n, x, c)
                    )
                    m = mask(x, c)
                    if m is not None:
                        new = m * new
                    if left > 0:
                        u_ref[x, c] = new
                        k_ref[x, c] = coeff(eta[x, c], new)
                    if c == 1 and far == 0:
                        out[base + n, x - BX] = new
            for c in range(3):
                if flux[c] is not None:
                    f_ref[c] = flux[c]
            return carry

        lax.fori_loop(0, once, body, 0)

    for n in range(1, count + 1):
        left = count - n
        planes = list(range(BX - left, 2 * BX + left))
        parts = -(-len(planes) * (3 if left else 1) // GROUP)
        size = -(-len(planes) // parts)
        for a in range(0, len(planes), size):
            stretch(n, left, planes[a : a + size])


def first_kernel(eta, sent, below, above, out, u_ref, k_ref, f_ref):
    refs = (sent, below, above)
    for x in range(BX - FIRST, 2 * BX + FIRST):
        for c in range(3):
            if BX <= x < 2 * BX or c == 1 or max(BX - x, x - 2 * BX + 1) < FIRST:
                u_ref[x, c] = sent_tile(refs, 0, x, c)
            else:
                u_ref[x, c] = jnp.zeros((8, NZ), jnp.float32)
    for x in range(BX):
        out[0, x] = sent[0, x, ROWS : 2 * ROWS, :]
    coarse_steps(FIRST, 0, eta, refs, u_ref, k_ref, f_ref, out)


def second_kernel(eta, sent, below, above, low_u, own_u, high_u, done, out, u_ref, k_ref, f_ref):
    for b, ref in enumerate((low_u, own_u, high_u)):
        for x in range(BX):
            for c in range(3):
                u_ref[b * BX + x, c] = ref[x, c * ROWS : (c + 1) * ROWS, :]
    for i in range(FIRST + 1):
        for x in range(BX):
            out[i, x] = done[i, x]
    refs = (sent, below, above)
    coarse_steps(SLICES - 1 - FIRST, FIRST, eta, refs, u_ref, k_ref, f_ref, out)


def coarse_call(kernel, name, count, *operands):
    f32 = jnp.float32
    return pl.pallas_call(
        kernel,
        out_shape=jax.ShapeDtypeStruct((count, BX, ROWS, NZ), f32),
        in_specs=[VMEM] * len(operands),
        out_specs=VMEM,
        scratch_shapes=[
            pltpu.VMEM((3 * BX, 3, 8, NZ), f32),
            pltpu.VMEM((3 * BX, 3, 8, NZ), f32),
            pltpu.VMEM((3, 8, NZ), f32),
        ],
        compiler_params=pltpu.CompilerParams(vmem_limit_bytes=8 << 20),
        name=name,
    )(*operands)


def both_ways(down, up, axis):
    count = lax.axis_size(axis)
    forward = [(i, i + 1) for i in range(count - 1)]
    backward = [(i + 1, i) for i in range(count - 1)]
    return lax.ppermute(up, axis, forward), lax.ppermute(down, axis, backward)


def per_device(start_values, regions, resistivity):
    own_a, own_b = own_part(start_values[0], regions, resistivity)
    low_b, high_a = both_ways(own_a, own_b, "space")
    low_a, high_b = both_ways(own_b, own_a, "space")
    sent = outer(low_a, high_b, *inner(low_b, own_a, own_b, high_a))
    sent = lax.all_to_all(sent, "tm", 0, 0)
    below, above = both_ways(*pack(sent), "space")
    eta = strip_part(low_a, low_b, own_a, own_b, high_a, high_b)
    done = coarse_call(first_kernel, "first", FIRST + 1, eta, sent, below, above)
    state = done[FIRST]
    y_low, y_high = both_ways(state, state, "tm")
    strip = jnp.concatenate([y_low, state, y_high], axis=1)
    x_low, x_high = both_ways(strip, strip, "space")
    ends = coarse_call(
        second_kernel, "second", SLICES, eta, sent, below, above, x_low, strip, x_high, done
    )
    result = lax.all_to_all(ends, "tm", 0, 0)
    result = jnp.transpose(result, (1, 0, 2, 3)).reshape(BX, NY, NZ)
    return result[None]


def solution(mesh):
    in_specs = (P("tm", "space", None, None), P("space", None, None), P())
    out_specs = P("tm", "space", None, None)
    return jax.shard_map(
        per_device, mesh=mesh, in_specs=in_specs, out_specs=out_specs, check_vma=False
    )
```

```python
import jax
import jax.numpy as jnp
from jax import lax
from jax.experimental import pallas as pl
from jax.experimental.pallas import tpu as pltpu
from jax.sharding import PartitionSpec as P

STEPS = 8
fine_step = 0.008

SIDE = 4
ORDER = [a * SIDE + (b if a % 2 == 0 else SIDE - 1 - b) for a in range(SIDE) for b in range(SIDE)]
BX = 8
HALF = BX // 2
NY = 128
NZ = 128
SLICES = 16
REGIONS = 4
ROWS = 8
EXT = 3 * ROWS
SMEM = pl.BlockSpec(memory_space=pltpu.SMEM)
FIRST = 7
VMEM = pl.BlockSpec(memory_space=pltpu.VMEM)
HBM = pltpu.MemorySpace.HBM


def halo_depth(i):
    return FIRST - i if i <= FIRST else SLICES - 1 - i


def packed_tiles():
    tiles = []
    for i in range(SLICES):
        depth = halo_depth(i)
        for d in range(1, depth + 1):
            tiles.append((i, d, "mid"))
            beyond = depth - d
            if 1 <= beyond <= 4:
                tiles.append((i, d, "both"))
            elif beyond > 4:
                tiles.append((i, d, "low"))
                tiles.append((i, d, "high"))
    return tiles


TILES = packed_tiles()
PLACE = {}
for _n, (_i, _d, _kind) in enumerate(TILES):
    for _c in {"mid": (1,), "both": (0, 2), "low": (0,), "high": (2,)}[_kind]:
        PLACE[_i, _d, _c] = _n
PARTS = NY // 8
GROUP = 40


def coeff(eta, u):
    return eta * (2.0 - 1.0 / (1.0 + u * u))


def z_flux(u0, k0, lane):
    up = pltpu.roll(u0, NZ - 1, 1)
    kp = pltpu.roll(k0, NZ - 1, 1)
    edge = k0 * u0
    upper = jnp.where(lane == NZ - 1, -edge, (k0 + kp) * (up - u0))
    lower = jnp.where(lane == 0, edge, pltpu.roll(upper, 1, 1))
    return upper - lower


def strip_of(tm):
    across, along = lax.div(tm, SIDE), lax.rem(tm, SIDE)
    return across * SIDE + jnp.where(lax.rem(across, 2) == 0, along, SIDE - 1 - along)


def iotas():
    shape = (8, NZ)
    return lax.broadcasted_iota(jnp.int32, shape, 1), lax.broadcasted_iota(jnp.int32, shape, 0)


def has_neighbours(index, count):
    below = jnp.where(index == 0, 0.0, 1.0).astype(jnp.float32)
    above = jnp.where(index == count - 1, 0.0, 1.0).astype(jnp.float32)
    return below, above


def one_trip():
    return jnp.where(lax.axis_index("space") < 0, 2, 1)


def own_kernel(start, regions, resistivity, *refs):
    outs, (start_v, regions_v, resistivity_s, sems) = refs[:2], refs[2:]
    small = pltpu.make_async_copy(resistivity, resistivity_s, sems.at[4])
    small.start()
    copies = []
    for h in range(2):
        part = pl.ds(h * HALF, HALF)
        pair = (
            pltpu.make_async_copy(start.at[part], start_v.at[part], sems.at[2 * h]),
            pltpu.make_async_copy(regions.at[part], regions_v.at[part], sems.at[2 * h + 1]),
        )
        for copy in pair:
            copy.start()
        copies.append(pair)
    small.wait()
    scaled = [resistivity_s[i] * jnp.float32(0.5 * fine_step) for i in range(REGIONS)]
    for h in range(2):
        for copy in copies[h]:
            copy.wait()

        def plane(x, _, h=h):
            for r in range(PARTS):
                outs[h][x, r] = start_v[h * HALF + x, pl.ds(r, 8, stride=PARTS), :]
                region = regions_v[h * HALF + x, pl.ds(r, 8, stride=PARTS), :]
                value = jnp.zeros((8, NZ), jnp.float32)
                for i in range(REGIONS):
                    value = jnp.where(region == i, scaled[i], value)
                outs[h][HALF + x, r] = value
            return 0

        lax.fori_loop(0, HALF, plane, 0)


def own_part(start, regions, resistivity):
    hbm = pl.BlockSpec(memory_space=HBM)
    shape = jax.ShapeDtypeStruct((2 * HALF, PARTS, 8, NZ), jnp.float32)
    return pl.pallas_call(
        own_kernel,
        out_shape=(shape, shape),
        in_specs=[hbm] * 3,
        out_specs=(VMEM, VMEM),
        scratch_shapes=[
            pltpu.VMEM((BX, NY, NZ), jnp.float32),
            pltpu.VMEM((BX, NY, NZ), jnp.int32),
            pltpu.SMEM((REGIONS,), jnp.float32),
            pltpu.SemaphoreType.DMA((5,)),
        ],
        compiler_params=pltpu.CompilerParams(vmem_limit_bytes=8 << 20),
        name="own",
    )(*(pltpu.with_memory_space_constraint(a, HBM) for a in (start, regions, resistivity)))


class Fine:
    def __init__(self, u_ref, k_ref, e_ref, f_ref):
        self.u, self.k, self.e, self.f = u_ref, k_ref, e_ref, f_ref
        self.below, self.above = has_neighbours(lax.axis_index("space"), lax.axis_size("space"))
        self.lane, self.sub = iotas()

    def stage(self, ref, base):
        def one(x, _):
            for r in range(PARTS):
                u, e = ref[x, r], ref[HALF + x, r]
                self.u[base + x, r] = u
                self.e[base + x, r] = e
                self.k[base + x, r] = coeff(e, u)
            return 0

        lax.fori_loop(0, HALF, one, 0)

    def plane(self, x, emit, next_u=None, next_k=None):
        u_ref, k_ref, f_ref, sub = self.u, self.k, self.f, self.sub
        if next_u is None:
            next_u, next_k = u_ref.at[x + 1], k_ref.at[x + 1]
        u0, k0 = u_ref[x, 0], k_ref[x, 0]
        u_end, k_end = u_ref[x, PARTS - 1], k_ref[x, PARTS - 1]
        wrap_u = jnp.where(sub == 7, 0.0, pltpu.roll(u0, 7, 0))
        wrap_k = jnp.where(sub == 7, 0.0, pltpu.roll(k0, 7, 0))
        top = (k_end + wrap_k) * (wrap_u - u_end)
        y_low = jnp.where(sub == 0, k0 * u0, pltpu.roll(top, 1, 0))
        for r in range(PARTS):
            if r < PARTS - 1:
                u1, k1 = u_ref[x, r + 1], k_ref[x, r + 1]
                y_up = (k0 + k1) * (u1 - u0)
            else:
                u1 = k1 = None
                y_up = top
            x_up = (k0 + next_k[r]) * (next_u[r] - u0)
            x_low = f_ref[r]
            f_ref[r] = x_up
            total = (x_up - x_low) + (y_up - y_low) + z_flux(u0, k0, self.lane)
            emit(x, r, u0, total)
            u0, k0, y_low = u1, k1, y_up

    def begin(self, x, low_u, low_k):
        for r in range(PARTS):
            self.f[r] = (low_k[r] + self.k[x, r]) * (self.u[x, r] - low_u[r])

    def pairs(self, first, count, emit):
        def pair(n, _):
            for q in range(2):
                self.plane(first + 2 * n + q, emit)
            return 0

        lax.fori_loop(0, count, pair, 0)

    def step(self, first, count, emit):
        self.begin(first, self.u.at[first - 1], self.k.at[first - 1])
        self.pairs(first, count, emit)

    def keep(self, x, r, u0, total):
        inside = jnp.where(x < BX, self.below, jnp.where(x < 2 * BX, jnp.float32(1.0), self.above))
        new = inside * (u0 + total)
        self.u[x, r] = new
        self.k[x, r] = coeff(self.e[x, r], new)


def inner_kernel(low, own_a, own_b, high, u_ref, k_ref, e_ref, g_ref, save, f_ref):
    later = jnp.where(lax.axis_index("tm") == 0, 0.0, 1.0).astype(jnp.float32)
    fine = Fine(u_ref, k_ref, e_ref, f_ref)
    for n, ref in enumerate((low, own_a, own_b, high)):
        fine.stage(ref, (n + 1) * HALF)

    def keep_first(x, r, u0, total):
        g_ref[x - HALF, r] = later * (u0 + STEPS * total)
        fine.keep(x, r, u0, total)

    def stow(t):
        for r in range(PARTS):
            save[0, t, r] = u_ref[HALF + t, r]
            save[1, t, r] = k_ref[HALF + t, r]
            save[2, t, r] = u_ref[5 * HALF - 1 - t, r]
            save[3, t, r] = k_ref[5 * HALF - 1 - t, r]

    stow(1)
    fine.step(HALF + 1, 2 * HALF - 1, keep_first)

    def later_step(t, _):
        stow(t)
        fine.step(HALF + t, 2 * HALF - t, fine.keep)
        return 0

    lax.fori_loop(2, HALF + 1, later_step, 0)


def outer_kernel(low, high, u_in, k_in, e_in, g_ref, save, out, u_ref, k_ref, e_ref, f_ref, s_ref):
    fine = Fine(u_ref, k_ref, e_ref, f_ref)
    fine.stage(low, 0)
    fine.stage(high, 5 * HALF)

    once = one_trip()

    def wedges(t, _):
        fine.begin(t, u_ref.at[t - 1], k_ref.at[t - 1])
        fine.pairs(t, once, fine.keep)

        def last_pair(_, carry):
            fine.plane(t + 2, fine.keep)
            fine.plane(t + 3, fine.keep, save.at[0, t], save.at[1, t])
            return carry

        lax.fori_loop(0, once, last_pair, 0)
        fine.begin(5 * HALF - t, save.at[2, t], save.at[3, t])
        fine.pairs(5 * HALF - t, 2, fine.keep)
        return 0

    lax.fori_loop(1, HALF + 1, wedges, 0)

    def later_step(t, _):
        fine.step(t, 3 * HALF - t, fine.keep)
        return 0

    lax.fori_loop(HALF + 1, STEPS, later_step, 0)

    def keep_last(x, r, u0, total):
        s_ref[x - BX, pl.ds(r, 8, stride=PARTS), :] = (u0 + total) - g_ref[x - HALF, r]

    fine.step(BX, HALF, keep_last)

    def spread(x, _):
        for j in range(SLICES):
            for c in range(3):
                strip = ORDER[j] + c - 1
                if 0 <= strip < SLICES:
                    tile = s_ref[x, strip * ROWS : (strip + 1) * ROWS, :]
                else:
                    tile = jnp.zeros((ROWS, NZ), jnp.float32)
                out[j, x, c * ROWS : (c + 1) * ROWS, :] = tile
        return 0

    lax.fori_loop(0, BX, spread, 0)


GRID = jax.ShapeDtypeStruct((3 * BX + 1, PARTS, 8, NZ), jnp.float32)


def inner(low, own_a, own_b, high):
    f32 = jnp.float32
    return pl.pallas_call(
        inner_kernel,
        out_shape=(
            GRID,
            GRID,
            GRID,
            jax.ShapeDtypeStruct((4 * HALF, PARTS, 8, NZ), f32),
            jax.ShapeDtypeStruct((4, HALF + 1, PARTS, 8, NZ), f32),
        ),
        in_specs=[VMEM] * 4,
        out_specs=(VMEM,) * 5,
        scratch_shapes=[pltpu.VMEM((PARTS, 8, NZ), f32)],
        compiler_params=pltpu.CompilerParams(vmem_limit_bytes=16 << 20),
        cost_estimate=pl.CostEstimate(flops=10**8, bytes_accessed=10**7, transcendentals=0),
        name="inner",
    )(low, own_a, own_b, high)


def outer(low, high, u, k, e, g, save):
    f32 = jnp.float32
    return pl.pallas_call(
        outer_kernel,
        out_shape=(jax.ShapeDtypeStruct((SLICES, BX, EXT, NZ), f32), GRID, GRID, GRID),
        in_specs=[VMEM] * 7,
        out_specs=(VMEM,) * 4,
        scratch_shapes=[pltpu.VMEM((PARTS, 8, NZ), f32), pltpu.VMEM((BX, NY, NZ), f32)],
        input_output_aliases={2: 1, 3: 2, 4: 3},
        compiler_params=pltpu.CompilerParams(vmem_limit_bytes=16 << 20),
        name="outer",
    )(low, high, u, k, e, g, save)[0]


def pack_kernel(sent, down, up):
    row = lax.broadcasted_iota(jnp.int32, (ROWS, NZ), 0)

    def tile(i, x, c):
        return sent[i, x, c * ROWS : (c + 1) * ROWS, :]

    for n, (i, d, kind) in enumerate(TILES):
        for ref, x in ((down, d - 1), (up, BX - d)):
            if kind == "mid":
                value = tile(i, x, 1)
            elif kind == "both":
                value = jnp.where(row < 4, tile(i, x, 2), tile(i, x, 0))
            else:
                value = tile(i, x, 0 if kind == "low" else 2)
            ref[n] = value


def pack(sent):
    shape = jax.ShapeDtypeStruct((len(TILES), ROWS, NZ), jnp.float32)
    return pl.pallas_call(
        pack_kernel,
        out_shape=(shape, shape),
        in_specs=[VMEM],
        out_specs=(VMEM, VMEM),
        compiler_params=pltpu.CompilerParams(vmem_limit_bytes=8 << 20),
        name="pack",
    )(sent)


def strip_kernel(*refs):
    own = strip_of(lax.axis_index("tm"))
    parts, out = refs[:-1], refs[-1]
    for c in range(3):
        strip = own + (c - 1)
        scale = jnp.where((strip >= 0) & (strip < SLICES), float(STEPS), 0.0).astype(jnp.float32)
        strip = jnp.clip(strip, 0, SLICES - 1)
        start = lax.rem(strip, 2) * 64 + lax.div(strip, 2)
        for n, ref in enumerate(parts):
            for x in range(HALF):
                out[n * HALF + x, c] = scale * ref[HALF + x, pl.ds(start, 8, stride=8), :]


def strip_part(*parts):
    flat = [a.reshape(2 * HALF, NY, NZ) for a in parts]
    return pl.pallas_call(
        strip_kernel,
        out_shape=jax.ShapeDtypeStruct((3 * BX, 3, 8, NZ), jnp.float32),
        in_specs=[VMEM] * len(parts),
        out_specs=VMEM,
        compiler_params=pltpu.CompilerParams(vmem_limit_bytes=8 << 20),
        cost_estimate=pl.CostEstimate(flops=10**6, bytes_accessed=10**6, transcendentals=0),
        name="strip",
    )(*flat)


def sent_tile(refs, i, x, c):
    sent, below, above = refs
    if x < BX:
        return below[PLACE[i, BX - x, c]]
    if x >= 2 * BX:
        return above[PLACE[i, x - 2 * BX + 1, c]]
    return sent[i, x - BX, c * ROWS : (c + 1) * ROWS, :]


def coarse_steps(count, base, eta, refs, u_ref, k_ref, f_ref, out):
    lane, row = iotas()
    x_below, x_above = has_neighbours(lax.axis_index("space"), lax.axis_size("space"))
    y_below, y_above = has_neighbours(strip_of(lax.axis_index("tm")), SLICES)
    once = one_trip()

    def mask(x, c):
        factors = []
        if not BX <= x < 2 * BX:
            factors.append(x_below if x < BX else x_above)
        if c != 1:
            factors.append(y_below if c == 0 else y_above)
        return factors[0] * factors[1] if len(factors) == 2 else (factors or [None])[0]

    def begin(x, _):
        for c in range(3):
            k_ref[x, c] = coeff(eta[x, c], u_ref[x, c])
        return 0

    lax.fori_loop(BX - count, 2 * BX + count, begin, 0, unroll=4)

    def stretch(n, left, planes):
        def body(_, carry):
            flux = [None] * 3
            for x in planes:
                far = max(BX - x, x - (2 * BX - 1), 0)
                tiles = (0, 1, 2) if left - far >= 1 else (1,)
                us = [u_ref[x, c] for c in range(3)]
                ks = [k_ref[x, c] for c in range(3)]
                ru = [pltpu.roll(u, 7, 0) for u in us]
                rk = [pltpu.roll(k, 7, 0) for k in ks]
                ups = []
                for c in range(max(tiles) + 1):
                    un, kn = ru[c], rk[c]
                    if c < 2:
                        un = jnp.where(row == 7, ru[c + 1], un)
                        kn = jnp.where(row == 7, rk[c + 1], kn)
                    ups.append((ks[c] + kn) * (un - us[c]))
                rolled = [pltpu.roll(v, 1, 0) for v in ups]
                for c in tiles:
                    low = rolled[c]
                    if c > 0:
                        low = jnp.where(row == 0, rolled[c - 1], low)
                    u0, k0 = us[c], ks[c]
                    x_up = (k0 + k_ref[x + 1, c]) * (u_ref[x + 1, c] - u0)
                    x_low = flux[c]
                    if x_low is None:
                        if x == BX - (left if c == 1 else left - 1):
                            x_low = (k0 + k_ref[x - 1, c]) * (u0 - u_ref[x - 1, c])
                        else:
                            x_low = f_ref[c]
                    flux[c] = x_up
                    new = (u0 + (x_up - x_low) + (ups[c] - low) + z_flux(u0, k0, lane)) + (
                        sent_tile(refs, base + n, x, c)
                    )
                    m = mask(x, c)
                    if m is not None:
                        new = m * new
                    if left > 0:
                        u_ref[x, c] = new
                        k_ref[x, c] = coeff(eta[x, c], new)
                    if c == 1 and far == 0:
                        out[base + n, x - BX] = new
            for c in range(3):
                if flux[c] is not None:
                    f_ref[c] = flux[c]
            return carry

        lax.fori_loop(0, once, body, 0)

    for n in range(1, count + 1):
        left = count - n
        planes = list(range(BX - left, 2 * BX + left))
        parts = -(-len(planes) * (3 if left else 1) // GROUP)
        size = -(-len(planes) // parts)
        for a in range(0, len(planes), size):
            stretch(n, left, planes[a : a + size])


def first_kernel(eta, sent, below, above, out, u_ref, k_ref, f_ref):
    refs = (sent, below, above)
    for x in range(BX - FIRST, 2 * BX + FIRST):
        for c in range(3):
            if BX <= x < 2 * BX or c == 1 or max(BX - x, x - 2 * BX + 1) < FIRST:
                u_ref[x, c] = sent_tile(refs, 0, x, c)
            else:
                u_ref[x, c] = jnp.zeros((8, NZ), jnp.float32)
    for x in range(BX):
        out[0, x] = sent[0, x, ROWS : 2 * ROWS, :]
    coarse_steps(FIRST, 0, eta, refs, u_ref, k_ref, f_ref, out)


def second_kernel(eta, sent, below, above, low_u, own_u, high_u, done, out, u_ref, k_ref, f_ref):
    for b, ref in enumerate((low_u, own_u, high_u)):
        for x in range(BX):
            for c in range(3):
                u_ref[b * BX + x, c] = ref[x, c * ROWS : (c + 1) * ROWS, :]
    for i in range(FIRST + 1):
        for x in range(BX):
            out[i, x] = done[i, x]
    refs = (sent, below, above)
    coarse_steps(SLICES - 1 - FIRST, FIRST, eta, refs, u_ref, k_ref, f_ref, out)


def coarse_call(kernel, name, count, *operands):
    f32 = jnp.float32
    return pl.pallas_call(
        kernel,
        out_shape=jax.ShapeDtypeStruct((count, BX, ROWS, NZ), f32),
        in_specs=[VMEM] * len(operands),
        out_specs=VMEM,
        scratch_shapes=[
            pltpu.VMEM((3 * BX, 3, 8, NZ), f32),
            pltpu.VMEM((3 * BX, 3, 8, NZ), f32),
            pltpu.VMEM((3, 8, NZ), f32),
        ],
        compiler_params=pltpu.CompilerParams(vmem_limit_bytes=8 << 20),
        name=name,
    )(*operands)


def place_kernel(strips, out, sems):
    copies = [
        pltpu.make_async_copy(
            strips.at[j], out.at[:, pl.ds(ORDER[j] * ROWS, ROWS), :], sems.at[j]
        )
        for j in range(SLICES)
    ]
    for copy in copies:
        copy.start()
    for copy in copies:
        copy.wait()


def place(strips):
    return pl.pallas_call(
        place_kernel,
        out_shape=jax.ShapeDtypeStruct((BX, NY, NZ), jnp.float32),
        in_specs=[VMEM],
        out_specs=pl.BlockSpec(memory_space=HBM),
        scratch_shapes=[pltpu.SemaphoreType.DMA((SLICES,))],
        compiler_params=pltpu.CompilerParams(vmem_limit_bytes=4 << 20),
        name="place",
    )(strips)


def both_ways(down, up, axis):
    line = ORDER if axis == "tm" else range(lax.axis_size(axis))
    forward = list(zip(line[:-1], line[1:]))
    backward = [(b, a) for a, b in forward]
    return lax.ppermute(up, axis, forward), lax.ppermute(down, axis, backward)


def per_device(start_values, regions, resistivity):
    own_a, own_b = own_part(start_values[0], regions, resistivity)
    low_b, high_a = both_ways(own_a, own_b, "space")
    low_a, high_b = both_ways(own_b, own_a, "space")
    sent = outer(low_a, high_b, *inner(low_b, own_a, own_b, high_a))
    sent = lax.all_to_all(sent, "tm", 0, 0)
    below, above = both_ways(*pack(sent), "space")
    eta = strip_part(low_a, low_b, own_a, own_b, high_a, high_b)
    done = coarse_call(first_kernel, "first", FIRST + 1, eta, sent, below, above)
    state = done[FIRST]
    y_low, y_high = both_ways(state, state, "tm")
    strip = jnp.concatenate([y_low, state, y_high], axis=1)
    x_low, x_high = both_ways(strip, strip, "space")
    ends = coarse_call(
        second_kernel, "second", SLICES, eta, sent, below, above, x_low, strip, x_high, done
    )
    result = lax.all_to_all(ends, "tm", 0, 0)
    return place(result)[None]


def solution(mesh):
    in_specs = (P("tm", "space", None, None), P("space", None, None), P())
    out_specs = P("tm", "space", None, None)
    return jax.shard_map(
        per_device, mesh=mesh, in_specs=in_specs, out_specs=out_specs, check_vma=False
    )
```

```python
import jax
import jax.numpy as jnp
from jax import lax
from jax.experimental import pallas as pl
from jax.experimental.pallas import tpu as pltpu
from jax.sharding import PartitionSpec as P

STEPS = 8
fine_step = 0.008

SIDE = 4
ORDER = [a * SIDE + (b if a % 2 == 0 else SIDE - 1 - b) for a in range(SIDE) for b in range(SIDE)]
BX = 8
HALF = BX // 2
NY = 128
NZ = 128
SLICES = 16
REGIONS = 4
ROWS = 8
EXT = 3 * ROWS
SMEM = pl.BlockSpec(memory_space=pltpu.SMEM)
FIRST = 7
VMEM = pl.BlockSpec(memory_space=pltpu.VMEM)
HBM = pltpu.MemorySpace.HBM


def halo_depth(i):
    return FIRST - i if i <= FIRST else SLICES - 1 - i


def packed_tiles():
    tiles = []
    for i in range(SLICES):
        depth = halo_depth(i)
        for d in range(1, depth + 1):
            tiles.append((i, d, "mid"))
            beyond = depth - d
            if 1 <= beyond <= 4:
                tiles.append((i, d, "both"))
            elif beyond > 4:
                tiles.append((i, d, "low"))
                tiles.append((i, d, "high"))
    return tiles


TILES = packed_tiles()
PLACE = {}
for _n, (_i, _d, _kind) in enumerate(TILES):
    for _c in {"mid": (1,), "both": (0, 2), "low": (0,), "high": (2,)}[_kind]:
        PLACE[_i, _d, _c] = _n
PARTS = NY // 8
GROUP = 40


def coeff(eta, u):
    return eta * (2.0 - 1.0 / (1.0 + u * u))


def z_flux(u0, k0, lane):
    up = pltpu.roll(u0, NZ - 1, 1)
    kp = pltpu.roll(k0, NZ - 1, 1)
    edge = k0 * u0
    upper = jnp.where(lane == NZ - 1, -edge, (k0 + kp) * (up - u0))
    lower = jnp.where(lane == 0, edge, pltpu.roll(upper, 1, 1))
    return upper - lower


Q = 4
CHUNK = NZ // Q


def by_chunk(lane, values):
    low = jnp.where(lane < CHUNK, values[0], values[1])
    return jnp.where(lane < 2 * CHUNK, low, jnp.where(lane < 3 * CHUNK, values[2], values[3]))


def interleave(rows):
    lane, _ = iotas()
    turned = []
    for h in range(Q):
        source = Q * (lane & (CHUNK - 1)) + (((lane >> 5) - h) & (Q - 1))
        turned.append(jnp.take_along_axis(rows[h], source, axis=1))
    tiles = []
    for rz in range(Q):
        tile = by_chunk(lane, [turned[(c - rz) % Q] for c in range(Q)])
        tiles.append(pltpu.roll(tile, NZ - CHUNK * rz, 1) if rz else tile)
    return tiles


def separate(tiles):
    lane, _ = iotas()
    turned = [pltpu.roll(t, CHUNK * rz, 1) if rz else t for rz, t in enumerate(tiles)]
    rows = []
    for h in range(Q):
        mixed = by_chunk(lane, [turned[(c - h) % Q] for c in range(Q)])
        source = CHUNK * (((lane & (Q - 1)) + h) & (Q - 1)) + (lane >> 2)
        rows.append(jnp.take_along_axis(mixed, source, axis=1))
    return rows


def rows_at(h, ry):
    return pl.ds(CHUNK * h + ry, 8, stride=Q)


def strip_of(tm):
    across, along = lax.div(tm, SIDE), lax.rem(tm, SIDE)
    return across * SIDE + jnp.where(lax.rem(across, 2) == 0, along, SIDE - 1 - along)


def iotas():
    shape = (8, NZ)
    return lax.broadcasted_iota(jnp.int32, shape, 1), lax.broadcasted_iota(jnp.int32, shape, 0)


def has_neighbours(index, count):
    below = jnp.where(index == 0, 0.0, 1.0).astype(jnp.float32)
    above = jnp.where(index == count - 1, 0.0, 1.0).astype(jnp.float32)
    return below, above


def one_trip():
    return jnp.where(lax.axis_index("space") < 0, 2, 1)


def own_kernel(start, regions, resistivity, *refs):
    outs, (start_v, regions_v, resistivity_s, sems) = refs[:2], refs[2:]
    small = pltpu.make_async_copy(resistivity, resistivity_s, sems.at[4])
    small.start()
    copies = []
    for h in range(2):
        part = pl.ds(h * HALF, HALF)
        pair = (
            pltpu.make_async_copy(start.at[part], start_v.at[part], sems.at[2 * h]),
            pltpu.make_async_copy(regions.at[part], regions_v.at[part], sems.at[2 * h + 1]),
        )
        for copy in pair:
            copy.start()
        copies.append(pair)
    small.wait()
    scaled = [resistivity_s[i] * jnp.float32(0.5 * fine_step) for i in range(REGIONS)]
    for h in range(2):
        for copy in copies[h]:
            copy.wait()

        def planes(n, _, h=h):
            for x in (2 * n, 2 * n + 1):
                for ry in range(Q):
                    u, e = [], []
                    for g in range(Q):
                        where = rows_at(g, ry)
                        u.append(start_v[h * HALF + x, where, :])
                        region = regions_v[h * HALF + x, where, :]
                        value = jnp.zeros((8, NZ), jnp.float32)
                        for i in range(REGIONS):
                            value = jnp.where(region == i, scaled[i], value)
                        e.append(value)
                    u, e = interleave(u), interleave(e)
                    for rz in range(Q):
                        outs[h][x, Q * ry + rz] = u[rz]
                        outs[h][HALF + x, Q * ry + rz] = e[rz]
            return 0

        lax.fori_loop(0, HALF // 2, planes, 0)


def own_part(start, regions, resistivity):
    hbm = pl.BlockSpec(memory_space=HBM)
    shape = jax.ShapeDtypeStruct((2 * HALF, PARTS, 8, NZ), jnp.float32)
    return pl.pallas_call(
        own_kernel,
        out_shape=(shape, shape),
        in_specs=[hbm] * 3,
        out_specs=(VMEM, VMEM),
        scratch_shapes=[
            pltpu.VMEM((BX, NY, NZ), jnp.float32),
            pltpu.VMEM((BX, NY, NZ), jnp.int32),
            pltpu.SMEM((REGIONS,), jnp.float32),
            pltpu.SemaphoreType.DMA((5,)),
        ],
        compiler_params=pltpu.CompilerParams(vmem_limit_bytes=8 << 20),
        name="own",
    )(*(pltpu.with_memory_space_constraint(a, HBM) for a in (start, regions, resistivity)))


class Fine:
    def __init__(self, u_ref, k_ref, e_ref, f_ref):
        self.u, self.k, self.e, self.f = u_ref, k_ref, e_ref, f_ref
        self.below, self.above = has_neighbours(lax.axis_index("space"), lax.axis_size("space"))
        lane, sub = iotas()
        self.z_high, self.z_low = [(lane & (CHUNK - 1)) == v for v in (CHUNK - 1, 0)]
        self.y_high, self.y_low = sub == 7, sub == 0
        self.y_end = (sub == 7) & (lane >= NZ - CHUNK)
        self.y_start = (sub == 0) & (lane < CHUNK)

    def stage(self, ref, base):
        def one(x, _):
            for r in range(PARTS):
                u, e = ref[x, r], ref[HALF + x, r]
                self.u[base + x, r] = u
                self.e[base + x, r] = e
                self.k[base + x, r] = coeff(e, u)
            return 0

        lax.fori_loop(0, HALF, one, 0)

    def above_y(self, v):
        turned = pltpu.roll(pltpu.roll(v, NZ - CHUNK, 1), 7, 0)
        v = jnp.where(self.y_high, turned, pltpu.roll(v, 7, 0))
        return jnp.where(self.y_end, 0.0, v)

    def plane(self, x, emit, next_u=None, next_k=None):
        f_ref = self.f
        if next_u is None:
            next_u, next_k = self.u.at[x + 1], self.k.at[x + 1]

        def at(ry, rz):
            return self.u[x, Q * ry + rz], self.k[x, Q * ry + rz]

        z_ends, y_tops, y_lows = [], [], []
        for ry in range(Q):
            (u0, k0), (u3, k3) = at(ry, 0), at(ry, Q - 1)
            un, kn = pltpu.roll(u0, NZ - 1, 1), pltpu.roll(k0, NZ - 1, 1)
            top = jnp.where(self.z_high, -(k3 * u3), (k3 + kn) * (un - u3))
            low = jnp.where(self.z_low, k0 * u0, pltpu.roll(top, 1, 1))
            z_ends.append((low, top))
        for rz in range(Q):
            (u0, k0), (u3, k3) = at(0, rz), at(Q - 1, rz)
            top = (k3 + self.above_y(k0)) * (self.above_y(u0) - u3)
            turned = pltpu.roll(pltpu.roll(top, CHUNK, 1), 1, 0)
            low = jnp.where(self.y_low, turned, pltpu.roll(top, 1, 0))
            y_tops.append(top)
            y_lows.append(jnp.where(self.y_start, k0 * u0, low))
        for ry in range(Q):
            z_low, z_top = z_ends[ry]
            u0, k0 = at(ry, 0)
            for rz in range(Q):
                r = Q * ry + rz
                if rz < Q - 1:
                    u1, k1 = at(ry, rz + 1)
                    z_up = (k0 + k1) * (u1 - u0)
                else:
                    u1 = k1 = None
                    z_up = z_top
                if ry < Q - 1:
                    un, kn = at(ry + 1, rz)
                    y_up = (k0 + kn) * (un - u0)
                else:
                    y_up = y_tops[rz]
                x_up = (k0 + next_k[r]) * (next_u[r] - u0)
                x_low = f_ref[r]
                f_ref[r] = x_up
                total = (x_up - x_low) + (y_up - y_lows[rz]) + (z_up - z_low)
                emit(x, r, u0, total)
                y_lows[rz], z_low = y_up, z_up
                u0, k0 = u1, k1

    def begin(self, x, low_u, low_k):
        for r in range(PARTS):
            self.f[r] = (low_k[r] + self.k[x, r]) * (self.u[x, r] - low_u[r])

    def stretches(self, first, count, size, emit):
        def stretch(n, _):
            for q in range(size):
                self.plane(first + size * n + q, emit)
            return 0

        lax.fori_loop(0, count, stretch, 0)

    def step(self, first, count, size, emit):
        self.begin(first, self.u.at[first - 1], self.k.at[first - 1])
        self.stretches(first, count, size, emit)

    def keep(self, x, r, u0, total):
        inside = jnp.where(x < BX, self.below, jnp.where(x < 2 * BX, jnp.float32(1.0), self.above))
        new = inside * (u0 + total)
        self.u[x, r] = new
        self.k[x, r] = coeff(self.e[x, r], new)


def to_rows(tiles, rows):
    for ry in range(Q):
        parts = separate([tiles[Q * ry + rz] for rz in range(Q)])
        for h in range(Q):
            rows[rows_at(h, ry), :] = parts[h]


def inner_kernel(low, own_a, own_b, high, u_ref, k_ref, e_ref, g_ref, save, f_ref):
    later = jnp.where(lax.axis_index("tm") == 0, 0.0, 1.0).astype(jnp.float32)
    fine = Fine(u_ref, k_ref, e_ref, f_ref)
    for n, ref in enumerate((low, own_a, own_b, high)):
        fine.stage(ref, (n + 1) * HALF)

    def keep_first(x, r, u0, total):
        g_ref[x - HALF, r] = later * (u0 + STEPS * total)
        fine.keep(x, r, u0, total)

    def stow(t):
        for r in range(PARTS):
            save[0, t, r] = u_ref[HALF + t, r]
            save[1, t, r] = k_ref[HALF + t, r]
            save[2, t, r] = u_ref[5 * HALF - 1 - t, r]
            save[3, t, r] = k_ref[5 * HALF - 1 - t, r]

    for t in range(1, HALF + 1):
        stow(t)
        fine.step(HALF + t, 2, BX - t, keep_first if t == 1 else fine.keep)


def outer_kernel(low, high, u_in, k_in, e_in, g_ref, save, out, u_ref, k_ref, e_ref, f_ref, s_ref):
    fine = Fine(u_ref, k_ref, e_ref, f_ref)
    fine.stage(low, 0)
    fine.stage(high, 5 * HALF)

    once = one_trip()

    def wedges(t, _):
        fine.begin(t, u_ref.at[t - 1], k_ref.at[t - 1])

        def low_side(_, carry):
            for q in range(HALF - 1):
                fine.plane(t + q, fine.keep)
            fine.plane(t + HALF - 1, fine.keep, save.at[0, t], save.at[1, t])
            return carry

        lax.fori_loop(0, once, low_side, 0)
        fine.begin(5 * HALF - t, save.at[2, t], save.at[3, t])
        fine.stretches(5 * HALF - t, once, HALF, fine.keep)
        return 0

    lax.fori_loop(1, HALF + 1, wedges, 0)
    for t in range(HALF + 1, STEPS):
        fine.step(t, 2, 3 * HALF - t, fine.keep)

    def keep_last(x, r, u0, total):
        u_ref[x - BX, r] = (u0 + total) - g_ref[x - HALF, r]

    fine.step(BX, 2, HALF, keep_last)

    def natural(n, _):
        for x in (2 * n, 2 * n + 1):
            to_rows(u_ref.at[x], s_ref.at[x])
        return 0

    lax.fori_loop(0, BX // 2, natural, 0)

    def spread(x, _):
        for j in range(SLICES):
            for c in range(3):
                strip = ORDER[j] + c - 1
                if 0 <= strip < SLICES:
                    tile = s_ref[x, strip * ROWS : (strip + 1) * ROWS, :]
                else:
                    tile = jnp.zeros((ROWS, NZ), jnp.float32)
                out[j, x, c * ROWS : (c + 1) * ROWS, :] = tile
        return 0

    lax.fori_loop(0, BX, spread, 0)


GRID = jax.ShapeDtypeStruct((3 * BX + 1, PARTS, 8, NZ), jnp.float32)


def inner(low, own_a, own_b, high):
    f32 = jnp.float32
    return pl.pallas_call(
        inner_kernel,
        out_shape=(
            GRID,
            GRID,
            GRID,
            jax.ShapeDtypeStruct((4 * HALF, PARTS, 8, NZ), f32),
            jax.ShapeDtypeStruct((4, HALF + 1, PARTS, 8, NZ), f32),
        ),
        in_specs=[VMEM] * 4,
        out_specs=(VMEM,) * 5,
        scratch_shapes=[pltpu.VMEM((PARTS, 8, NZ), f32)],
        compiler_params=pltpu.CompilerParams(vmem_limit_bytes=16 << 20),
        cost_estimate=pl.CostEstimate(flops=10**8, bytes_accessed=10**7, transcendentals=0),
        name="inner",
    )(low, own_a, own_b, high)


def outer(low, high, u, k, e, g, save):
    f32 = jnp.float32
    return pl.pallas_call(
        outer_kernel,
        out_shape=(jax.ShapeDtypeStruct((SLICES, BX, EXT, NZ), f32), GRID, GRID, GRID),
        in_specs=[VMEM] * 7,
        out_specs=(VMEM,) * 4,
        scratch_shapes=[pltpu.VMEM((PARTS, 8, NZ), f32), pltpu.VMEM((BX, NY, NZ), f32)],
        input_output_aliases={2: 1, 3: 2, 4: 3},
        compiler_params=pltpu.CompilerParams(vmem_limit_bytes=16 << 20),
        name="outer",
    )(low, high, u, k, e, g, save)[0]


def pack_kernel(sent, down, up):
    row = lax.broadcasted_iota(jnp.int32, (ROWS, NZ), 0)

    def tile(i, x, c):
        return sent[i, x, c * ROWS : (c + 1) * ROWS, :]

    for n, (i, d, kind) in enumerate(TILES):
        for ref, x in ((down, d - 1), (up, BX - d)):
            if kind == "mid":
                value = tile(i, x, 1)
            elif kind == "both":
                value = jnp.where(row < 4, tile(i, x, 2), tile(i, x, 0))
            else:
                value = tile(i, x, 0 if kind == "low" else 2)
            ref[n] = value


def pack(sent):
    shape = jax.ShapeDtypeStruct((len(TILES), ROWS, NZ), jnp.float32)
    return pl.pallas_call(
        pack_kernel,
        out_shape=(shape, shape),
        in_specs=[VMEM],
        out_specs=(VMEM, VMEM),
        compiler_params=pltpu.CompilerParams(vmem_limit_bytes=8 << 20),
        name="pack",
    )(sent)


def strip_kernel(*refs):
    own = strip_of(lax.axis_index("tm"))
    parts, (out, rows) = refs[:-2], refs[-2:]
    for n, ref in enumerate(parts):

        def natural(m, _, n=n, ref=ref):
            for x in (2 * m, 2 * m + 1):
                to_rows(ref.at[HALF + x], rows.at[n * HALF + x])
            return 0

        lax.fori_loop(0, HALF // 2, natural, 0)
    for c in range(3):
        strip = own + (c - 1)
        scale = jnp.where((strip >= 0) & (strip < SLICES), float(STEPS), 0.0).astype(jnp.float32)
        start = pl.multiple_of(jnp.clip(strip, 0, SLICES - 1) * ROWS, ROWS)
        for x in range(3 * BX):
            out[x, c] = scale * rows[x, pl.ds(start, ROWS), :]


def strip_part(*parts):
    return pl.pallas_call(
        strip_kernel,
        out_shape=jax.ShapeDtypeStruct((3 * BX, 3, 8, NZ), jnp.float32),
        in_specs=[VMEM] * len(parts),
        out_specs=VMEM,
        scratch_shapes=[pltpu.VMEM((3 * BX, NY, NZ), jnp.float32)],
        compiler_params=pltpu.CompilerParams(vmem_limit_bytes=8 << 20),
        cost_estimate=pl.CostEstimate(flops=10**6, bytes_accessed=10**6, transcendentals=0),
        name="strip",
    )(*parts)


def sent_tile(refs, i, x, c):
    sent, below, above = refs
    if x < BX:
        return below[PLACE[i, BX - x, c]]
    if x >= 2 * BX:
        return above[PLACE[i, x - 2 * BX + 1, c]]
    return sent[i, x - BX, c * ROWS : (c + 1) * ROWS, :]


def coarse_steps(count, base, eta, refs, u_ref, k_ref, f_ref, out):
    lane, row = iotas()
    x_below, x_above = has_neighbours(lax.axis_index("space"), lax.axis_size("space"))
    y_below, y_above = has_neighbours(strip_of(lax.axis_index("tm")), SLICES)
    once = one_trip()

    def mask(x, c):
        factors = []
        if not BX <= x < 2 * BX:
            factors.append(x_below if x < BX else x_above)
        if c != 1:
            factors.append(y_below if c == 0 else y_above)
        return factors[0] * factors[1] if len(factors) == 2 else (factors or [None])[0]

    def begin(x, _):
        for c in range(3):
            k_ref[x, c] = coeff(eta[x, c], u_ref[x, c])
        return 0

    lax.fori_loop(BX - count, 2 * BX + count, begin, 0, unroll=4)

    def stretch(n, left, planes):
        def body(_, carry):
            flux = [None] * 3
            for x in planes:
                far = max(BX - x, x - (2 * BX - 1), 0)
                tiles = (0, 1, 2) if left - far >= 1 else (1,)
                us = [u_ref[x, c] for c in range(3)]
                ks = [k_ref[x, c] for c in range(3)]
                ru = [pltpu.roll(u, 7, 0) for u in us]
                rk = [pltpu.roll(k, 7, 0) for k in ks]
                ups = []
                for c in range(max(tiles) + 1):
                    un, kn = ru[c], rk[c]
                    if c < 2:
                        un = jnp.where(row == 7, ru[c + 1], un)
                        kn = jnp.where(row == 7, rk[c + 1], kn)
                    ups.append((ks[c] + kn) * (un - us[c]))
                rolled = [pltpu.roll(v, 1, 0) for v in ups]
                for c in tiles:
                    low = rolled[c]
                    if c > 0:
                        low = jnp.where(row == 0, rolled[c - 1], low)
                    u0, k0 = us[c], ks[c]
                    x_up = (k0 + k_ref[x + 1, c]) * (u_ref[x + 1, c] - u0)
                    x_low = flux[c]
                    if x_low is None:
                        if x == BX - (left if c == 1 else left - 1):
                            x_low = (k0 + k_ref[x - 1, c]) * (u0 - u_ref[x - 1, c])
                        else:
                            x_low = f_ref[c]
                    flux[c] = x_up
                    new = (u0 + (x_up - x_low) + (ups[c] - low) + z_flux(u0, k0, lane)) + (
                        sent_tile(refs, base + n, x, c)
                    )
                    m = mask(x, c)
                    if m is not None:
                        new = m * new
                    if left > 0:
                        u_ref[x, c] = new
                        k_ref[x, c] = coeff(eta[x, c], new)
                    if c == 1 and far == 0:
                        out[base + n, x - BX] = new
            for c in range(3):
                if flux[c] is not None:
                    f_ref[c] = flux[c]
            return carry

        lax.fori_loop(0, once, body, 0)

    for n in range(1, count + 1):
        left = count - n
        planes = list(range(BX - left, 2 * BX + left))
        parts = -(-len(planes) * (3 if left else 1) // GROUP)
        size = -(-len(planes) // parts)
        for a in range(0, len(planes), size):
            stretch(n, left, planes[a : a + size])


def first_kernel(eta, sent, below, above, out, u_ref, k_ref, f_ref):
    refs = (sent, below, above)
    for x in range(BX - FIRST, 2 * BX + FIRST):
        for c in range(3):
            if BX <= x < 2 * BX or c == 1 or max(BX - x, x - 2 * BX + 1) < FIRST:
                u_ref[x, c] = sent_tile(refs, 0, x, c)
            else:
                u_ref[x, c] = jnp.zeros((8, NZ), jnp.float32)
    for x in range(BX):
        out[0, x] = sent[0, x, ROWS : 2 * ROWS, :]
    coarse_steps(FIRST, 0, eta, refs, u_ref, k_ref, f_ref, out)


def second_kernel(eta, sent, below, above, low_u, own_u, high_u, done, out, u_ref, k_ref, f_ref):
    for b, ref in enumerate((low_u, own_u, high_u)):
        for x in range(BX):
            for c in range(3):
                u_ref[b * BX + x, c] = ref[x, c * ROWS : (c + 1) * ROWS, :]
    for i in range(FIRST + 1):
        for x in range(BX):
            out[i, x] = done[i, x]
    refs = (sent, below, above)
    coarse_steps(SLICES - 1 - FIRST, FIRST, eta, refs, u_ref, k_ref, f_ref, out)


def coarse_call(kernel, name, count, *operands):
    f32 = jnp.float32
    return pl.pallas_call(
        kernel,
        out_shape=jax.ShapeDtypeStruct((count, BX, ROWS, NZ), f32),
        in_specs=[VMEM] * len(operands),
        out_specs=VMEM,
        scratch_shapes=[
            pltpu.VMEM((3 * BX, 3, 8, NZ), f32),
            pltpu.VMEM((3 * BX, 3, 8, NZ), f32),
            pltpu.VMEM((3, 8, NZ), f32),
        ],
        compiler_params=pltpu.CompilerParams(vmem_limit_bytes=8 << 20),
        name=name,
    )(*operands)


def place_kernel(strips, out, sems):
    copies = [
        pltpu.make_async_copy(
            strips.at[j], out.at[:, pl.ds(ORDER[j] * ROWS, ROWS), :], sems.at[j]
        )
        for j in range(SLICES)
    ]
    for copy in copies:
        copy.start()
    for copy in copies:
        copy.wait()


def place(strips):
    return pl.pallas_call(
        place_kernel,
        out_shape=jax.ShapeDtypeStruct((BX, NY, NZ), jnp.float32),
        in_specs=[VMEM],
        out_specs=pl.BlockSpec(memory_space=HBM),
        scratch_shapes=[pltpu.SemaphoreType.DMA((SLICES,))],
        compiler_params=pltpu.CompilerParams(vmem_limit_bytes=4 << 20),
        name="place",
    )(strips)


def both_ways(down, up, axis):
    line = ORDER if axis == "tm" else range(lax.axis_size(axis))
    forward = list(zip(line[:-1], line[1:]))
    backward = [(b, a) for a, b in forward]
    return lax.ppermute(up, axis, forward), lax.ppermute(down, axis, backward)


def per_device(start_values, regions, resistivity):
    own_a, own_b = own_part(start_values[0], regions, resistivity)
    low_b, high_a = both_ways(own_a, own_b, "space")
    low_a, high_b = both_ways(own_b, own_a, "space")
    sent = outer(low_a, high_b, *inner(low_b, own_a, own_b, high_a))
    sent = lax.all_to_all(sent, "tm", 0, 0)
    below, above = both_ways(*pack(sent), "space")
    eta = strip_part(low_a, low_b, own_a, own_b, high_a, high_b)
    done = coarse_call(first_kernel, "first", FIRST + 1, eta, sent, below, above)
    state = done[FIRST]
    y_low, y_high = both_ways(state, state, "tm")
    strip = jnp.concatenate([y_low, state, y_high], axis=1)
    x_low, x_high = both_ways(strip, strip, "space")
    ends = coarse_call(
        second_kernel, "second", SLICES, eta, sent, below, above, x_low, strip, x_high, done
    )
    result = lax.all_to_all(ends, "tm", 0, 0)
    return place(result)[None]


def solution(mesh):
    in_specs = (P("tm", "space", None, None), P("space", None, None), P())
    out_specs = P("tm", "space", None, None)
    return jax.shard_map(
        per_device, mesh=mesh, in_specs=in_specs, out_specs=out_specs, check_vma=False
    )
```

```python
import jax
import jax.numpy as jnp
from jax import lax
from jax.experimental import pallas as pl
from jax.experimental.pallas import tpu as pltpu
from jax.sharding import PartitionSpec as P

STEPS = 8
fine_step = 0.008

SIDE = 4
ORDER = [a * SIDE + (b if a % 2 == 0 else SIDE - 1 - b) for a in range(SIDE) for b in range(SIDE)]
BX = 8
HALF = BX // 2
NY = 128
NZ = 128
SLICES = 16
REGIONS = 4
ROWS = 8
EXT = 3 * ROWS
SMEM = pl.BlockSpec(memory_space=pltpu.SMEM)
FIRST = 7
VMEM = pl.BlockSpec(memory_space=pltpu.VMEM)
HBM = pltpu.MemorySpace.HBM


def halo_depth(i):
    return FIRST - i if i <= FIRST else SLICES - 1 - i


def packed_tiles():
    tiles = []
    for i in range(SLICES):
        depth = halo_depth(i)
        for d in range(1, depth + 1):
            tiles.append((i, d, "mid"))
            beyond = depth - d
            if 1 <= beyond <= 4:
                tiles.append((i, d, "both"))
            elif beyond > 4:
                tiles.append((i, d, "low"))
                tiles.append((i, d, "high"))
    return tiles


TILES = packed_tiles()
PLACE = {}
for _n, (_i, _d, _kind) in enumerate(TILES):
    for _c in {"mid": (1,), "both": (0, 2), "low": (0,), "high": (2,)}[_kind]:
        PLACE[_i, _d, _c] = _n
PARTS = NY // 8
GROUP = 40


def coeff(eta, u):
    return eta * (2.0 - 1.0 / (1.0 + u * u))


def z_flux(u0, k0, lane):
    up = pltpu.roll(u0, NZ - 1, 1)
    kp = pltpu.roll(k0, NZ - 1, 1)
    edge = k0 * u0
    upper = jnp.where(lane == NZ - 1, -edge, (k0 + kp) * (up - u0))
    lower = jnp.where(lane == 0, edge, pltpu.roll(upper, 1, 1))
    return upper - lower


Q = 4
CHUNK = NZ // Q


def by_chunk(lane, values):
    low = jnp.where(lane < CHUNK, values[0], values[1])
    return jnp.where(lane < 2 * CHUNK, low, jnp.where(lane < 3 * CHUNK, values[2], values[3]))


def interleave(rows):
    lane, _ = iotas()
    turned = []
    for h in range(Q):
        source = Q * (lane & (CHUNK - 1)) + (((lane >> 5) - h) & (Q - 1))
        turned.append(jnp.take_along_axis(rows[h], source, axis=1))
    tiles = []
    for rz in range(Q):
        tile = by_chunk(lane, [turned[(c - rz) % Q] for c in range(Q)])
        tiles.append(pltpu.roll(tile, NZ - CHUNK * rz, 1) if rz else tile)
    return tiles


def separate(tiles):
    lane, _ = iotas()
    turned = [pltpu.roll(t, CHUNK * rz, 1) if rz else t for rz, t in enumerate(tiles)]
    rows = []
    for h in range(Q):
        mixed = by_chunk(lane, [turned[(c - h) % Q] for c in range(Q)])
        source = CHUNK * (((lane & (Q - 1)) + h) & (Q - 1)) + (lane >> 2)
        rows.append(jnp.take_along_axis(mixed, source, axis=1))
    return rows


def rows_at(h, ry):
    return pl.ds(CHUNK * h + ry, 8, stride=Q)


def strip_of(tm):
    across, along = lax.div(tm, SIDE), lax.rem(tm, SIDE)
    return across * SIDE + jnp.where(lax.rem(across, 2) == 0, along, SIDE - 1 - along)


def iotas():
    shape = (8, NZ)
    return lax.broadcasted_iota(jnp.int32, shape, 1), lax.broadcasted_iota(jnp.int32, shape, 0)


def has_neighbours(index, count):
    below = jnp.where(index == 0, 0.0, 1.0).astype(jnp.float32)
    above = jnp.where(index == count - 1, 0.0, 1.0).astype(jnp.float32)
    return below, above


def is_mirrored():
    return lax.rem(lax.axis_index("space"), 2) == 1


def next_chip_exists():
    index = lax.axis_index("space")
    at_end = (index == 0) | (index == lax.axis_size("space") - 1)
    return jnp.where(at_end, 0.0, 1.0).astype(jnp.float32)


def one_trip():
    return jnp.where(lax.axis_index("space") < 0, 2, 1)


def own_kernel(start, regions, resistivity, *refs):
    outs, (start_v, regions_v, resistivity_s, sems) = refs[:2], refs[2:]
    small = pltpu.make_async_copy(resistivity, resistivity_s, sems.at[4])
    small.start()
    copies = []
    odd = is_mirrored()
    for h in range(2):
        part = pl.ds(jnp.where(odd, 1 - h, h) * HALF, HALF)
        pair = (
            pltpu.make_async_copy(start.at[part], start_v.at[h], sems.at[2 * h]),
            pltpu.make_async_copy(regions.at[part], regions_v.at[h], sems.at[2 * h + 1]),
        )
        for copy in pair:
            copy.start()
        copies.append(pair)
    small.wait()
    scaled = [resistivity_s[i] * jnp.float32(0.5 * fine_step) for i in range(REGIONS)]
    once = one_trip()
    for h in range(2):
        for copy in copies[h]:
            copy.wait()

        def planes(_, carry, h=h):
            for x in range(HALF):
                source = jnp.where(odd, HALF - 1 - x, x)
                for ry in range(Q):
                    u, e = [], []
                    for g in range(Q):
                        where = rows_at(g, ry)
                        u.append(start_v[h, source, where, :])
                        region = regions_v[h, source, where, :]
                        value = jnp.zeros((8, NZ), jnp.float32)
                        for i in range(REGIONS):
                            value = jnp.where(region == i, scaled[i], value)
                        e.append(value)
                    u, e = interleave(u), interleave(e)
                    for rz in range(Q):
                        outs[h][x, Q * ry + rz] = u[rz]
                        outs[h][HALF + x, Q * ry + rz] = e[rz]
            return carry

        lax.fori_loop(0, once, planes, 0)


def own_part(start, regions, resistivity):
    hbm = pl.BlockSpec(memory_space=HBM)
    shape = jax.ShapeDtypeStruct((2 * HALF, PARTS, 8, NZ), jnp.float32)
    return pl.pallas_call(
        own_kernel,
        out_shape=(shape, shape),
        in_specs=[hbm] * 3,
        out_specs=(VMEM, VMEM),
        scratch_shapes=[
            pltpu.VMEM((2, HALF, NY, NZ), jnp.float32),
            pltpu.VMEM((2, HALF, NY, NZ), jnp.int32),
            pltpu.SMEM((REGIONS,), jnp.float32),
            pltpu.SemaphoreType.DMA((5,)),
        ],
        compiler_params=pltpu.CompilerParams(vmem_limit_bytes=8 << 20),
        name="own",
    )(*(pltpu.with_memory_space_constraint(a, HBM) for a in (start, regions, resistivity)))


class Fine:
    def __init__(self, u_ref, k_ref, e_ref, f_ref):
        self.u, self.k, self.e, self.f = u_ref, k_ref, e_ref, f_ref
        self.below = next_chip_exists()
        lane, sub = iotas()
        self.z_high, self.z_low = [(lane & (CHUNK - 1)) == v for v in (CHUNK - 1, 0)]
        self.y_high, self.y_low = sub == 7, sub == 0
        self.y_end = (sub == 7) & (lane >= NZ - CHUNK)
        self.y_start = (sub == 0) & (lane < CHUNK)

    def stage(self, ref, base, turn=False):
        def one(x, _):
            to = base + (HALF - 1 - x if turn else x)
            for r in range(PARTS):
                u, e = ref[x, r], ref[HALF + x, r]
                self.u[to, r] = u
                self.e[to, r] = e
                self.k[to, r] = coeff(e, u)
            return 0

        lax.fori_loop(0, HALF, one, 0)

    def above_y(self, v):
        turned = pltpu.roll(pltpu.roll(v, NZ - CHUNK, 1), 7, 0)
        v = jnp.where(self.y_high, turned, pltpu.roll(v, 7, 0))
        return jnp.where(self.y_end, 0.0, v)

    def plane(self, x, emit, next_u=None, next_k=None):
        f_ref = self.f
        if next_u is None:
            next_u, next_k = self.u.at[x + 1], self.k.at[x + 1]

        def at(ry, rz):
            return self.u[x, Q * ry + rz], self.k[x, Q * ry + rz]

        z_ends, y_tops, y_lows = [], [], []
        for ry in range(Q):
            (u0, k0), (u3, k3) = at(ry, 0), at(ry, Q - 1)
            un, kn = pltpu.roll(u0, NZ - 1, 1), pltpu.roll(k0, NZ - 1, 1)
            top = jnp.where(self.z_high, -(k3 * u3), (k3 + kn) * (un - u3))
            low = jnp.where(self.z_low, k0 * u0, pltpu.roll(top, 1, 1))
            z_ends.append((low, top))
        for rz in range(Q):
            (u0, k0), (u3, k3) = at(0, rz), at(Q - 1, rz)
            top = (k3 + self.above_y(k0)) * (self.above_y(u0) - u3)
            turned = pltpu.roll(pltpu.roll(top, CHUNK, 1), 1, 0)
            low = jnp.where(self.y_low, turned, pltpu.roll(top, 1, 0))
            y_tops.append(top)
            y_lows.append(jnp.where(self.y_start, k0 * u0, low))
        for ry in range(Q):
            z_low, z_top = z_ends[ry]
            u0, k0 = at(ry, 0)
            for rz in range(Q):
                r = Q * ry + rz
                if rz < Q - 1:
                    u1, k1 = at(ry, rz + 1)
                    z_up = (k0 + k1) * (u1 - u0)
                else:
                    u1 = k1 = None
                    z_up = z_top
                if ry < Q - 1:
                    un, kn = at(ry + 1, rz)
                    y_up = (k0 + kn) * (un - u0)
                else:
                    y_up = y_tops[rz]
                x_up = (k0 + next_k[r]) * (next_u[r] - u0)
                x_low = f_ref[r]
                f_ref[r] = x_up
                total = (x_up - x_low) + (y_up - y_lows[rz]) + (z_up - z_low)
                emit(x, r, u0, total)
                y_lows[rz], z_low = y_up, z_up
                u0, k0 = u1, k1

    def begin(self, x, low_u, low_k):
        for r in range(PARTS):
            self.f[r] = (low_k[r] + self.k[x, r]) * (self.u[x, r] - low_u[r])

    def stretches(self, first, count, size, emit):
        def stretch(n, _):
            for q in range(size):
                self.plane(first + size * n + q, emit)
            return 0

        lax.fori_loop(0, count, stretch, 0)

    def step(self, first, count, size, emit):
        self.begin(first, self.u.at[first - 1], self.k.at[first - 1])
        self.stretches(first, count, size, emit)

    def keep(self, x, r, u0, total):
        inside = jnp.where(x < BX, self.below, jnp.float32(1.0))
        new = inside * (u0 + total)
        self.u[x, r] = new
        self.k[x, r] = coeff(self.e[x, r], new)


def to_rows(tiles, rows):
    for ry in range(Q):
        parts = separate([tiles[Q * ry + rz] for rz in range(Q)])
        for h in range(Q):
            rows[rows_at(h, ry), :] = parts[h]


def inner_kernel(low, own_a, own_b, high, u_ref, k_ref, e_ref, g_ref, save, f_ref):
    later = jnp.where(lax.axis_index("tm") == 0, 0.0, 1.0).astype(jnp.float32)
    fine = Fine(u_ref, k_ref, e_ref, f_ref)
    for n, ref in enumerate((low, own_a, own_b, high)):
        fine.stage(ref, (n + 1) * HALF, turn=n in (0, 3))

    def keep_first(x, r, u0, total):
        g_ref[x - HALF, r] = later * (u0 + STEPS * total)
        fine.keep(x, r, u0, total)

    def stow(t):
        for r in range(PARTS):
            save[0, t, r] = u_ref[HALF + t, r]
            save[1, t, r] = k_ref[HALF + t, r]
            save[2, t, r] = u_ref[5 * HALF - 1 - t, r]
            save[3, t, r] = k_ref[5 * HALF - 1 - t, r]

    for t in range(1, HALF + 1):
        stow(t)
        fine.step(HALF + t, 2, BX - t, keep_first if t == 1 else fine.keep)


def outer_kernel(low, high, u_in, k_in, e_in, g_ref, save, out, u_ref, k_ref, e_ref, f_ref, s_ref):
    fine = Fine(u_ref, k_ref, e_ref, f_ref)
    fine.stage(low, 0, turn=True)
    fine.stage(high, 5 * HALF, turn=True)

    once = one_trip()

    def wedges(t, _):
        fine.begin(t, u_ref.at[t - 1], k_ref.at[t - 1])

        def low_side(_, carry):
            for q in range(HALF - 1):
                fine.plane(t + q, fine.keep)
            fine.plane(t + HALF - 1, fine.keep, save.at[0, t], save.at[1, t])
            return carry

        lax.fori_loop(0, once, low_side, 0)
        fine.begin(5 * HALF - t, save.at[2, t], save.at[3, t])
        fine.stretches(5 * HALF - t, once, HALF, fine.keep)
        return 0

    lax.fori_loop(1, HALF + 1, wedges, 0)
    for t in range(HALF + 1, STEPS):
        fine.step(t, 2, 3 * HALF - t, fine.keep)

    def keep_last(x, r, u0, total):
        u_ref[x - BX, r] = (u0 + total) - g_ref[x - HALF, r]

    fine.step(BX, 2, HALF, keep_last)

    def natural(n, _):
        for q in range(HALF):
            to_rows(u_ref.at[HALF * n + q], s_ref.at[HALF * n + q])
        return 0

    lax.fori_loop(0, 2, natural, 0)

    def spread(x, _):
        for j in range(SLICES):
            for c in range(3):
                strip = ORDER[j] + c - 1
                if 0 <= strip < SLICES:
                    tile = s_ref[x, strip * ROWS : (strip + 1) * ROWS, :]
                else:
                    tile = jnp.zeros((ROWS, NZ), jnp.float32)
                out[j, x, c * ROWS : (c + 1) * ROWS, :] = tile
        return 0

    lax.fori_loop(0, BX, spread, 0)


GRID = jax.ShapeDtypeStruct((3 * BX + 1, PARTS, 8, NZ), jnp.float32)


def inner(low, own_a, own_b, high):
    f32 = jnp.float32
    return pl.pallas_call(
        inner_kernel,
        out_shape=(
            GRID,
            GRID,
            GRID,
            jax.ShapeDtypeStruct((4 * HALF, PARTS, 8, NZ), f32),
            jax.ShapeDtypeStruct((4, HALF + 1, PARTS, 8, NZ), f32),
        ),
        in_specs=[VMEM] * 4,
        out_specs=(VMEM,) * 5,
        scratch_shapes=[pltpu.VMEM((PARTS, 8, NZ), f32)],
        compiler_params=pltpu.CompilerParams(vmem_limit_bytes=16 << 20),
        cost_estimate=pl.CostEstimate(flops=10**8, bytes_accessed=10**7, transcendentals=0),
        name="inner",
    )(low, own_a, own_b, high)


def outer(low, high, u, k, e, g, save):
    f32 = jnp.float32
    return pl.pallas_call(
        outer_kernel,
        out_shape=(jax.ShapeDtypeStruct((SLICES, BX, EXT, NZ), f32), GRID, GRID, GRID),
        in_specs=[VMEM] * 7,
        out_specs=(VMEM,) * 4,
        scratch_shapes=[pltpu.VMEM((PARTS, 8, NZ), f32), pltpu.VMEM((BX, NY, NZ), f32)],
        input_output_aliases={2: 1, 3: 2, 4: 3},
        compiler_params=pltpu.CompilerParams(vmem_limit_bytes=16 << 20),
        name="outer",
    )(low, high, u, k, e, g, save)[0]


def pack_kernel(sent, down, up):
    row = lax.broadcasted_iota(jnp.int32, (ROWS, NZ), 0)

    def tile(i, x, c):
        return sent[i, x, c * ROWS : (c + 1) * ROWS, :]

    for n, (i, d, kind) in enumerate(TILES):
        for ref, x in ((down, d - 1), (up, BX - d)):
            if kind == "mid":
                value = tile(i, x, 1)
            elif kind == "both":
                value = jnp.where(row < 4, tile(i, x, 2), tile(i, x, 0))
            else:
                value = tile(i, x, 0 if kind == "low" else 2)
            ref[n] = value


def pack(sent):
    shape = jax.ShapeDtypeStruct((len(TILES), ROWS, NZ), jnp.float32)
    return pl.pallas_call(
        pack_kernel,
        out_shape=(shape, shape),
        in_specs=[VMEM],
        out_specs=(VMEM, VMEM),
        compiler_params=pltpu.CompilerParams(vmem_limit_bytes=8 << 20),
        name="pack",
    )(sent)


def strip_kernel(*refs):
    own = strip_of(lax.axis_index("tm"))
    parts, (out, rows) = refs[:-2], refs[-2:]
    for n, ref in enumerate(parts):

        def natural(m, _, n=n, ref=ref):
            for x in (2 * m, 2 * m + 1):
                to = HALF - 1 - x if n in (0, 1, 4, 5) else x
                to_rows(ref.at[HALF + x], rows.at[n * HALF + to])
            return 0

        lax.fori_loop(0, HALF // 2, natural, 0)
    for c in range(3):
        strip = own + (c - 1)
        scale = jnp.where((strip >= 0) & (strip < SLICES), float(STEPS), 0.0).astype(jnp.float32)
        start = pl.multiple_of(jnp.clip(strip, 0, SLICES - 1) * ROWS, ROWS)
        for x in range(3 * BX):
            out[x, c] = scale * rows[x, pl.ds(start, ROWS), :]


def strip_part(*parts):
    return pl.pallas_call(
        strip_kernel,
        out_shape=jax.ShapeDtypeStruct((3 * BX, 3, 8, NZ), jnp.float32),
        in_specs=[VMEM] * len(parts),
        out_specs=VMEM,
        scratch_shapes=[pltpu.VMEM((3 * BX, NY, NZ), jnp.float32)],
        compiler_params=pltpu.CompilerParams(vmem_limit_bytes=8 << 20),
        cost_estimate=pl.CostEstimate(flops=10**6, bytes_accessed=10**6, transcendentals=0),
        name="strip",
    )(*parts)


def sent_tile(refs, i, x, c):
    sent, below, above = refs
    if x < BX:
        return below[PLACE[i, BX - x, c]]
    if x >= 2 * BX:
        return above[PLACE[i, x - 2 * BX + 1, c]]
    return sent[i, x - BX, c * ROWS : (c + 1) * ROWS, :]


def coarse_steps(count, base, eta, refs, u_ref, k_ref, f_ref, out):
    lane, row = iotas()
    x_below = next_chip_exists()
    y_below, y_above = has_neighbours(strip_of(lax.axis_index("tm")), SLICES)
    once = one_trip()

    def mask(x, c):
        factors = []
        if x < BX:
            factors.append(x_below)
        if c != 1:
            factors.append(y_below if c == 0 else y_above)
        return factors[0] * factors[1] if len(factors) == 2 else (factors or [None])[0]

    def begin(x, _):
        for c in range(3):
            k_ref[x, c] = coeff(eta[x, c], u_ref[x, c])
        return 0

    lax.fori_loop(BX - count, 2 * BX + count, begin, 0, unroll=4)

    def stretch(n, left, planes):
        def body(_, carry):
            flux = [None] * 3
            for x in planes:
                far = max(BX - x, x - (2 * BX - 1), 0)
                tiles = (0, 1, 2) if left - far >= 1 else (1,)
                us = [u_ref[x, c] for c in range(3)]
                ks = [k_ref[x, c] for c in range(3)]
                ru = [pltpu.roll(u, 7, 0) for u in us]
                rk = [pltpu.roll(k, 7, 0) for k in ks]
                ups = []
                for c in range(max(tiles) + 1):
                    un, kn = ru[c], rk[c]
                    if c < 2:
                        un = jnp.where(row == 7, ru[c + 1], un)
                        kn = jnp.where(row == 7, rk[c + 1], kn)
                    ups.append((ks[c] + kn) * (un - us[c]))
                rolled = [pltpu.roll(v, 1, 0) for v in ups]
                for c in tiles:
                    low = rolled[c]
                    if c > 0:
                        low = jnp.where(row == 0, rolled[c - 1], low)
                    u0, k0 = us[c], ks[c]
                    x_up = (k0 + k_ref[x + 1, c]) * (u_ref[x + 1, c] - u0)
                    x_low = flux[c]
                    if x_low is None:
                        if x == BX - (left if c == 1 else left - 1):
                            x_low = (k0 + k_ref[x - 1, c]) * (u0 - u_ref[x - 1, c])
                        else:
                            x_low = f_ref[c]
                    flux[c] = x_up
                    new = (u0 + (x_up - x_low) + (ups[c] - low) + z_flux(u0, k0, lane)) + (
                        sent_tile(refs, base + n, x, c)
                    )
                    m = mask(x, c)
                    if m is not None:
                        new = m * new
                    if left > 0:
                        u_ref[x, c] = new
                        k_ref[x, c] = coeff(eta[x, c], new)
                    if c == 1 and far == 0:
                        out(n, x - BX, new)
            for c in range(3):
                if flux[c] is not None:
                    f_ref[c] = flux[c]
            return carry

        lax.fori_loop(0, once, body, 0)

    for n in range(1, count + 1):
        left = count - n
        planes = list(range(BX - left, 2 * BX + left))
        parts = -(-len(planes) * (3 if left else 1) // GROUP)
        size = -(-len(planes) // parts)
        for a in range(0, len(planes), size):
            stretch(n, left, planes[a : a + size])


def first_kernel(eta, sent, below, above, out, u_ref, k_ref, f_ref):
    refs = (sent, below, above)
    for x in range(BX - FIRST, 2 * BX + FIRST):
        for c in range(3):
            if BX <= x < 2 * BX or c == 1 or max(BX - x, x - 2 * BX + 1) < FIRST:
                u_ref[x, c] = sent_tile(refs, 0, x, c)
            else:
                u_ref[x, c] = jnp.zeros((8, NZ), jnp.float32)
    for x in range(BX):
        out[0, x] = sent[0, x, ROWS : 2 * ROWS, :]

    def put(n, x, value):
        out[n, x] = value

    coarse_steps(FIRST, 0, eta, refs, u_ref, k_ref, f_ref, put)


def second_kernel(eta, sent, below, above, low_u, own_u, high_u, done, out, u_ref, k_ref, f_ref):
    odd = is_mirrored()

    def true_plane(x):
        return jnp.where(odd, BX - 1 - x, x)

    for b, ref in enumerate((low_u, own_u, high_u)):
        for x in range(BX):
            for c in range(3):
                to = b * BX + (x if b == 1 else BX - 1 - x)
                u_ref[to, c] = ref[x, c * ROWS : (c + 1) * ROWS, :]
    for i in range(FIRST + 1):
        for x in range(BX):
            out[i, true_plane(x)] = done[i, x]
    refs = (sent, below, above)

    def put(n, x, value):
        out[FIRST + n, true_plane(x)] = value

    coarse_steps(SLICES - 1 - FIRST, FIRST, eta, refs, u_ref, k_ref, f_ref, put)


def coarse_call(kernel, name, count, *operands):
    f32 = jnp.float32
    return pl.pallas_call(
        kernel,
        out_shape=jax.ShapeDtypeStruct((count, BX, ROWS, NZ), f32),
        in_specs=[VMEM] * len(operands),
        out_specs=VMEM,
        scratch_shapes=[
            pltpu.VMEM((3 * BX, 3, 8, NZ), f32),
            pltpu.VMEM((3 * BX, 3, 8, NZ), f32),
            pltpu.VMEM((3, 8, NZ), f32),
        ],
        compiler_params=pltpu.CompilerParams(vmem_limit_bytes=8 << 20),
        name=name,
    )(*operands)


def place_kernel(strips, out, sems):
    copies = [
        pltpu.make_async_copy(
            strips.at[j], out.at[:, pl.ds(ORDER[j] * ROWS, ROWS), :], sems.at[j]
        )
        for j in range(SLICES)
    ]
    for copy in copies:
        copy.start()
    for copy in copies:
        copy.wait()


def place(strips):
    return pl.pallas_call(
        place_kernel,
        out_shape=jax.ShapeDtypeStruct((BX, NY, NZ), jnp.float32),
        in_specs=[VMEM],
        out_specs=pl.BlockSpec(memory_space=HBM),
        scratch_shapes=[pltpu.SemaphoreType.DMA((SLICES,))],
        compiler_params=pltpu.CompilerParams(vmem_limit_bytes=4 << 20),
        name="place",
    )(strips)


def across(value):
    count = lax.axis_size("space")
    pairs = [(i, i + 1) for i in range(1, count - 1, 2)]
    return lax.ppermute(value, "space", pairs + [(b, a) for a, b in pairs])


def beside(value):
    pairs = [(i, i + 1) for i in range(0, lax.axis_size("space"), 2)]
    return lax.ppermute(value, "space", pairs + [(b, a) for a, b in pairs])


def with_strips(state):
    sides = []
    for first in (0, 1):
        pairs = [(ORDER[q], ORDER[q + 1]) for q in range(first, SLICES - 1, 2)]
        sides.append(lax.ppermute(state, "tm", pairs + [(b, a) for a, b in pairs]))
    even = lax.rem(strip_of(lax.axis_index("tm")), 2) == 0
    low = jnp.where(even, sides[1], sides[0])
    high = jnp.where(even, sides[0], sides[1])
    return jnp.concatenate([low, state, high], axis=1)


def per_device(start_values, regions, resistivity):
    own_a, own_b = own_part(start_values[0], regions, resistivity)
    low_near, high_near = across(own_a), beside(own_b)
    low_far, high_far = across(own_b), beside(own_a)
    sent = outer(low_far, high_far, *inner(low_near, own_a, own_b, high_near))
    sent = lax.all_to_all(sent, "tm", 0, 0)
    down, up = pack(sent)
    below, above = across(down), beside(up)
    eta = strip_part(low_far, low_near, own_a, own_b, high_near, high_far)
    done = coarse_call(first_kernel, "first", FIRST + 1, eta, sent, below, above)
    strip = with_strips(done[FIRST])
    x_low, x_high = across(strip), beside(strip)
    ends = coarse_call(
        second_kernel, "second", SLICES, eta, sent, below, above, x_low, strip, x_high, done
    )
    result = lax.all_to_all(ends, "tm", 0, 0)
    return place(result)[None]


def solution(mesh):
    in_specs = (P("tm", "space", None, None), P("space", None, None), P())
    out_specs = P("tm", "space", None, None)
    return jax.shard_map(
        per_device, mesh=mesh, in_specs=in_specs, out_specs=out_specs, check_vma=False
    )
```

```python
import jax
import jax.numpy as jnp
from jax import lax
from jax.experimental import pallas as pl
from jax.experimental.pallas import tpu as pltpu
from jax.sharding import PartitionSpec as P

STEPS = 8
fine_step = 0.008

SIDE = 4
ORDER = [a * SIDE + (b if a % 2 == 0 else SIDE - 1 - b) for a in range(SIDE) for b in range(SIDE)]
BX = 8
HALF = BX // 2
NY = 128
NZ = 128
SLICES = 16
REGIONS = 4
ROWS = 8
EXT = 3 * ROWS
SMEM = pl.BlockSpec(memory_space=pltpu.SMEM)
FIRST = 7
VMEM = pl.BlockSpec(memory_space=pltpu.VMEM)
HBM = pltpu.MemorySpace.HBM


def halo_depth(i):
    return FIRST - i if i <= FIRST else SLICES - 1 - i


def packed_tiles():
    tiles = []
    for i in range(SLICES):
        depth = halo_depth(i)
        for d in range(1, depth + 1):
            tiles.append((i, d, "mid"))
            beyond = depth - d
            if 1 <= beyond <= 4:
                tiles.append((i, d, "both"))
            elif beyond > 4:
                tiles.append((i, d, "low"))
                tiles.append((i, d, "high"))
    return tiles


TILES = packed_tiles()
PLACE = {}
for _n, (_i, _d, _kind) in enumerate(TILES):
    for _c in {"mid": (1,), "both": (0, 2), "low": (0,), "high": (2,)}[_kind]:
        PLACE[_i, _d, _c] = _n
PARTS = NY // 8
LOAD = 3 * BX - 2
GROUP = 40


def coeff(eta, u):
    return eta * (2.0 - 1.0 / (1.0 + u * u))


def z_flux(u0, k0, lane):
    up = pltpu.roll(u0, NZ - 1, 1)
    kp = pltpu.roll(k0, NZ - 1, 1)
    edge = k0 * u0
    upper = jnp.where(lane == NZ - 1, -edge, (k0 + kp) * (up - u0))
    lower = jnp.where(lane == 0, edge, pltpu.roll(upper, 1, 1))
    return upper - lower


Q = 4
CHUNK = NZ // Q


def by_chunk(lane, values):
    low = jnp.where(lane < CHUNK, values[0], values[1])
    return jnp.where(lane < 2 * CHUNK, low, jnp.where(lane < 3 * CHUNK, values[2], values[3]))


def turn(h, rows):
    lane, _ = iotas()
    source = Q * (lane & (CHUNK - 1)) + (((lane >> 5) - h) & (Q - 1))
    return jnp.take_along_axis(rows, source, axis=1)


def gather_tiles(turned):
    lane, _ = iotas()
    tiles = []
    for rz in range(Q):
        tile = by_chunk(lane, [turned[(c - rz) % Q] for c in range(Q)])
        tiles.append(pltpu.roll(tile, NZ - CHUNK * rz, 1) if rz else tile)
    return tiles


def separate(tiles):
    lane, _ = iotas()
    turned = [pltpu.roll(t, CHUNK * rz, 1) if rz else t for rz, t in enumerate(tiles)]
    rows = []
    for h in range(Q):
        mixed = by_chunk(lane, [turned[(c - h) % Q] for c in range(Q)])
        source = CHUNK * (((lane & (Q - 1)) + h) & (Q - 1)) + (lane >> 2)
        rows.append(jnp.take_along_axis(mixed, source, axis=1))
    return rows


def rows_at(h, ry):
    return pl.ds(CHUNK * h + ry, 8, stride=Q)


def strip_of(tm):
    across, along = lax.div(tm, SIDE), lax.rem(tm, SIDE)
    return across * SIDE + jnp.where(lax.rem(across, 2) == 0, along, SIDE - 1 - along)


def iotas():
    shape = (8, NZ)
    return lax.broadcasted_iota(jnp.int32, shape, 1), lax.broadcasted_iota(jnp.int32, shape, 0)


def has_neighbours(index, count):
    below = jnp.where(index == 0, 0.0, 1.0).astype(jnp.float32)
    above = jnp.where(index == count - 1, 0.0, 1.0).astype(jnp.float32)
    return below, above


def is_mirrored():
    return lax.rem(lax.axis_index("space"), 2) == 1


def next_chip_exists():
    index = lax.axis_index("space")
    at_end = (index == 0) | (index == lax.axis_size("space") - 1)
    return jnp.where(at_end, 0.0, 1.0).astype(jnp.float32)


def one_trip():
    return jnp.where(lax.axis_index("space") < 0, 2, 1)


def own_kernel(start, regions, resistivity, *refs):
    outs, (start_v, regions_v, half_v, resistivity_s, sems) = refs[:2], refs[2:]
    small = pltpu.make_async_copy(resistivity, resistivity_s, sems.at[4])
    small.start()
    copies = []
    odd = is_mirrored()
    for h in range(2):
        part = pl.ds(jnp.where(odd, 1 - h, h) * HALF, HALF)
        pair = (
            pltpu.make_async_copy(start.at[part], start_v.at[h], sems.at[2 * h]),
            pltpu.make_async_copy(regions.at[part], regions_v.at[h], sems.at[2 * h + 1]),
        )
        for copy in pair:
            copy.start()
        copies.append(pair)
    small.wait()
    scaled = [resistivity_s[i] * jnp.float32(0.5 * fine_step) for i in range(REGIONS)]
    for h in range(2):
        for copy in copies[h]:
            copy.wait()

        def first_pass(n, _, h=h):
            for x in (2 * n, 2 * n + 1):
                source = jnp.where(odd, HALF - 1 - x, x)
                for ry in range(Q):
                    for g in range(Q):
                        where = rows_at(g, ry)
                        region = regions_v[h, source, where, :]
                        value = jnp.zeros((8, NZ), jnp.float32)
                        for i in range(REGIONS):
                            value = jnp.where(region == i, scaled[i], value)
                        half_v[x, Q * ry + g] = turn(g, start_v[h, source, where, :])
                        half_v[HALF + x, Q * ry + g] = turn(g, value)
            return 0

        def second_pass(n, _, h=h):
            for x in (2 * n, 2 * n + 1):
                for ry in range(Q):
                    tiles = gather_tiles([half_v[x, Q * ry + g] for g in range(Q)])
                    for rz in range(Q):
                        outs[h][x, Q * ry + rz] = tiles[rz]
            return 0

        lax.fori_loop(0, HALF // 2, first_pass, 0)
        lax.fori_loop(0, HALF, second_pass, 0)


def own_part(start, regions, resistivity):
    hbm = pl.BlockSpec(memory_space=HBM)
    shape = jax.ShapeDtypeStruct((2 * HALF, PARTS, 8, NZ), jnp.float32)
    return pl.pallas_call(
        own_kernel,
        out_shape=(shape, shape),
        in_specs=[hbm] * 3,
        out_specs=(VMEM, VMEM),
        scratch_shapes=[
            pltpu.VMEM((2, HALF, NY, NZ), jnp.float32),
            pltpu.VMEM((2, HALF, NY, NZ), jnp.int32),
            pltpu.VMEM((2 * HALF, PARTS, 8, NZ), jnp.float32),
            pltpu.SMEM((REGIONS,), jnp.float32),
            pltpu.SemaphoreType.DMA((5,)),
        ],
        compiler_params=pltpu.CompilerParams(vmem_limit_bytes=8 << 20),
        name="own",
    )(*(pltpu.with_memory_space_constraint(a, HBM) for a in (start, regions, resistivity)))


class Fine:
    def __init__(self, u_ref, k_ref, e_ref, f_ref):
        self.u, self.k, self.e, self.f = u_ref, k_ref, e_ref, f_ref
        self.below = next_chip_exists()
        lane, sub = iotas()
        self.z_high, self.z_low = [(lane & (CHUNK - 1)) == v for v in (CHUNK - 1, 0)]
        self.y_high, self.y_low = sub == 7, sub == 0
        self.y_end = (sub == 7) & (lane >= NZ - CHUNK)
        self.y_start = (sub == 0) & (lane < CHUNK)

    def stage(self, ref, base, turn=False):
        def one(x, _):
            to = base + (HALF - 1 - x if turn else x)
            for r in range(PARTS):
                u, e = ref[x, r], ref[HALF + x, r]
                self.u[to, r] = u
                self.e[to, r] = e
                self.k[to, r] = coeff(e, u)
            return 0

        lax.fori_loop(0, HALF, one, 0)

    def above_y(self, v):
        turned = pltpu.roll(pltpu.roll(v, NZ - CHUNK, 1), 7, 0)
        v = jnp.where(self.y_high, turned, pltpu.roll(v, 7, 0))
        return jnp.where(self.y_end, 0.0, v)

    def plane(self, x, emit, next_u=None, next_k=None):
        f_ref = self.f
        if next_u is None:
            next_u, next_k = self.u.at[x + 1], self.k.at[x + 1]

        def at(ry, rz):
            return self.u[x, Q * ry + rz], self.k[x, Q * ry + rz]

        z_ends, y_tops, y_lows = [], [], []
        for ry in range(Q):
            (u0, k0), (u3, k3) = at(ry, 0), at(ry, Q - 1)
            un, kn = pltpu.roll(u0, NZ - 1, 1), pltpu.roll(k0, NZ - 1, 1)
            top = jnp.where(self.z_high, -(k3 * u3), (k3 + kn) * (un - u3))
            low = jnp.where(self.z_low, k0 * u0, pltpu.roll(top, 1, 1))
            z_ends.append((low, top))
        for rz in range(Q):
            (u0, k0), (u3, k3) = at(0, rz), at(Q - 1, rz)
            top = (k3 + self.above_y(k0)) * (self.above_y(u0) - u3)
            turned = pltpu.roll(pltpu.roll(top, CHUNK, 1), 1, 0)
            low = jnp.where(self.y_low, turned, pltpu.roll(top, 1, 0))
            y_tops.append(top)
            y_lows.append(jnp.where(self.y_start, k0 * u0, low))
        for ry in range(Q):
            z_low, z_top = z_ends[ry]
            u0, k0 = at(ry, 0)
            for rz in range(Q):
                r = Q * ry + rz
                if rz < Q - 1:
                    u1, k1 = at(ry, rz + 1)
                    z_up = (k0 + k1) * (u1 - u0)
                else:
                    u1 = k1 = None
                    z_up = z_top
                if ry < Q - 1:
                    un, kn = at(ry + 1, rz)
                    y_up = (k0 + kn) * (un - u0)
                else:
                    y_up = y_tops[rz]
                x_up = (k0 + next_k[r]) * (next_u[r] - u0)
                x_low = f_ref[r]
                f_ref[r] = x_up
                total = (x_up - x_low) + (y_up - y_lows[rz]) + (z_up - z_low)
                emit(x, r, u0, total)
                y_lows[rz], z_low = y_up, z_up
                u0, k0 = u1, k1

    def begin(self, x, low_u, low_k):
        for r in range(PARTS):
            self.f[r] = (low_k[r] + self.k[x, r]) * (self.u[x, r] - low_u[r])

    def stretches(self, first, count, size, emit):
        def stretch(n, _):
            for q in range(size):
                self.plane(first + size * n + q, emit)
            return 0

        lax.fori_loop(0, count, stretch, 0)

    def step(self, first, count, size, emit):
        self.begin(first, self.u.at[first - 1], self.k.at[first - 1])
        self.stretches(first, count, size, emit)

    def keep(self, x, r, u0, total):
        inside = jnp.where(x < BX, self.below, jnp.float32(1.0))
        new = inside * (u0 + total)
        self.u[x, r] = new
        self.k[x, r] = coeff(self.e[x, r], new)


def to_rows(tiles, rows):
    for ry in range(Q):
        parts = separate([tiles[Q * ry + rz] for rz in range(Q)])
        for h in range(Q):
            rows[rows_at(h, ry), :] = parts[h]


def inner_kernel(low, own_a, own_b, high, u_ref, k_ref, e_ref, g_ref, save, f_ref):
    later = jnp.where(lax.axis_index("tm") == 0, 0.0, 1.0).astype(jnp.float32)
    fine = Fine(u_ref, k_ref, e_ref, f_ref)
    for n, ref in enumerate((low, own_a, own_b, high)):
        fine.stage(ref, (n + 1) * HALF, turn=n in (0, 3))

    def keep_first(x, r, u0, total):
        g_ref[x - HALF, r] = later * (u0 + STEPS * total)
        fine.keep(x, r, u0, total)

    def stow(t):
        for r in range(PARTS):
            save[0, t, r] = u_ref[HALF + t, r]
            save[1, t, r] = k_ref[HALF + t, r]
            save[2, t, r] = u_ref[5 * HALF - 1 - t, r]
            save[3, t, r] = k_ref[5 * HALF - 1 - t, r]

    for t in range(1, HALF + 1):
        stow(t)
        fine.step(HALF + t, 2, BX - t, keep_first if t == 1 else fine.keep)


def outer_kernel(low, high, u_in, k_in, e_in, g_ref, save, out, u_ref, k_ref, e_ref, f_ref, s_ref):
    fine = Fine(u_ref, k_ref, e_ref, f_ref)
    fine.stage(low, 0, turn=True)
    fine.stage(high, 5 * HALF, turn=True)

    once = one_trip()

    def wedges(t, _):
        fine.begin(t, u_ref.at[t - 1], k_ref.at[t - 1])

        def low_side(_, carry):
            for q in range(HALF - 1):
                fine.plane(t + q, fine.keep)
            fine.plane(t + HALF - 1, fine.keep, save.at[0, t], save.at[1, t])
            return carry

        lax.fori_loop(0, once, low_side, 0)
        fine.begin(5 * HALF - t, save.at[2, t], save.at[3, t])
        fine.stretches(5 * HALF - t, once, HALF, fine.keep)
        return 0

    lax.fori_loop(1, HALF + 1, wedges, 0)
    for t in range(HALF + 1, STEPS):
        fine.step(t, 2, 3 * HALF - t, fine.keep)

    def keep_last(x, r, u0, total):
        u_ref[x - BX, r] = (u0 + total) - g_ref[x - HALF, r]

    fine.step(BX, 2, HALF, keep_last)

    def natural(n, _):
        for q in range(HALF):
            to_rows(u_ref.at[HALF * n + q], s_ref.at[HALF * n + q])
        return 0

    lax.fori_loop(0, 2, natural, 0)

    row = lax.broadcasted_iota(jnp.int32, (ROWS, NZ), 0)
    for j in range(SLICES):

        def tile(x, c, j=j):
            strip = ORDER[j] + c - 1
            if 0 <= strip < SLICES:
                return s_ref[x, strip * ROWS : (strip + 1) * ROWS, :]
            return jnp.zeros((ROWS, NZ), jnp.float32)

        low_end, high_end = tile(BX - 1, 0), tile(BX - 1, 2)
        for x in range(BX):
            out[j, x] = tile(x, 1)
        for x in range(BX - 1):
            shift = BX - 1 - x
            low = pltpu.roll(low_end, shift, 0) if shift else low_end
            high = pltpu.roll(high_end, shift, 0) if shift else high_end
            out[j, BX + x] = jnp.where(row == 0, low, tile(x, 0))
            out[j, 2 * BX - 1 + x] = jnp.where(row == ROWS - 1, high, tile(x, 2))


GRID = jax.ShapeDtypeStruct((3 * BX + 1, PARTS, 8, NZ), jnp.float32)


def inner(low, own_a, own_b, high):
    f32 = jnp.float32
    return pl.pallas_call(
        inner_kernel,
        out_shape=(
            GRID,
            GRID,
            GRID,
            jax.ShapeDtypeStruct((4 * HALF, PARTS, 8, NZ), f32),
            jax.ShapeDtypeStruct((4, HALF + 1, PARTS, 8, NZ), f32),
        ),
        in_specs=[VMEM] * 4,
        out_specs=(VMEM,) * 5,
        scratch_shapes=[pltpu.VMEM((PARTS, 8, NZ), f32)],
        compiler_params=pltpu.CompilerParams(vmem_limit_bytes=16 << 20),
        cost_estimate=pl.CostEstimate(flops=10**8, bytes_accessed=10**7, transcendentals=0),
        name="inner",
    )(low, own_a, own_b, high)


def outer(low, high, u, k, e, g, save):
    f32 = jnp.float32
    return pl.pallas_call(
        outer_kernel,
        out_shape=(jax.ShapeDtypeStruct((SLICES, LOAD, ROWS, NZ), f32), GRID, GRID, GRID),
        in_specs=[VMEM] * 7,
        out_specs=(VMEM,) * 4,
        scratch_shapes=[pltpu.VMEM((PARTS, 8, NZ), f32), pltpu.VMEM((BX, NY, NZ), f32)],
        input_output_aliases={2: 1, 3: 2, 4: 3},
        compiler_params=pltpu.CompilerParams(vmem_limit_bytes=16 << 20),
        name="outer",
    )(low, high, u, k, e, g, save)[0]


def own_tile(sent, ends, i, x, c):
    if c == 1:
        return sent[i, x]
    if x == BX - 1:
        return ends[i, c // 2]
    return sent[i, (BX if c == 0 else 2 * BX - 1) + x]


def pack_kernel(sent, down, up, ends):
    row = lax.broadcasted_iota(jnp.int32, (ROWS, NZ), 0)

    def rebuild(i, _):
        low, high = sent[i, 2 * BX - 2], sent[i, 3 * BX - 3]
        low = pltpu.roll(low, BX - 1, 0)
        for x in range(BX - 1):
            low = jnp.where(row == x + 1, pltpu.roll(sent[i, BX + x], x + 1, 0), low)
            high = jnp.where(row == x, pltpu.roll(sent[i, 2 * BX - 1 + x], (x + 1) % 8, 0), high)
        ends[i, 0] = low
        ends[i, 1] = high
        return 0

    lax.fori_loop(0, SLICES, rebuild, 0, unroll=4)
    for n, (i, d, kind) in enumerate(TILES):
        for ref, x in ((down, d - 1), (up, BX - d)):
            if kind == "mid":
                value = own_tile(sent, ends, i, x, 1)
            elif kind == "both":
                high, low = own_tile(sent, ends, i, x, 2), own_tile(sent, ends, i, x, 0)
                value = jnp.where(row < 4, high, low)
            else:
                value = own_tile(sent, ends, i, x, 0 if kind == "low" else 2)
            ref[n] = value


def pack(sent):
    shape = jax.ShapeDtypeStruct((len(TILES), ROWS, NZ), jnp.float32)
    return pl.pallas_call(
        pack_kernel,
        out_shape=(shape, shape, jax.ShapeDtypeStruct((SLICES, 2, ROWS, NZ), jnp.float32)),
        in_specs=[VMEM],
        out_specs=(VMEM,) * 3,
        compiler_params=pltpu.CompilerParams(vmem_limit_bytes=8 << 20),
        name="pack",
    )(sent)


def strip_kernel(*refs):
    own = strip_of(lax.axis_index("tm"))
    parts, (out, rows) = refs[:-2], refs[-2:]
    for n, ref in enumerate(parts):

        def natural(m, _, n=n, ref=ref):
            for x in (2 * m, 2 * m + 1):
                to = HALF - 1 - x if n in (0, 1, 4, 5) else x
                to_rows(ref.at[HALF + x], rows.at[n * HALF + to])
            return 0

        lax.fori_loop(0, HALF // 2, natural, 0)
    for c in range(3):
        strip = own + (c - 1)
        scale = jnp.where((strip >= 0) & (strip < SLICES), float(STEPS), 0.0).astype(jnp.float32)
        start = pl.multiple_of(jnp.clip(strip, 0, SLICES - 1) * ROWS, ROWS)
        for x in range(3 * BX):
            out[x, c] = scale * rows[x, pl.ds(start, ROWS), :]


def strip_part(*parts):
    return pl.pallas_call(
        strip_kernel,
        out_shape=jax.ShapeDtypeStruct((3 * BX, 3, 8, NZ), jnp.float32),
        in_specs=[VMEM] * len(parts),
        out_specs=VMEM,
        scratch_shapes=[pltpu.VMEM((3 * BX, NY, NZ), jnp.float32)],
        compiler_params=pltpu.CompilerParams(vmem_limit_bytes=8 << 20),
        cost_estimate=pl.CostEstimate(flops=10**6, bytes_accessed=10**6, transcendentals=0),
        name="strip",
    )(*parts)


def sent_tile(refs, i, x, c):
    sent, ends, below, above = refs
    if x < BX:
        return below[PLACE[i, BX - x, c]]
    if x >= 2 * BX:
        return above[PLACE[i, x - 2 * BX + 1, c]]
    return own_tile(sent, ends, i, x - BX, c)


def coarse_steps(count, base, eta, refs, u_ref, k_ref, f_ref, out):
    lane, row = iotas()
    x_below = next_chip_exists()
    y_below, y_above = has_neighbours(strip_of(lax.axis_index("tm")), SLICES)
    once = one_trip()

    def mask(x, c):
        factors = []
        if x < BX:
            factors.append(x_below)
        if c != 1:
            factors.append(y_below if c == 0 else y_above)
        return factors[0] * factors[1] if len(factors) == 2 else (factors or [None])[0]

    def begin(x, _):
        for c in range(3):
            k_ref[x, c] = coeff(eta[x, c], u_ref[x, c])
        return 0

    lax.fori_loop(BX - count, 2 * BX + count, begin, 0, unroll=4)

    def stretch(n, left, planes):
        def body(_, carry):
            flux = [None] * 3
            for x in planes:
                far = max(BX - x, x - (2 * BX - 1), 0)
                tiles = (0, 1, 2) if left - far >= 1 else (1,)
                us = [u_ref[x, c] for c in range(3)]
                ks = [k_ref[x, c] for c in range(3)]
                ru = [pltpu.roll(u, 7, 0) for u in us]
                rk = [pltpu.roll(k, 7, 0) for k in ks]
                ups = []
                for c in range(max(tiles) + 1):
                    un, kn = ru[c], rk[c]
                    if c < 2:
                        un = jnp.where(row == 7, ru[c + 1], un)
                        kn = jnp.where(row == 7, rk[c + 1], kn)
                    ups.append((ks[c] + kn) * (un - us[c]))
                rolled = [pltpu.roll(v, 1, 0) for v in ups]
                for c in tiles:
                    low = rolled[c]
                    if c > 0:
                        low = jnp.where(row == 0, rolled[c - 1], low)
                    u0, k0 = us[c], ks[c]
                    x_up = (k0 + k_ref[x + 1, c]) * (u_ref[x + 1, c] - u0)
                    x_low = flux[c]
                    if x_low is None:
                        if x == BX - (left if c == 1 else left - 1):
                            x_low = (k0 + k_ref[x - 1, c]) * (u0 - u_ref[x - 1, c])
                        else:
                            x_low = f_ref[c]
                    flux[c] = x_up
                    new = (u0 + (x_up - x_low) + (ups[c] - low) + z_flux(u0, k0, lane)) + (
                        sent_tile(refs, base + n, x, c)
                    )
                    m = mask(x, c)
                    if m is not None:
                        new = m * new
                    if left > 0:
                        u_ref[x, c] = new
                        k_ref[x, c] = coeff(eta[x, c], new)
                    if c == 1 and far == 0:
                        out(n, x - BX, new)
            for c in range(3):
                if flux[c] is not None:
                    f_ref[c] = flux[c]
            return carry

        lax.fori_loop(0, once, body, 0)

    for n in range(1, count + 1):
        left = count - n
        planes = list(range(BX - left, 2 * BX + left))
        parts = -(-len(planes) * (3 if left else 1) // GROUP)
        size = -(-len(planes) // parts)
        for a in range(0, len(planes), size):
            stretch(n, left, planes[a : a + size])


def first_kernel(eta, sent, ends, below, above, out, u_ref, k_ref, f_ref):
    refs = (sent, ends, below, above)
    for x in range(BX - FIRST, 2 * BX + FIRST):
        for c in range(3):
            if BX <= x < 2 * BX or c == 1 or max(BX - x, x - 2 * BX + 1) < FIRST:
                u_ref[x, c] = sent_tile(refs, 0, x, c)
            else:
                u_ref[x, c] = jnp.zeros((8, NZ), jnp.float32)
    for x in range(BX):
        out[0, x] = sent[0, x]

    def put(n, x, value):
        out[n, x] = value

    coarse_steps(FIRST, 0, eta, refs, u_ref, k_ref, f_ref, put)


def second_kernel(
    eta, sent, ends, below, above, low_u, own_u, high_u, done, out, u_ref, k_ref, f_ref
):
    odd = is_mirrored()

    def true_plane(x):
        return jnp.where(odd, BX - 1 - x, x)

    for b, ref in enumerate((low_u, own_u, high_u)):
        for x in range(BX):
            for c in range(3):
                to = b * BX + (x if b == 1 else BX - 1 - x)
                u_ref[to, c] = ref[x, c * ROWS : (c + 1) * ROWS, :]
    for i in range(FIRST + 1):
        for x in range(BX):
            out[i, true_plane(x)] = done[i, x]
    refs = (sent, ends, below, above)

    def put(n, x, value):
        out[FIRST + n, true_plane(x)] = value

    coarse_steps(SLICES - 1 - FIRST, FIRST, eta, refs, u_ref, k_ref, f_ref, put)


def coarse_call(kernel, name, count, *operands):
    f32 = jnp.float32
    return pl.pallas_call(
        kernel,
        out_shape=jax.ShapeDtypeStruct((count, BX, ROWS, NZ), f32),
        in_specs=[VMEM] * len(operands),
        out_specs=VMEM,
        scratch_shapes=[
            pltpu.VMEM((3 * BX, 3, 8, NZ), f32),
            pltpu.VMEM((3 * BX, 3, 8, NZ), f32),
            pltpu.VMEM((3, 8, NZ), f32),
        ],
        compiler_params=pltpu.CompilerParams(vmem_limit_bytes=8 << 20),
        name=name,
    )(*operands)


def place_kernel(strips, out, sems):
    copies = [
        pltpu.make_async_copy(
            strips.at[j], out.at[:, pl.ds(ORDER[j] * ROWS, ROWS), :], sems.at[j]
        )
        for j in range(SLICES)
    ]
    for copy in copies:
        copy.start()
    for copy in copies:
        copy.wait()


def place(strips):
    return pl.pallas_call(
        place_kernel,
        out_shape=jax.ShapeDtypeStruct((BX, NY, NZ), jnp.float32),
        in_specs=[VMEM],
        out_specs=pl.BlockSpec(memory_space=HBM),
        scratch_shapes=[pltpu.SemaphoreType.DMA((SLICES,))],
        compiler_params=pltpu.CompilerParams(vmem_limit_bytes=4 << 20),
        name="place",
    )(strips)


def across(value):
    count = lax.axis_size("space")
    pairs = [(i, i + 1) for i in range(1, count - 1, 2)]
    return lax.ppermute(value, "space", pairs + [(b, a) for a, b in pairs])


def beside(value):
    pairs = [(i, i + 1) for i in range(0, lax.axis_size("space"), 2)]
    return lax.ppermute(value, "space", pairs + [(b, a) for a, b in pairs])


def with_strips(state):
    sides = []
    for first in (0, 1):
        pairs = [(ORDER[q], ORDER[q + 1]) for q in range(first, SLICES - 1, 2)]
        sides.append(lax.ppermute(state, "tm", pairs + [(b, a) for a, b in pairs]))
    even = lax.rem(strip_of(lax.axis_index("tm")), 2) == 0
    low = jnp.where(even, sides[1], sides[0])
    high = jnp.where(even, sides[0], sides[1])
    return jnp.concatenate([low, state, high], axis=1)


def per_device(start_values, regions, resistivity):
    own_a, own_b = own_part(start_values[0], regions, resistivity)
    low_near, high_near = across(own_a), beside(own_b)
    low_far, high_far = across(own_b), beside(own_a)
    sent = outer(low_far, high_far, *inner(low_near, own_a, own_b, high_near))
    sent = lax.all_to_all(sent, "tm", 0, 0)
    down, up, ends = pack(sent)
    below, above = across(down), beside(up)
    eta = strip_part(low_far, low_near, own_a, own_b, high_near, high_far)
    done = coarse_call(first_kernel, "first", FIRST + 1, eta, sent, ends, below, above)
    strip = with_strips(done[FIRST])
    x_low, x_high = across(strip), beside(strip)
    ends = coarse_call(
        second_kernel, "second", SLICES, eta, sent, ends, below, above, x_low, strip, x_high, done
    )
    result = lax.all_to_all(ends, "tm", 0, 0)
    return place(result)[None]


def solution(mesh):
    in_specs = (P("tm", "space", None, None), P("space", None, None), P())
    out_specs = P("tm", "space", None, None)
    return jax.shard_map(
        per_device, mesh=mesh, in_specs=in_specs, out_specs=out_specs, check_vma=False
    )
```

```python
import jax
import jax.numpy as jnp
from jax import lax
from jax.experimental import pallas as pl
from jax.experimental.pallas import tpu as pltpu
from jax.sharding import PartitionSpec as P

STEPS = 8
fine_step = 0.008

SIDE = 4
ORDER = [a * SIDE + (b if a % 2 == 0 else SIDE - 1 - b) for a in range(SIDE) for b in range(SIDE)]
BX = 8
HALF = BX // 2
NY = 128
NZ = 128
SLICES = 16
REGIONS = 4
ROWS = 8
EXT = 3 * ROWS
SMEM = pl.BlockSpec(memory_space=pltpu.SMEM)
FIRST = 7
VMEM = pl.BlockSpec(memory_space=pltpu.VMEM)
HBM = pltpu.MemorySpace.HBM


def halo_depth(i):
    return FIRST - i if i <= FIRST else SLICES - 1 - i


def packed_tiles():
    tiles, groups = [], []
    for i in range(SLICES):
        depth = halo_depth(i)
        for d in range(1, depth + 1):
            tiles.append([(i, d, 1, ROWS, 0)])
            if depth > d:
                groups += [(depth - d, i, d, 0), (depth - d, i, d, 2)]
    used = []
    for rows, i, d, part in sorted(groups, reverse=True):
        for tile in used:
            start = sum(entry[3] for entry in tile)
            if start + rows <= ROWS:
                break
        else:
            tile, start = [], 0
            used.append(tile)
        tile.append((i, d, part, rows, start))
    return tiles + used


TILES = packed_tiles()
PLACE = {
    (i, d, part): (n, (start if part else start + rows) % ROWS)
    for n, tile in enumerate(TILES)
    for i, d, part, rows, start in tile
}
PARTS = NY // 8
LOAD = 3 * BX - 2
GROUP = 40


def coeff(eta, u):
    return eta * (2.0 - 1.0 / (1.0 + u * u))


def z_flux(u0, k0, lane):
    up = pltpu.roll(u0, NZ - 1, 1)
    kp = pltpu.roll(k0, NZ - 1, 1)
    edge = k0 * u0
    upper = jnp.where(lane == NZ - 1, -edge, (k0 + kp) * (up - u0))
    lower = jnp.where(lane == 0, edge, pltpu.roll(upper, 1, 1))
    return upper - lower


Q = 4
CHUNK = NZ // Q


def by_chunk(lane, values):
    low = jnp.where(lane < CHUNK, values[0], values[1])
    return jnp.where(lane < 2 * CHUNK, low, jnp.where(lane < 3 * CHUNK, values[2], values[3]))


def turn(h, rows):
    lane, _ = iotas()
    source = Q * (lane & (CHUNK - 1)) + (((lane >> 5) - h) & (Q - 1))
    return jnp.take_along_axis(rows, source, axis=1)


def gather_tiles(turned):
    lane, _ = iotas()
    tiles = []
    for rz in range(Q):
        tile = by_chunk(lane, [turned[(c - rz) % Q] for c in range(Q)])
        tiles.append(pltpu.roll(tile, NZ - CHUNK * rz, 1) if rz else tile)
    return tiles


def separate(tiles):
    lane, _ = iotas()
    turned = [pltpu.roll(t, CHUNK * rz, 1) if rz else t for rz, t in enumerate(tiles)]
    rows = []
    for h in range(Q):
        mixed = by_chunk(lane, [turned[(c - h) % Q] for c in range(Q)])
        source = CHUNK * (((lane & (Q - 1)) + h) & (Q - 1)) + (lane >> 2)
        rows.append(jnp.take_along_axis(mixed, source, axis=1))
    return rows


def rows_at(h, ry):
    return pl.ds(CHUNK * h + ry, 8, stride=Q)


def strip_of(tm):
    across, along = lax.div(tm, SIDE), lax.rem(tm, SIDE)
    return across * SIDE + jnp.where(lax.rem(across, 2) == 0, along, SIDE - 1 - along)


def iotas():
    shape = (8, NZ)
    return lax.broadcasted_iota(jnp.int32, shape, 1), lax.broadcasted_iota(jnp.int32, shape, 0)


def has_neighbours(index, count):
    below = jnp.where(index == 0, 0.0, 1.0).astype(jnp.float32)
    above = jnp.where(index == count - 1, 0.0, 1.0).astype(jnp.float32)
    return below, above


def is_mirrored():
    return lax.rem(lax.axis_index("space"), 2) == 1


def next_chip_exists():
    index = lax.axis_index("space")
    at_end = (index == 0) | (index == lax.axis_size("space") - 1)
    return jnp.where(at_end, 0.0, 1.0).astype(jnp.float32)


def one_trip():
    return jnp.where(lax.axis_index("space") < 0, 2, 1)


def own_kernel(start, regions, resistivity, *refs):
    outs, (start_v, regions_v, half_v, resistivity_s, sems) = refs[:2], refs[2:]
    small = pltpu.make_async_copy(resistivity, resistivity_s, sems.at[4])
    small.start()
    copies = []
    odd = is_mirrored()
    for h in range(2):
        part = pl.ds(jnp.where(odd, 1 - h, h) * HALF, HALF)
        pair = (
            pltpu.make_async_copy(start.at[part], start_v.at[h], sems.at[2 * h]),
            pltpu.make_async_copy(regions.at[part], regions_v.at[h], sems.at[2 * h + 1]),
        )
        for copy in pair:
            copy.start()
        copies.append(pair)
    small.wait()
    scaled = [resistivity_s[i] * jnp.float32(0.5 * fine_step) for i in range(REGIONS)]
    once = one_trip()
    for h in range(2):
        for copy in copies[h]:
            copy.wait()

        def first_pass(_, carry, h=h):
            for x in range(HALF):
                source = jnp.where(odd, HALF - 1 - x, x)
                for ry in range(Q):
                    for g in range(Q):
                        where = rows_at(g, ry)
                        region = regions_v[h, source, where, :]
                        value = jnp.zeros((8, NZ), jnp.float32)
                        for i in range(REGIONS):
                            value = jnp.where(region == i, scaled[i], value)
                        half_v[x, Q * ry + g] = turn(g, start_v[h, source, where, :])
                        half_v[HALF + x, Q * ry + g] = turn(g, value)
            return carry

        def second_pass(n, _, h=h):
            for x in [HALF * n + q for q in range(HALF)]:
                for ry in range(Q):
                    tiles = gather_tiles([half_v[x, Q * ry + g] for g in range(Q)])
                    for rz in range(Q):
                        outs[h][x, Q * ry + rz] = tiles[rz]
            return 0

        lax.fori_loop(0, once, first_pass, 0)
        lax.fori_loop(0, 2, second_pass, 0)


def own_part(start, regions, resistivity):
    hbm = pl.BlockSpec(memory_space=HBM)
    shape = jax.ShapeDtypeStruct((2 * HALF, PARTS, 8, NZ), jnp.float32)
    return pl.pallas_call(
        own_kernel,
        out_shape=(shape, shape),
        in_specs=[hbm] * 3,
        out_specs=(VMEM, VMEM),
        scratch_shapes=[
            pltpu.VMEM((2, HALF, NY, NZ), jnp.float32),
            pltpu.VMEM((2, HALF, NY, NZ), jnp.int32),
            pltpu.VMEM((2 * HALF, PARTS, 8, NZ), jnp.float32),
            pltpu.SMEM((REGIONS,), jnp.float32),
            pltpu.SemaphoreType.DMA((5,)),
        ],
        compiler_params=pltpu.CompilerParams(vmem_limit_bytes=8 << 20),
        name="own",
    )(*(pltpu.with_memory_space_constraint(a, HBM) for a in (start, regions, resistivity)))


class Fine:
    def __init__(self, u_ref, k_ref, e_ref, f_ref):
        self.u, self.k, self.e, self.f = u_ref, k_ref, e_ref, f_ref
        self.below = next_chip_exists()
        lane, sub = iotas()
        self.z_high, self.z_low = [(lane & (CHUNK - 1)) == v for v in (CHUNK - 1, 0)]
        self.y_high, self.y_low = sub == 7, sub == 0
        self.y_end = (sub == 7) & (lane >= NZ - CHUNK)
        self.y_start = (sub == 0) & (lane < CHUNK)

    def stage(self, ref, base, turn=False):
        def two(n, _):
            for x in (2 * n, 2 * n + 1):
                to = base + (HALF - 1 - x if turn else x)
                for r in range(PARTS):
                    u, e = ref[x, r], ref[HALF + x, r]
                    self.u[to, r] = u
                    self.e[to, r] = e
                    self.k[to, r] = coeff(e, u)
            return 0

        lax.fori_loop(0, HALF // 2, two, 0)

    def above_y(self, v):
        turned = pltpu.roll(pltpu.roll(v, NZ - CHUNK, 1), 7, 0)
        v = jnp.where(self.y_high, turned, pltpu.roll(v, 7, 0))
        return jnp.where(self.y_end, 0.0, v)

    def plane(self, x, emit, next_u=None, next_k=None):
        f_ref = self.f
        if next_u is None:
            next_u, next_k = self.u.at[x + 1], self.k.at[x + 1]

        def at(ry, rz):
            return self.u[x, Q * ry + rz], self.k[x, Q * ry + rz]

        z_ends, y_tops, y_lows = [], [], []
        for ry in range(Q):
            (u0, k0), (u3, k3) = at(ry, 0), at(ry, Q - 1)
            un, kn = pltpu.roll(u0, NZ - 1, 1), pltpu.roll(k0, NZ - 1, 1)
            top = jnp.where(self.z_high, -(k3 * u3), (k3 + kn) * (un - u3))
            low = jnp.where(self.z_low, k0 * u0, pltpu.roll(top, 1, 1))
            z_ends.append((low, top))
        for rz in range(Q):
            (u0, k0), (u3, k3) = at(0, rz), at(Q - 1, rz)
            top = (k3 + self.above_y(k0)) * (self.above_y(u0) - u3)
            turned = pltpu.roll(pltpu.roll(top, CHUNK, 1), 1, 0)
            low = jnp.where(self.y_low, turned, pltpu.roll(top, 1, 0))
            y_tops.append(top)
            y_lows.append(jnp.where(self.y_start, k0 * u0, low))
        for ry in range(Q):
            z_low, z_top = z_ends[ry]
            u0, k0 = at(ry, 0)
            for rz in range(Q):
                r = Q * ry + rz
                if rz < Q - 1:
                    u1, k1 = at(ry, rz + 1)
                    z_up = (k0 + k1) * (u1 - u0)
                else:
                    u1 = k1 = None
                    z_up = z_top
                if ry < Q - 1:
                    un, kn = at(ry + 1, rz)
                    y_up = (k0 + kn) * (un - u0)
                else:
                    y_up = y_tops[rz]
                x_up = (k0 + next_k[r]) * (next_u[r] - u0)
                x_low = f_ref[r]
                f_ref[r] = x_up
                total = (x_up - x_low) + (y_up - y_lows[rz]) + (z_up - z_low)
                emit(x, r, u0, total)
                y_lows[rz], z_low = y_up, z_up
                u0, k0 = u1, k1

    def begin(self, x, low_u, low_k):
        for r in range(PARTS):
            self.f[r] = (low_k[r] + self.k[x, r]) * (self.u[x, r] - low_u[r])

    def stretches(self, first, count, size, emit):
        def stretch(n, _):
            for q in range(size):
                self.plane(first + size * n + q, emit)
            return 0

        lax.fori_loop(0, count, stretch, 0)

    def step(self, first, count, size, emit):
        self.begin(first, self.u.at[first - 1], self.k.at[first - 1])
        self.stretches(first, count, size, emit)

    def keep(self, x, r, u0, total):
        inside = jnp.where(x < BX, self.below, jnp.float32(1.0))
        new = inside * (u0 + total)
        self.u[x, r] = new
        self.k[x, r] = coeff(self.e[x, r], new)


def to_rows(tiles, rows):
    for ry in range(Q):
        parts = separate([tiles[Q * ry + rz] for rz in range(Q)])
        for h in range(Q):
            rows[rows_at(h, ry), :] = parts[h]


def inner_kernel(low, own_a, own_b, high, u_ref, k_ref, e_ref, g_ref, save, f_ref):
    later = jnp.where(lax.axis_index("tm") == 0, 0.0, 1.0).astype(jnp.float32)
    fine = Fine(u_ref, k_ref, e_ref, f_ref)
    for n, ref in enumerate((low, own_a, own_b, high)):
        fine.stage(ref, (n + 1) * HALF, turn=n in (0, 3))

    def keep_first(x, r, u0, total):
        g_ref[x - HALF, r] = later * (u0 + STEPS * total)
        fine.keep(x, r, u0, total)

    def stow(t):
        for r in range(PARTS):
            save[0, t, r] = u_ref[HALF + t, r]
            save[1, t, r] = k_ref[HALF + t, r]
            save[2, t, r] = u_ref[5 * HALF - 1 - t, r]
            save[3, t, r] = k_ref[5 * HALF - 1 - t, r]

    for t in range(1, HALF + 1):
        stow(t)
        fine.step(HALF + t, 2, BX - t, keep_first if t == 1 else fine.keep)


def outer_kernel(low, high, u_in, k_in, e_in, g_ref, save, out, u_ref, k_ref, e_ref, f_ref, s_ref):
    fine = Fine(u_ref, k_ref, e_ref, f_ref)
    fine.stage(low, 0, turn=True)
    fine.stage(high, 5 * HALF, turn=True)

    once = one_trip()

    def wedges(t, _):
        fine.begin(t, u_ref.at[t - 1], k_ref.at[t - 1])

        def low_side(_, carry):
            for q in range(HALF - 1):
                fine.plane(t + q, fine.keep)
            fine.plane(t + HALF - 1, fine.keep, save.at[0, t], save.at[1, t])
            return carry

        lax.fori_loop(0, once, low_side, 0)
        fine.begin(5 * HALF - t, save.at[2, t], save.at[3, t])
        fine.stretches(5 * HALF - t, once, HALF, fine.keep)
        return 0

    lax.fori_loop(1, HALF + 1, wedges, 0)
    for t in range(HALF + 1, STEPS):
        fine.step(t, 2, 3 * HALF - t, fine.keep)

    def keep_last(x, r, u0, total):
        u_ref[x - BX, r] = (u0 + total) - g_ref[x - HALF, r]

    fine.step(BX, 2, HALF, keep_last)

    def natural(n, _):
        for q in range(HALF):
            to_rows(u_ref.at[HALF * n + q], s_ref.at[HALF * n + q])
        return 0

    lax.fori_loop(0, 2, natural, 0)

    row = lax.broadcasted_iota(jnp.int32, (ROWS, NZ), 0)
    for j in range(SLICES):

        def tile(x, c, j=j):
            strip = ORDER[j] + c - 1
            if 0 <= strip < SLICES:
                return s_ref[x, strip * ROWS : (strip + 1) * ROWS, :]
            return jnp.zeros((ROWS, NZ), jnp.float32)

        low_end, high_end = tile(BX - 1, 0), tile(BX - 1, 2)
        for x in range(BX):
            out[j, x] = tile(x, 1)
        for x in range(BX - 1):
            shift = BX - 1 - x
            low = pltpu.roll(low_end, shift, 0) if shift else low_end
            high = pltpu.roll(high_end, shift, 0) if shift else high_end
            out[j, BX + x] = jnp.where(row == 0, low, tile(x, 0))
            out[j, 2 * BX - 1 + x] = jnp.where(row == ROWS - 1, high, tile(x, 2))


GRID = jax.ShapeDtypeStruct((3 * BX + 1, PARTS, 8, NZ), jnp.float32)


def inner(low, own_a, own_b, high):
    f32 = jnp.float32
    return pl.pallas_call(
        inner_kernel,
        out_shape=(
            GRID,
            GRID,
            GRID,
            jax.ShapeDtypeStruct((4 * HALF, PARTS, 8, NZ), f32),
            jax.ShapeDtypeStruct((4, HALF + 1, PARTS, 8, NZ), f32),
        ),
        in_specs=[VMEM] * 4,
        out_specs=(VMEM,) * 5,
        scratch_shapes=[pltpu.VMEM((PARTS, 8, NZ), f32)],
        compiler_params=pltpu.CompilerParams(vmem_limit_bytes=16 << 20),
        cost_estimate=pl.CostEstimate(flops=10**8, bytes_accessed=10**7, transcendentals=0),
        name="inner",
    )(low, own_a, own_b, high)


def outer(low, high, u, k, e, g, save):
    f32 = jnp.float32
    return pl.pallas_call(
        outer_kernel,
        out_shape=(jax.ShapeDtypeStruct((SLICES, LOAD, ROWS, NZ), f32), GRID, GRID, GRID),
        in_specs=[VMEM] * 7,
        out_specs=(VMEM,) * 4,
        scratch_shapes=[pltpu.VMEM((PARTS, 8, NZ), f32), pltpu.VMEM((BX, NY, NZ), f32)],
        input_output_aliases={2: 1, 3: 2, 4: 3},
        compiler_params=pltpu.CompilerParams(vmem_limit_bytes=16 << 20),
        name="outer",
    )(low, high, u, k, e, g, save)[0]


def own_tile(sent, ends, i, x, c):
    if c == 1:
        return sent[i, x]
    if x == BX - 1:
        return ends[i, c // 2]
    return sent[i, (BX if c == 0 else 2 * BX - 1) + x]


def pack_kernel(sent, down, up, ends):
    row = lax.broadcasted_iota(jnp.int32, (ROWS, NZ), 0)

    def rebuild(i, _):
        low, high = sent[i, 2 * BX - 2], sent[i, 3 * BX - 3]
        low = pltpu.roll(low, BX - 1, 0)
        for x in range(BX - 1):
            low = jnp.where(row == x + 1, pltpu.roll(sent[i, BX + x], x + 1, 0), low)
            high = jnp.where(row == x, pltpu.roll(sent[i, 2 * BX - 1 + x], (x + 1) % 8, 0), high)
        ends[i, 0] = low
        ends[i, 1] = high
        return 0

    lax.fori_loop(0, SLICES, rebuild, 0, unroll=4)
    for n, tile in enumerate(TILES):
        for ref, near in ((down, True), (up, False)):
            value = None
            for i, d, part, rows, start in tile:
                part_of = own_tile(sent, ends, i, d - 1 if near else BX - d, part)
                shift = PLACE[i, d, part][1]
                if shift:
                    part_of = pltpu.roll(part_of, shift, 0)
                value = part_of if value is None else jnp.where(row >= start, part_of, value)
            ref[n] = value


def pack(sent):
    shape = jax.ShapeDtypeStruct((len(TILES), ROWS, NZ), jnp.float32)
    return pl.pallas_call(
        pack_kernel,
        out_shape=(shape, shape, jax.ShapeDtypeStruct((SLICES, 2, ROWS, NZ), jnp.float32)),
        in_specs=[VMEM],
        out_specs=(VMEM,) * 3,
        compiler_params=pltpu.CompilerParams(vmem_limit_bytes=8 << 20),
        name="pack",
    )(sent)


def strip_kernel(*refs):
    own = strip_of(lax.axis_index("tm"))
    parts, (out, rows) = refs[:-2], refs[-2:]
    for n, ref in enumerate(parts):

        def natural(m, _, n=n, ref=ref):
            for x in (2 * m, 2 * m + 1):
                to = HALF - 1 - x if n in (0, 1, 4, 5) else x
                to_rows(ref.at[HALF + x], rows.at[n * HALF + to])
            return 0

        lax.fori_loop(0, HALF // 2, natural, 0)
    for c in range(3):
        strip = own + (c - 1)
        scale = jnp.where((strip >= 0) & (strip < SLICES), float(STEPS), 0.0).astype(jnp.float32)
        start = pl.multiple_of(jnp.clip(strip, 0, SLICES - 1) * ROWS, ROWS)
        for x in range(3 * BX):
            out[x, c] = scale * rows[x, pl.ds(start, ROWS), :]


def strip_part(*parts):
    return pl.pallas_call(
        strip_kernel,
        out_shape=jax.ShapeDtypeStruct((3 * BX, 3, 8, NZ), jnp.float32),
        in_specs=[VMEM] * len(parts),
        out_specs=VMEM,
        scratch_shapes=[pltpu.VMEM((3 * BX, NY, NZ), jnp.float32)],
        compiler_params=pltpu.CompilerParams(vmem_limit_bytes=8 << 20),
        cost_estimate=pl.CostEstimate(flops=10**6, bytes_accessed=10**6, transcendentals=0),
        name="strip",
    )(*parts)


def sent_tile(refs, i, x, c):
    sent, ends, below, above = refs
    if x < BX or x >= 2 * BX:
        ref, d = (below, BX - x) if x < BX else (above, x - 2 * BX + 1)
        n, shift = PLACE[i, d, c]
        return pltpu.roll(ref[n], ROWS - shift, 0) if shift else ref[n]
    return own_tile(sent, ends, i, x - BX, c)


def coarse_steps(count, base, eta, refs, u_ref, k_ref, f_ref, out):
    lane, row = iotas()
    x_below = next_chip_exists()
    y_below, y_above = has_neighbours(strip_of(lax.axis_index("tm")), SLICES)
    once = one_trip()

    def mask(x, c):
        factors = []
        if x < BX:
            factors.append(x_below)
        if c != 1:
            factors.append(y_below if c == 0 else y_above)
        return factors[0] * factors[1] if len(factors) == 2 else (factors or [None])[0]

    def begin(x, _):
        for c in range(3):
            k_ref[x, c] = coeff(eta[x, c], u_ref[x, c])
        return 0

    lax.fori_loop(BX - count, 2 * BX + count, begin, 0, unroll=4)

    def stretch(n, left, planes):
        def body(_, carry):
            flux = [None] * 3
            for x in planes:
                far = max(BX - x, x - (2 * BX - 1), 0)
                tiles = (0, 1, 2) if left - far >= 1 else (1,)
                us = [u_ref[x, c] for c in range(3)]
                ks = [k_ref[x, c] for c in range(3)]
                ru = [pltpu.roll(u, 7, 0) for u in us]
                rk = [pltpu.roll(k, 7, 0) for k in ks]
                ups = []
                for c in range(max(tiles) + 1):
                    un, kn = ru[c], rk[c]
                    if c < 2:
                        un = jnp.where(row == 7, ru[c + 1], un)
                        kn = jnp.where(row == 7, rk[c + 1], kn)
                    ups.append((ks[c] + kn) * (un - us[c]))
                rolled = [pltpu.roll(v, 1, 0) for v in ups]
                for c in tiles:
                    low = rolled[c]
                    if c > 0:
                        low = jnp.where(row == 0, rolled[c - 1], low)
                    u0, k0 = us[c], ks[c]
                    x_up = (k0 + k_ref[x + 1, c]) * (u_ref[x + 1, c] - u0)
                    x_low = flux[c]
                    if x_low is None:
                        if x == BX - (left if c == 1 else left - 1):
                            x_low = (k0 + k_ref[x - 1, c]) * (u0 - u_ref[x - 1, c])
                        else:
                            x_low = f_ref[c]
                    flux[c] = x_up
                    new = (u0 + (x_up - x_low) + (ups[c] - low) + z_flux(u0, k0, lane)) + (
                        sent_tile(refs, base + n, x, c)
                    )
                    m = mask(x, c)
                    if m is not None:
                        new = m * new
                    if left > 0:
                        u_ref[x, c] = new
                        k_ref[x, c] = coeff(eta[x, c], new)
                    if c == 1 and far == 0:
                        out(n, x - BX, new)
            for c in range(3):
                if flux[c] is not None:
                    f_ref[c] = flux[c]
            return carry

        lax.fori_loop(0, once, body, 0)

    for n in range(1, count + 1):
        left = count - n
        planes = list(range(BX - left, 2 * BX + left))
        parts = -(-len(planes) * (3 if left else 1) // GROUP)
        size = -(-len(planes) // parts)
        for a in range(0, len(planes), size):
            stretch(n, left, planes[a : a + size])


def first_kernel(eta, sent, ends, below, above, out, u_ref, k_ref, f_ref):
    refs = (sent, ends, below, above)
    for x in range(BX - FIRST, 2 * BX + FIRST):
        for c in range(3):
            if BX <= x < 2 * BX or c == 1 or max(BX - x, x - 2 * BX + 1) < FIRST:
                u_ref[x, c] = sent_tile(refs, 0, x, c)
            else:
                u_ref[x, c] = jnp.zeros((8, NZ), jnp.float32)
    for x in range(BX):
        out[0, x] = sent[0, x]

    def put(n, x, value):
        out[n, x] = value

    coarse_steps(FIRST, 0, eta, refs, u_ref, k_ref, f_ref, put)


def second_kernel(
    eta, sent, ends, below, above, low_u, own_u, high_u, done, out, u_ref, k_ref, f_ref
):
    odd = is_mirrored()

    def true_plane(x):
        return jnp.where(odd, BX - 1 - x, x)

    for b, ref in enumerate((low_u, own_u, high_u)):
        for x in range(BX):
            for c in range(3):
                to = b * BX + (x if b == 1 else BX - 1 - x)
                u_ref[to, c] = ref[x, c * ROWS : (c + 1) * ROWS, :]
    for i in range(FIRST + 1):
        for x in range(BX):
            out[i, true_plane(x)] = done[i, x]
    refs = (sent, ends, below, above)

    def put(n, x, value):
        out[FIRST + n, true_plane(x)] = value

    coarse_steps(SLICES - 1 - FIRST, FIRST, eta, refs, u_ref, k_ref, f_ref, put)


def coarse_call(kernel, name, count, *operands):
    f32 = jnp.float32
    return pl.pallas_call(
        kernel,
        out_shape=jax.ShapeDtypeStruct((count, BX, ROWS, NZ), f32),
        in_specs=[VMEM] * len(operands),
        out_specs=VMEM,
        scratch_shapes=[
            pltpu.VMEM((3 * BX, 3, 8, NZ), f32),
            pltpu.VMEM((3 * BX, 3, 8, NZ), f32),
            pltpu.VMEM((3, 8, NZ), f32),
        ],
        compiler_params=pltpu.CompilerParams(vmem_limit_bytes=8 << 20),
        name=name,
    )(*operands)


def place_kernel(strips, out, sems):
    copies = [
        pltpu.make_async_copy(
            strips.at[j], out.at[:, pl.ds(ORDER[j] * ROWS, ROWS), :], sems.at[j]
        )
        for j in range(SLICES)
    ]
    for copy in copies:
        copy.start()
    for copy in copies:
        copy.wait()


def place(strips):
    return pl.pallas_call(
        place_kernel,
        out_shape=jax.ShapeDtypeStruct((BX, NY, NZ), jnp.float32),
        in_specs=[VMEM],
        out_specs=pl.BlockSpec(memory_space=HBM),
        scratch_shapes=[pltpu.SemaphoreType.DMA((SLICES,))],
        compiler_params=pltpu.CompilerParams(vmem_limit_bytes=4 << 20),
        name="place",
    )(strips)


def across(value):
    count = lax.axis_size("space")
    pairs = [(i, i + 1) for i in range(1, count - 1, 2)]
    return lax.ppermute(value, "space", pairs + [(b, a) for a, b in pairs])


def beside(value):
    pairs = [(i, i + 1) for i in range(0, lax.axis_size("space"), 2)]
    return lax.ppermute(value, "space", pairs + [(b, a) for a, b in pairs])


def with_strips(state):
    sides = []
    for first in (0, 1):
        pairs = [(ORDER[q], ORDER[q + 1]) for q in range(first, SLICES - 1, 2)]
        sides.append(lax.ppermute(state, "tm", pairs + [(b, a) for a, b in pairs]))
    even = lax.rem(strip_of(lax.axis_index("tm")), 2) == 0
    low = jnp.where(even, sides[1], sides[0])
    high = jnp.where(even, sides[0], sides[1])
    return jnp.concatenate([low, state, high], axis=1)


def per_device(start_values, regions, resistivity):
    own_a, own_b = own_part(start_values[0], regions, resistivity)
    low_near, high_near = across(own_a), beside(own_b)
    low_far, high_far = across(own_b), beside(own_a)
    sent = outer(low_far, high_far, *inner(low_near, own_a, own_b, high_near))
    sent = lax.all_to_all(sent, "tm", 0, 0)
    down, up, ends = pack(sent)
    below, above = across(down), beside(up)
    eta = strip_part(low_far, low_near, own_a, own_b, high_near, high_far)
    done = coarse_call(first_kernel, "first", FIRST + 1, eta, sent, ends, below, above)
    strip = with_strips(done[FIRST])
    x_low, x_high = across(strip), beside(strip)
    ends = coarse_call(
        second_kernel, "second", SLICES, eta, sent, ends, below, above, x_low, strip, x_high, done
    )
    result = lax.all_to_all(ends, "tm", 0, 0)
    return place(result)[None]


def solution(mesh):
    in_specs = (P("tm", "space", None, None), P("space", None, None), P())
    out_specs = P("tm", "space", None, None)
    return jax.shard_map(
        per_device, mesh=mesh, in_specs=in_specs, out_specs=out_specs, check_vma=False
    )
```

```python
import jax
import jax.numpy as jnp
from jax import lax
from jax.experimental import pallas as pl
from jax.experimental.pallas import tpu as pltpu
from jax.sharding import PartitionSpec as P

STEPS = 8
fine_step = 0.008

SIDE = 4
ORDER = [a * SIDE + (b if a % 2 == 0 else SIDE - 1 - b) for a in range(SIDE) for b in range(SIDE)]
BX = 8
HALF = BX // 2
NY = 128
NZ = 128
SLICES = 16
REGIONS = 4
ROWS = 8
EXT = 3 * ROWS
SMEM = pl.BlockSpec(memory_space=pltpu.SMEM)
FIRST = 7
VMEM = pl.BlockSpec(memory_space=pltpu.VMEM)
HBM = pltpu.MemorySpace.HBM


def halo_depth(i):
    return FIRST - i if i <= FIRST else SLICES - 1 - i


def packed_tiles():
    tiles, groups = [], []
    for i in range(SLICES):
        depth = halo_depth(i)
        for d in range(1, depth + 1):
            tiles.append([(i, d, 1, ROWS, 0)])
            if depth > d:
                groups += [(depth - d, i, d, 0), (depth - d, i, d, 2)]
    used = []
    for rows, i, d, part in sorted(groups, reverse=True):
        for tile in used:
            start = sum(entry[3] for entry in tile)
            if start + rows <= ROWS:
                break
        else:
            tile, start = [], 0
            used.append(tile)
        tile.append((i, d, part, rows, start))
    return tiles + used


TILES = packed_tiles()
PLACE = {
    (i, d, part): (n, (start if part else start + rows) % ROWS)
    for n, tile in enumerate(TILES)
    for i, d, part, rows, start in tile
}
PARTS = NY // 8
LOAD = 3 * BX - 2
GROUP = 40


def coeff(eta, u):
    return eta * (2.0 - 1.0 / (1.0 + u * u))


def z_flux(u0, k0, lane):
    up = pltpu.roll(u0, NZ - 1, 1)
    kp = pltpu.roll(k0, NZ - 1, 1)
    edge = k0 * u0
    upper = jnp.where(lane == NZ - 1, -edge, (k0 + kp) * (up - u0))
    lower = jnp.where(lane == 0, edge, pltpu.roll(upper, 1, 1))
    return upper - lower


Q = 4
CHUNK = NZ // Q


def by_chunk(lane, values):
    low = jnp.where(lane < CHUNK, values[0], values[1])
    return jnp.where(lane < 2 * CHUNK, low, jnp.where(lane < 3 * CHUNK, values[2], values[3]))


def turn(h, rows):
    lane, _ = iotas()
    source = Q * (lane & (CHUNK - 1)) + (((lane >> 5) - h) & (Q - 1))
    return jnp.take_along_axis(rows, source, axis=1)


def gather_tiles(turned):
    lane, _ = iotas()
    tiles = []
    for rz in range(Q):
        tile = by_chunk(lane, [turned[(c - rz) % Q] for c in range(Q)])
        tiles.append(pltpu.roll(tile, NZ - CHUNK * rz, 1) if rz else tile)
    return tiles


def separate(tiles):
    lane, _ = iotas()
    turned = [pltpu.roll(t, CHUNK * rz, 1) if rz else t for rz, t in enumerate(tiles)]
    rows = []
    for h in range(Q):
        mixed = by_chunk(lane, [turned[(c - h) % Q] for c in range(Q)])
        source = CHUNK * (((lane & (Q - 1)) + h) & (Q - 1)) + (lane >> 2)
        rows.append(jnp.take_along_axis(mixed, source, axis=1))
    return rows


def rows_at(h, ry):
    return pl.ds(CHUNK * h + ry, 8, stride=Q)


def strip_of(tm):
    across, along = lax.div(tm, SIDE), lax.rem(tm, SIDE)
    return across * SIDE + jnp.where(lax.rem(across, 2) == 0, along, SIDE - 1 - along)


def iotas():
    shape = (8, NZ)
    return lax.broadcasted_iota(jnp.int32, shape, 1), lax.broadcasted_iota(jnp.int32, shape, 0)


def has_neighbours(index, count):
    below = jnp.where(index == 0, 0.0, 1.0).astype(jnp.float32)
    above = jnp.where(index == count - 1, 0.0, 1.0).astype(jnp.float32)
    return below, above


def is_mirrored():
    return lax.rem(lax.axis_index("space"), 2) == 1


def next_chip_exists():
    index = lax.axis_index("space")
    at_end = (index == 0) | (index == lax.axis_size("space") - 1)
    return jnp.where(at_end, 0.0, 1.0).astype(jnp.float32)


def one_trip():
    return jnp.where(lax.axis_index("space") < 0, 2, 1)


def own_kernel(start, regions, resistivity, *refs):
    outs, (start_v, regions_v, half_v, resistivity_s, sems) = refs[:2], refs[2:]
    small = pltpu.make_async_copy(resistivity, resistivity_s, sems.at[4])
    small.start()
    copies = []
    odd = is_mirrored()
    for h in range(2):
        part = pl.ds(jnp.where(odd, 1 - h, h) * HALF, HALF)
        pair = (
            pltpu.make_async_copy(start.at[part], start_v.at[h], sems.at[2 * h]),
            pltpu.make_async_copy(regions.at[part], regions_v.at[h], sems.at[2 * h + 1]),
        )
        for copy in pair:
            copy.start()
        copies.append(pair)
    small.wait()
    scaled = [resistivity_s[i] * jnp.float32(0.5 * fine_step) for i in range(REGIONS)]
    once = one_trip()
    for h in range(2):
        for copy in copies[h]:
            copy.wait()

        def first_pass(_, carry, h=h):
            for x in range(HALF):
                source = jnp.where(odd, HALF - 1 - x, x)
                for ry in range(Q):
                    for g in range(Q):
                        where = rows_at(g, ry)
                        region = regions_v[h, source, where, :]
                        value = jnp.zeros((8, NZ), jnp.float32)
                        for i in range(REGIONS):
                            value = jnp.where(region == i, scaled[i], value)
                        half_v[x, Q * ry + g] = turn(g, start_v[h, source, where, :])
                        half_v[HALF + x, Q * ry + g] = turn(g, value)
            return carry

        def second_pass(n, _, h=h):
            for x in [HALF * n + q for q in range(HALF)]:
                for ry in range(Q):
                    tiles = gather_tiles([half_v[x, Q * ry + g] for g in range(Q)])
                    for rz in range(Q):
                        outs[h][x, Q * ry + rz] = tiles[rz]
            return 0

        lax.fori_loop(0, once, first_pass, 0)
        lax.fori_loop(0, 2, second_pass, 0)


def own_part(start, regions, resistivity):
    hbm = pl.BlockSpec(memory_space=HBM)
    shape = jax.ShapeDtypeStruct((2 * HALF, PARTS, 8, NZ), jnp.float32)
    return pl.pallas_call(
        own_kernel,
        out_shape=(shape, shape),
        in_specs=[hbm] * 3,
        out_specs=(VMEM, VMEM),
        scratch_shapes=[
            pltpu.VMEM((2, HALF, NY, NZ), jnp.float32),
            pltpu.VMEM((2, HALF, NY, NZ), jnp.int32),
            pltpu.VMEM((2 * HALF, PARTS, 8, NZ), jnp.float32),
            pltpu.SMEM((REGIONS,), jnp.float32),
            pltpu.SemaphoreType.DMA((5,)),
        ],
        compiler_params=pltpu.CompilerParams(vmem_limit_bytes=8 << 20),
        name="own",
    )(*(pltpu.with_memory_space_constraint(a, HBM) for a in (start, regions, resistivity)))


class Fine:
    def __init__(self, u_ref, k_ref, e_ref, f_ref):
        self.u, self.k, self.e, self.f = u_ref, k_ref, e_ref, f_ref
        self.below = next_chip_exists()
        lane, sub = iotas()
        self.z_high, self.z_low = [(lane & (CHUNK - 1)) == v for v in (CHUNK - 1, 0)]
        self.y_high, self.y_low = sub == 7, sub == 0
        self.y_end = (sub == 7) & (lane >= NZ - CHUNK)
        self.y_start = (sub == 0) & (lane < CHUNK)

    def stage(self, ref, base, turn=False):
        def two(n, _):
            for x in (2 * n, 2 * n + 1):
                to = base + (HALF - 1 - x if turn else x)
                for r in range(PARTS):
                    u, e = ref[x, r], ref[HALF + x, r]
                    self.u[to, r] = u
                    self.e[to, r] = e
                    self.k[to, r] = coeff(e, u)
            return 0

        lax.fori_loop(0, HALF // 2, two, 0)

    def above_y(self, v):
        turned = pltpu.roll(pltpu.roll(v, NZ - CHUNK, 1), 7, 0)
        v = jnp.where(self.y_high, turned, pltpu.roll(v, 7, 0))
        return jnp.where(self.y_end, 0.0, v)

    def plane(self, x, emit, next_u=None, next_k=None):
        f_ref = self.f
        if next_u is None:
            next_u, next_k = self.u.at[x + 1], self.k.at[x + 1]

        def at(ry, rz):
            return self.u[x, Q * ry + rz], self.k[x, Q * ry + rz]

        z_ends, y_tops, y_lows = [], [], []
        for ry in range(Q):
            (u0, k0), (u3, k3) = at(ry, 0), at(ry, Q - 1)
            un, kn = pltpu.roll(u0, NZ - 1, 1), pltpu.roll(k0, NZ - 1, 1)
            top = jnp.where(self.z_high, -(k3 * u3), (k3 + kn) * (un - u3))
            low = jnp.where(self.z_low, k0 * u0, pltpu.roll(top, 1, 1))
            z_ends.append((low, top))
        for rz in range(Q):
            (u0, k0), (u3, k3) = at(0, rz), at(Q - 1, rz)
            top = (k3 + self.above_y(k0)) * (self.above_y(u0) - u3)
            turned = pltpu.roll(pltpu.roll(top, CHUNK, 1), 1, 0)
            low = jnp.where(self.y_low, turned, pltpu.roll(top, 1, 0))
            y_tops.append(top)
            y_lows.append(jnp.where(self.y_start, k0 * u0, low))
        for ry in range(Q):
            z_low, z_top = z_ends[ry]
            u0, k0 = at(ry, 0)
            for rz in range(Q):
                r = Q * ry + rz
                if rz < Q - 1:
                    u1, k1 = at(ry, rz + 1)
                    z_up = (k0 + k1) * (u1 - u0)
                else:
                    u1 = k1 = None
                    z_up = z_top
                if ry < Q - 1:
                    un, kn = at(ry + 1, rz)
                    y_up = (k0 + kn) * (un - u0)
                else:
                    y_up = y_tops[rz]
                x_up = (k0 + next_k[r]) * (next_u[r] - u0)
                x_low = f_ref[r]
                f_ref[r] = x_up
                total = (x_up - x_low) + (y_up - y_lows[rz]) + (z_up - z_low)
                emit(x, r, u0, total)
                y_lows[rz], z_low = y_up, z_up
                u0, k0 = u1, k1

    def begin(self, x, low_u, low_k):
        for r in range(PARTS):
            self.f[r] = (low_k[r] + self.k[x, r]) * (self.u[x, r] - low_u[r])

    def stretches(self, first, count, size, emit):
        def stretch(n, _):
            for q in range(size):
                self.plane(first + size * n + q, emit)
            return 0

        lax.fori_loop(0, count, stretch, 0)

    def step(self, first, count, size, emit):
        self.begin(first, self.u.at[first - 1], self.k.at[first - 1])
        self.stretches(first, count, size, emit)

    def keep(self, x, r, u0, total):
        inside = jnp.where(x < BX, self.below, jnp.float32(1.0))
        new = inside * (u0 + total)
        self.u[x, r] = new
        self.k[x, r] = coeff(self.e[x, r], new)


def to_rows(tiles, rows):
    for ry in range(Q):
        parts = separate([tiles[Q * ry + rz] for rz in range(Q)])
        for h in range(Q):
            rows[rows_at(h, ry), :] = parts[h]


def inner_kernel(low, own_a, own_b, high, u_ref, k_ref, e_ref, g_ref, save, f_ref):
    later = jnp.where(lax.axis_index("tm") == 0, 0.0, 1.0).astype(jnp.float32)
    fine = Fine(u_ref, k_ref, e_ref, f_ref)
    for n, ref in enumerate((low, own_a, own_b, high)):
        fine.stage(ref, (n + 1) * HALF, turn=n in (0, 3))

    def keep_first(x, r, u0, total):
        g_ref[x - HALF, r] = later * (u0 + STEPS * total)
        fine.keep(x, r, u0, total)

    def stow(t):
        for r in range(PARTS):
            save[0, t, r] = u_ref[HALF + t, r]
            save[1, t, r] = k_ref[HALF + t, r]
            save[2, t, r] = u_ref[5 * HALF - 1 - t, r]
            save[3, t, r] = k_ref[5 * HALF - 1 - t, r]

    for t in range(1, HALF + 1):
        stow(t)
        fine.step(HALF + t, 2, BX - t, keep_first if t == 1 else fine.keep)


def outer_kernel(low, high, u_in, k_in, e_in, g_ref, save, out, u_ref, k_ref, e_ref, f_ref, s_ref):
    fine = Fine(u_ref, k_ref, e_ref, f_ref)
    fine.stage(low, 0, turn=True)
    fine.stage(high, 5 * HALF, turn=True)

    once = one_trip()

    def wedges(t, _):
        fine.begin(t, u_ref.at[t - 1], k_ref.at[t - 1])

        def low_side(_, carry):
            for q in range(HALF - 1):
                fine.plane(t + q, fine.keep)
            fine.plane(t + HALF - 1, fine.keep, save.at[0, t], save.at[1, t])
            return carry

        lax.fori_loop(0, once, low_side, 0)
        fine.begin(5 * HALF - t, save.at[2, t], save.at[3, t])
        fine.stretches(5 * HALF - t, once, HALF, fine.keep)
        return 0

    lax.fori_loop(1, HALF + 1, wedges, 0)
    for t in range(HALF + 1, STEPS):
        fine.step(t, 2, 3 * HALF - t, fine.keep)

    def keep_last(x, r, u0, total):
        u_ref[x - BX, r] = (u0 + total) - g_ref[x - HALF, r]

    fine.step(BX, 2, HALF, keep_last)

    def natural(n, _):
        for q in range(HALF):
            to_rows(u_ref.at[HALF * n + q], s_ref.at[HALF * n + q])
        return 0

    lax.fori_loop(0, 2, natural, 0)

    row = lax.broadcasted_iota(jnp.int32, (ROWS, NZ), 0)
    for j in range(SLICES):

        def tile(x, c, j=j):
            strip = ORDER[j] + c - 1
            if 0 <= strip < SLICES:
                return s_ref[x, strip * ROWS : (strip + 1) * ROWS, :]
            return jnp.zeros((ROWS, NZ), jnp.float32)

        low_end, high_end = tile(BX - 1, 0), tile(BX - 1, 2)
        for x in range(BX):
            out[j, x] = tile(x, 1)
        for x in range(BX - 1):
            shift = BX - 1 - x
            low = pltpu.roll(low_end, shift, 0) if shift else low_end
            high = pltpu.roll(high_end, shift, 0) if shift else high_end
            out[j, BX + x] = jnp.where(row == 0, low, tile(x, 0))
            out[j, 2 * BX - 1 + x] = jnp.where(row == ROWS - 1, high, tile(x, 2))


GRID = jax.ShapeDtypeStruct((3 * BX + 1, PARTS, 8, NZ), jnp.float32)


def inner(low, own_a, own_b, high):
    f32 = jnp.float32
    return pl.pallas_call(
        inner_kernel,
        out_shape=(
            GRID,
            GRID,
            GRID,
            jax.ShapeDtypeStruct((4 * HALF, PARTS, 8, NZ), f32),
            jax.ShapeDtypeStruct((4, HALF + 1, PARTS, 8, NZ), f32),
        ),
        in_specs=[VMEM] * 4,
        out_specs=(VMEM,) * 5,
        scratch_shapes=[pltpu.VMEM((PARTS, 8, NZ), f32)],
        compiler_params=pltpu.CompilerParams(vmem_limit_bytes=16 << 20),
        cost_estimate=pl.CostEstimate(flops=10**8, bytes_accessed=10**7, transcendentals=0),
        name="inner",
    )(low, own_a, own_b, high)


def outer(low, high, u, k, e, g, save):
    f32 = jnp.float32
    return pl.pallas_call(
        outer_kernel,
        out_shape=(jax.ShapeDtypeStruct((SLICES, LOAD, ROWS, NZ), f32), GRID, GRID, GRID),
        in_specs=[VMEM] * 7,
        out_specs=(VMEM,) * 4,
        scratch_shapes=[pltpu.VMEM((PARTS, 8, NZ), f32), pltpu.VMEM((BX, NY, NZ), f32)],
        input_output_aliases={2: 1, 3: 2, 4: 3},
        compiler_params=pltpu.CompilerParams(vmem_limit_bytes=16 << 20),
        name="outer",
    )(low, high, u, k, e, g, save)[0]


def own_tile(sent, ends, i, x, c):
    if c == 1:
        return sent[i, x]
    if x == BX - 1:
        return ends[i, c // 2]
    return sent[i, (BX if c == 0 else 2 * BX - 1) + x]


def pack_kernel(sent, down, up, ends):
    row = lax.broadcasted_iota(jnp.int32, (ROWS, NZ), 0)

    def rebuild(i, _):
        low, high = sent[i, 2 * BX - 2], sent[i, 3 * BX - 3]
        low = pltpu.roll(low, BX - 1, 0)
        for x in range(BX - 1):
            low = jnp.where(row == x + 1, pltpu.roll(sent[i, BX + x], x + 1, 0), low)
            high = jnp.where(row == x, pltpu.roll(sent[i, 2 * BX - 1 + x], (x + 1) % 8, 0), high)
        ends[i, 0] = low
        ends[i, 1] = high
        return 0

    lax.fori_loop(0, SLICES, rebuild, 0, unroll=4)
    for n, tile in enumerate(TILES):
        for ref, near in ((down, True), (up, False)):
            value = None
            for i, d, part, rows, start in tile:
                part_of = own_tile(sent, ends, i, d - 1 if near else BX - d, part)
                shift = PLACE[i, d, part][1]
                if shift:
                    part_of = pltpu.roll(part_of, shift, 0)
                value = part_of if value is None else jnp.where(row >= start, part_of, value)
            ref[n] = value


def pack(sent):
    shape = jax.ShapeDtypeStruct((len(TILES), ROWS, NZ), jnp.float32)
    return pl.pallas_call(
        pack_kernel,
        out_shape=(shape, shape, jax.ShapeDtypeStruct((SLICES, 2, ROWS, NZ), jnp.float32)),
        in_specs=[VMEM],
        out_specs=(VMEM,) * 3,
        compiler_params=pltpu.CompilerParams(vmem_limit_bytes=8 << 20),
        name="pack",
    )(sent)


def strip_kernel(*refs):
    own = strip_of(lax.axis_index("tm"))
    parts, out = refs[:-1], refs[-1]
    lane, _ = iotas()
    for c in range(3):
        strip = own + (c - 1)
        scale = jnp.where((strip >= 0) & (strip < SLICES), float(STEPS), 0.0).astype(jnp.float32)
        strip = jnp.clip(strip, 0, SLICES - 1)
        h, s0 = lax.div(strip, Q), 2 * lax.rem(strip, Q)
        source = CHUNK * h + (lane >> 2)
        for n, ref in enumerate(parts):
            for x in range(HALF):
                turned = []
                for rz in range(Q):
                    halves = [
                        ref[HALF + x, pl.ds(8 * rz + s0 + ds, Q, stride=8 * Q), :]
                        for ds in range(2)
                    ]
                    both = jnp.concatenate(halves, axis=0)
                    turned.append(jnp.take_along_axis(both, source, axis=1))
                low = jnp.where((lane & 3) == 0, turned[0], turned[1])
                high = jnp.where((lane & 3) == 2, turned[2], turned[3])
                value = jnp.where((lane & 3) < 2, low, high)
                to = HALF - 1 - x if n in (0, 1, 4, 5) else x
                out[n * HALF + to, c] = scale * value


def strip_part(*parts):
    flat = [a.reshape(2 * HALF, NY, NZ) for a in parts]
    return pl.pallas_call(
        strip_kernel,
        out_shape=jax.ShapeDtypeStruct((3 * BX, 3, 8, NZ), jnp.float32),
        in_specs=[VMEM] * len(parts),
        out_specs=VMEM,
        compiler_params=pltpu.CompilerParams(vmem_limit_bytes=8 << 20),
        cost_estimate=pl.CostEstimate(flops=10**6, bytes_accessed=10**6, transcendentals=0),
        name="strip",
    )(*flat)


def sent_tile(refs, i, x, c):
    sent, ends, below, above = refs
    if x < BX or x >= 2 * BX:
        ref, d = (below, BX - x) if x < BX else (above, x - 2 * BX + 1)
        n, shift = PLACE[i, d, c]
        return pltpu.roll(ref[n], ROWS - shift, 0) if shift else ref[n]
    return own_tile(sent, ends, i, x - BX, c)


def coarse_steps(count, base, eta, refs, u_ref, k_ref, f_ref, out):
    lane, row = iotas()
    x_below = next_chip_exists()
    y_below, y_above = has_neighbours(strip_of(lax.axis_index("tm")), SLICES)
    once = one_trip()

    def mask(x, c):
        factors = []
        if x < BX:
            factors.append(x_below)
        if c != 1:
            factors.append(y_below if c == 0 else y_above)
        return factors[0] * factors[1] if len(factors) == 2 else (factors or [None])[0]

    def begin(x, _):
        for c in range(3):
            k_ref[x, c] = coeff(eta[x, c], u_ref[x, c])
        return 0

    lax.fori_loop(BX - count, 2 * BX + count, begin, 0, unroll=4)

    def stretch(n, left, planes):
        def body(_, carry):
            flux = [None] * 3
            for x in planes:
                far = max(BX - x, x - (2 * BX - 1), 0)
                tiles = (0, 1, 2) if left - far >= 1 else (1,)
                us = [u_ref[x, c] for c in range(3)]
                ks = [k_ref[x, c] for c in range(3)]
                ru = [pltpu.roll(u, 7, 0) for u in us]
                rk = [pltpu.roll(k, 7, 0) for k in ks]
                ups = []
                for c in range(max(tiles) + 1):
                    un, kn = ru[c], rk[c]
                    if c < 2:
                        un = jnp.where(row == 7, ru[c + 1], un)
                        kn = jnp.where(row == 7, rk[c + 1], kn)
                    ups.append((ks[c] + kn) * (un - us[c]))
                rolled = [pltpu.roll(v, 1, 0) for v in ups]
                for c in tiles:
                    low = rolled[c]
                    if c > 0:
                        low = jnp.where(row == 0, rolled[c - 1], low)
                    u0, k0 = us[c], ks[c]
                    x_up = (k0 + k_ref[x + 1, c]) * (u_ref[x + 1, c] - u0)
                    x_low = flux[c]
                    if x_low is None:
                        if x == BX - (left if c == 1 else left - 1):
                            x_low = (k0 + k_ref[x - 1, c]) * (u0 - u_ref[x - 1, c])
                        else:
                            x_low = f_ref[c]
                    flux[c] = x_up
                    new = (u0 + (x_up - x_low) + (ups[c] - low) + z_flux(u0, k0, lane)) + (
                        sent_tile(refs, base + n, x, c)
                    )
                    m = mask(x, c)
                    if m is not None:
                        new = m * new
                    if left > 0:
                        u_ref[x, c] = new
                        k_ref[x, c] = coeff(eta[x, c], new)
                    if c == 1 and far == 0:
                        out(n, x - BX, new)
            for c in range(3):
                if flux[c] is not None:
                    f_ref[c] = flux[c]
            return carry

        lax.fori_loop(0, once, body, 0)

    for n in range(1, count + 1):
        left = count - n
        planes = list(range(BX - left, 2 * BX + left))
        parts = -(-len(planes) * (3 if left else 1) // GROUP)
        size = -(-len(planes) // parts)
        for a in range(0, len(planes), size):
            stretch(n, left, planes[a : a + size])


def first_kernel(eta, sent, ends, below, above, out, u_ref, k_ref, f_ref):
    refs = (sent, ends, below, above)
    for x in range(BX - FIRST, 2 * BX + FIRST):
        for c in range(3):
            if BX <= x < 2 * BX or c == 1 or max(BX - x, x - 2 * BX + 1) < FIRST:
                u_ref[x, c] = sent_tile(refs, 0, x, c)
            else:
                u_ref[x, c] = jnp.zeros((8, NZ), jnp.float32)
    for x in range(BX):
        out[0, x] = sent[0, x]

    def put(n, x, value):
        out[n, x] = value

    coarse_steps(FIRST, 0, eta, refs, u_ref, k_ref, f_ref, put)


def second_kernel(
    eta, sent, ends, below, above, low_u, own_u, high_u, done, out, u_ref, k_ref, f_ref
):
    odd = is_mirrored()

    def true_plane(x):
        return jnp.where(odd, BX - 1 - x, x)

    for b, ref in enumerate((low_u, own_u, high_u)):
        for x in range(BX):
            for c in range(3):
                to = b * BX + (x if b == 1 else BX - 1 - x)
                u_ref[to, c] = ref[x, c * ROWS : (c + 1) * ROWS, :]
    for i in range(FIRST + 1):
        for x in range(BX):
            out[i, true_plane(x)] = done[i, x]
    refs = (sent, ends, below, above)

    def put(n, x, value):
        out[FIRST + n, true_plane(x)] = value

    coarse_steps(SLICES - 1 - FIRST, FIRST, eta, refs, u_ref, k_ref, f_ref, put)


def coarse_call(kernel, name, count, *operands):
    f32 = jnp.float32
    return pl.pallas_call(
        kernel,
        out_shape=jax.ShapeDtypeStruct((count, BX, ROWS, NZ), f32),
        in_specs=[VMEM] * len(operands),
        out_specs=VMEM,
        scratch_shapes=[
            pltpu.VMEM((3 * BX, 3, 8, NZ), f32),
            pltpu.VMEM((3 * BX, 3, 8, NZ), f32),
            pltpu.VMEM((3, 8, NZ), f32),
        ],
        compiler_params=pltpu.CompilerParams(vmem_limit_bytes=8 << 20),
        name=name,
    )(*operands)


def place_kernel(strips, out, sems):
    copies = [
        pltpu.make_async_copy(
            strips.at[j], out.at[:, pl.ds(ORDER[j] * ROWS, ROWS), :], sems.at[j]
        )
        for j in range(SLICES)
    ]
    for copy in copies:
        copy.start()
    for copy in copies:
        copy.wait()


def place(strips):
    return pl.pallas_call(
        place_kernel,
        out_shape=jax.ShapeDtypeStruct((BX, NY, NZ), jnp.float32),
        in_specs=[VMEM],
        out_specs=pl.BlockSpec(memory_space=HBM),
        scratch_shapes=[pltpu.SemaphoreType.DMA((SLICES,))],
        compiler_params=pltpu.CompilerParams(vmem_limit_bytes=4 << 20),
        name="place",
    )(strips)


def across(value):
    count = lax.axis_size("space")
    pairs = [(i, i + 1) for i in range(1, count - 1, 2)]
    return lax.ppermute(value, "space", pairs + [(b, a) for a, b in pairs])


def beside(value):
    pairs = [(i, i + 1) for i in range(0, lax.axis_size("space"), 2)]
    return lax.ppermute(value, "space", pairs + [(b, a) for a, b in pairs])


def with_strips(state):
    sides = []
    for first in (0, 1):
        pairs = [(ORDER[q], ORDER[q + 1]) for q in range(first, SLICES - 1, 2)]
        sides.append(lax.ppermute(state, "tm", pairs + [(b, a) for a, b in pairs]))
    even = lax.rem(strip_of(lax.axis_index("tm")), 2) == 0
    low = jnp.where(even, sides[1], sides[0])
    high = jnp.where(even, sides[0], sides[1])
    return jnp.concatenate([low, state, high], axis=1)


def per_device(start_values, regions, resistivity):
    own_a, own_b = own_part(start_values[0], regions, resistivity)
    low_near, high_near = across(own_a), beside(own_b)
    low_far, high_far = across(own_b), beside(own_a)
    sent = outer(low_far, high_far, *inner(low_near, own_a, own_b, high_near))
    sent = lax.all_to_all(sent, "tm", 0, 0)
    down, up, ends = pack(sent)
    below, above = across(down), beside(up)
    eta = strip_part(low_far, low_near, own_a, own_b, high_near, high_far)
    done = coarse_call(first_kernel, "first", FIRST + 1, eta, sent, ends, below, above)
    strip = with_strips(done[FIRST])
    x_low, x_high = across(strip), beside(strip)
    ends = coarse_call(
        second_kernel, "second", SLICES, eta, sent, ends, below, above, x_low, strip, x_high, done
    )
    result = lax.all_to_all(ends, "tm", 0, 0)
    return place(result)[None]


def solution(mesh):
    in_specs = (P("tm", "space", None, None), P("space", None, None), P())
    out_specs = P("tm", "space", None, None)
    return jax.shard_map(
        per_device, mesh=mesh, in_specs=in_specs, out_specs=out_specs, check_vma=False
    )
```

```python
import jax
import jax.numpy as jnp
from jax import lax
from jax.experimental import pallas as pl
from jax.experimental.pallas import tpu as pltpu
from jax.sharding import PartitionSpec as P

STEPS = 8
fine_step = 0.008

SIDE = 4
ORDER = [a * SIDE + (b if a % 2 == 0 else SIDE - 1 - b) for a in range(SIDE) for b in range(SIDE)]
BX = 8
HALF = BX // 2
NY = 128
NZ = 128
SLICES = 16
REGIONS = 4
ROWS = 8
SMEM = pl.BlockSpec(memory_space=pltpu.SMEM)
FIRST = 7
VMEM = pl.BlockSpec(memory_space=pltpu.VMEM)
HBM = pltpu.MemorySpace.HBM


def halo_depth(i):
    return FIRST - i if i <= FIRST else SLICES - 1 - i


def packed_tiles():
    tiles, groups = [], []
    for i in range(SLICES):
        depth = halo_depth(i)
        for d in range(1, depth + 1):
            tiles.append([(i, d, 1, ROWS, 0)])
            if depth > d:
                groups += [(depth - d, i, d, 0), (depth - d, i, d, 2)]
    used = []
    for rows, i, d, part in sorted(groups, reverse=True):
        for tile in used:
            start = sum(entry[3] for entry in tile)
            if start + rows <= ROWS:
                break
        else:
            tile, start = [], 0
            used.append(tile)
        tile.append((i, d, part, rows, start))
    return tiles + used


TILES = packed_tiles()
PLACE = {
    (i, d, part): (n, (start if part else start + rows) % ROWS)
    for n, tile in enumerate(TILES)
    for i, d, part, rows, start in tile
}
PARTS = NY // 8
LOAD = 3 * BX - 2
GROUP = 40


def coeff(eta, u):
    return eta * (2.0 - 1.0 / (1.0 + u * u))


def z_flux(u0, k0, lane):
    up = pltpu.roll(u0, NZ - 1, 1)
    kp = pltpu.roll(k0, NZ - 1, 1)
    edge = k0 * u0
    upper = jnp.where(lane == NZ - 1, -edge, (k0 + kp) * (up - u0))
    lower = jnp.where(lane == 0, edge, pltpu.roll(upper, 1, 1))
    return upper - lower


Q = 4
CHUNK = NZ // Q


def by_chunk(lane, values):
    low = jnp.where(lane < CHUNK, values[0], values[1])
    return jnp.where(lane < 2 * CHUNK, low, jnp.where(lane < 3 * CHUNK, values[2], values[3]))


def turn(h, rows):
    lane, _ = iotas()
    source = Q * (lane & (CHUNK - 1)) + (((lane >> 5) - h) & (Q - 1))
    return jnp.take_along_axis(rows, source, axis=1)


def gather_tiles(turned):
    lane, _ = iotas()
    tiles = []
    for rz in range(Q):
        tile = by_chunk(lane, [turned[(c - rz) % Q] for c in range(Q)])
        tiles.append(pltpu.roll(tile, NZ - CHUNK * rz, 1) if rz else tile)
    return tiles


def separate(tiles):
    lane, _ = iotas()
    turned = [pltpu.roll(t, CHUNK * rz, 1) if rz else t for rz, t in enumerate(tiles)]
    rows = []
    for h in range(Q):
        mixed = by_chunk(lane, [turned[(c - h) % Q] for c in range(Q)])
        source = CHUNK * (((lane & (Q - 1)) + h) & (Q - 1)) + (lane >> 2)
        rows.append(jnp.take_along_axis(mixed, source, axis=1))
    return rows


def rows_at(h, ry):
    return pl.ds(CHUNK * h + ry, 8, stride=Q)


def strip_of(tm):
    across, along = lax.div(tm, SIDE), lax.rem(tm, SIDE)
    return across * SIDE + jnp.where(lax.rem(across, 2) == 0, along, SIDE - 1 - along)


def iotas():
    shape = (8, NZ)
    return lax.broadcasted_iota(jnp.int32, shape, 1), lax.broadcasted_iota(jnp.int32, shape, 0)


def has_neighbours(index, count):
    below = jnp.where(index == 0, 0.0, 1.0).astype(jnp.float32)
    above = jnp.where(index == count - 1, 0.0, 1.0).astype(jnp.float32)
    return below, above


def is_mirrored():
    return lax.rem(lax.axis_index("space"), 2) == 1


def next_chip_exists():
    index = lax.axis_index("space")
    at_end = (index == 0) | (index == lax.axis_size("space") - 1)
    return jnp.where(at_end, 0.0, 1.0).astype(jnp.float32)


def one_trip():
    return jnp.where(lax.axis_index("space") < 0, 2, 1)


def own_kernel(start, regions, resistivity, *refs):
    outs, (start_v, regions_v, half_v, resistivity_s, sems) = refs[:2], refs[2:]
    small = pltpu.make_async_copy(resistivity, resistivity_s, sems.at[4])
    small.start()
    copies = []
    odd = is_mirrored()
    for h in range(2):
        part = pl.ds(jnp.where(odd, 1 - h, h) * HALF, HALF)
        pair = (
            pltpu.make_async_copy(start.at[part], start_v.at[h], sems.at[2 * h]),
            pltpu.make_async_copy(regions.at[part], regions_v.at[h], sems.at[2 * h + 1]),
        )
        for copy in pair:
            copy.start()
        copies.append(pair)
    small.wait()
    scaled = [resistivity_s[i] * jnp.float32(0.5 * fine_step) for i in range(REGIONS)]
    once = one_trip()
    for h in range(2):
        for copy in copies[h]:
            copy.wait()

        def first_pass(_, carry, h=h):
            for x in range(HALF):
                source = jnp.where(odd, HALF - 1 - x, x)
                for ry in range(Q):
                    for g in range(Q):
                        where = rows_at(g, ry)
                        region = regions_v[h, source, where, :]
                        value = jnp.zeros((8, NZ), jnp.float32)
                        for i in range(REGIONS):
                            value = jnp.where(region == i, scaled[i], value)
                        half_v[x, Q * ry + g] = turn(g, start_v[h, source, where, :])
                        half_v[HALF + x, Q * ry + g] = turn(g, value)
            return carry

        def second_pass(n, _, h=h):
            for x in [HALF * n + q for q in range(HALF)]:
                for ry in range(Q):
                    tiles = gather_tiles([half_v[x, Q * ry + g] for g in range(Q)])
                    for rz in range(Q):
                        outs[h][x, Q * ry + rz] = tiles[rz]
            return 0

        lax.fori_loop(0, once, first_pass, 0)
        lax.fori_loop(0, 2, second_pass, 0)


def own_part(start, regions, resistivity):
    hbm = pl.BlockSpec(memory_space=HBM)
    shape = jax.ShapeDtypeStruct((2 * HALF, PARTS, 8, NZ), jnp.float32)
    return pl.pallas_call(
        own_kernel,
        out_shape=(shape, shape),
        in_specs=[hbm] * 3,
        out_specs=(VMEM, VMEM),
        scratch_shapes=[
            pltpu.VMEM((2, HALF, NY, NZ), jnp.float32),
            pltpu.VMEM((2, HALF, NY, NZ), jnp.int32),
            pltpu.VMEM((2 * HALF, PARTS, 8, NZ), jnp.float32),
            pltpu.SMEM((REGIONS,), jnp.float32),
            pltpu.SemaphoreType.DMA((5,)),
        ],
        compiler_params=pltpu.CompilerParams(vmem_limit_bytes=8 << 20),
        name="own",
    )(*(pltpu.with_memory_space_constraint(a, HBM) for a in (start, regions, resistivity)))


class Fine:
    def __init__(self, u_ref, k_ref, e_ref, f_ref):
        self.u, self.k, self.e, self.f = u_ref, k_ref, e_ref, f_ref
        self.below = next_chip_exists()
        lane, sub = iotas()
        self.z_high, self.z_low = [(lane & (CHUNK - 1)) == v for v in (CHUNK - 1, 0)]
        self.y_high, self.y_low = sub == 7, sub == 0
        self.y_end = (sub == 7) & (lane >= NZ - CHUNK)
        self.y_start = (sub == 0) & (lane < CHUNK)

    def stage(self, ref, base, turn=False):
        def two(n, _):
            for x in (2 * n, 2 * n + 1):
                to = base + (HALF - 1 - x if turn else x)
                for r in range(PARTS):
                    u, e = ref[x, r], ref[HALF + x, r]
                    self.u[to, r] = u
                    self.e[to, r] = e
                    self.k[to, r] = coeff(e, u)
            return 0

        lax.fori_loop(0, HALF // 2, two, 0)

    def above_y(self, v):
        turned = pltpu.roll(pltpu.roll(v, NZ - CHUNK, 1), 7, 0)
        v = jnp.where(self.y_high, turned, pltpu.roll(v, 7, 0))
        return jnp.where(self.y_end, 0.0, v)

    def plane(self, x, emit, next_u=None, next_k=None):
        f_ref = self.f
        if next_u is None:
            next_u, next_k = self.u.at[x + 1], self.k.at[x + 1]

        def at(ry, rz):
            return self.u[x, Q * ry + rz], self.k[x, Q * ry + rz]

        z_ends, y_tops, y_lows = [], [], []
        for ry in range(Q):
            (u0, k0), (u3, k3) = at(ry, 0), at(ry, Q - 1)
            un, kn = pltpu.roll(u0, NZ - 1, 1), pltpu.roll(k0, NZ - 1, 1)
            top = jnp.where(self.z_high, -(k3 * u3), (k3 + kn) * (un - u3))
            low = jnp.where(self.z_low, k0 * u0, pltpu.roll(top, 1, 1))
            z_ends.append((low, top))
        for rz in range(Q):
            (u0, k0), (u3, k3) = at(0, rz), at(Q - 1, rz)
            top = (k3 + self.above_y(k0)) * (self.above_y(u0) - u3)
            turned = pltpu.roll(pltpu.roll(top, CHUNK, 1), 1, 0)
            low = jnp.where(self.y_low, turned, pltpu.roll(top, 1, 0))
            y_tops.append(top)
            y_lows.append(jnp.where(self.y_start, k0 * u0, low))
        for ry in range(Q):
            z_low, z_top = z_ends[ry]
            u0, k0 = at(ry, 0)
            for rz in range(Q):
                r = Q * ry + rz
                if rz < Q - 1:
                    u1, k1 = at(ry, rz + 1)
                    z_up = (k0 + k1) * (u1 - u0)
                else:
                    u1 = k1 = None
                    z_up = z_top
                if ry < Q - 1:
                    un, kn = at(ry + 1, rz)
                    y_up = (k0 + kn) * (un - u0)
                else:
                    y_up = y_tops[rz]
                x_up = (k0 + next_k[r]) * (next_u[r] - u0)
                x_low = f_ref[r]
                f_ref[r] = x_up
                total = (x_up - x_low) + (y_up - y_lows[rz]) + (z_up - z_low)
                emit(x, r, u0, total)
                y_lows[rz], z_low = y_up, z_up
                u0, k0 = u1, k1

    def begin(self, x, low_u, low_k):
        for r in range(PARTS):
            self.f[r] = (low_k[r] + self.k[x, r]) * (self.u[x, r] - low_u[r])

    def stretches(self, first, count, size, emit):
        def stretch(n, _):
            for q in range(size):
                self.plane(first + size * n + q, emit)
            return 0

        lax.fori_loop(0, count, stretch, 0)

    def step(self, first, count, size, emit):
        self.begin(first, self.u.at[first - 1], self.k.at[first - 1])
        self.stretches(first, count, size, emit)

    def keep(self, x, r, u0, total):
        inside = jnp.where(x < BX, self.below, jnp.float32(1.0))
        new = inside * (u0 + total)
        self.u[x, r] = new
        self.k[x, r] = coeff(self.e[x, r], new)


def to_rows(tiles, rows):
    for ry in range(Q):
        parts = separate([tiles[Q * ry + rz] for rz in range(Q)])
        for h in range(Q):
            rows[rows_at(h, ry), :] = parts[h]


def inner_kernel(low, own_a, own_b, high, u_ref, k_ref, e_ref, g_ref, save, f_ref):
    later = jnp.where(lax.axis_index("tm") == 0, 0.0, 1.0).astype(jnp.float32)
    fine = Fine(u_ref, k_ref, e_ref, f_ref)
    for n, ref in enumerate((low, own_a, own_b, high)):
        fine.stage(ref, (n + 1) * HALF, turn=n in (0, 3))

    def keep_first(x, r, u0, total):
        g_ref[x - HALF, r] = later * (u0 + STEPS * total)
        fine.keep(x, r, u0, total)

    def stow(t):
        for r in range(PARTS):
            save[0, t, r] = u_ref[HALF + t, r]
            save[1, t, r] = k_ref[HALF + t, r]
            save[2, t, r] = u_ref[5 * HALF - 1 - t, r]
            save[3, t, r] = k_ref[5 * HALF - 1 - t, r]

    for t in range(1, HALF + 1):
        stow(t)
        fine.step(HALF + t, 2, BX - t, keep_first if t == 1 else fine.keep)


def outer_kernel(low, high, u_in, k_in, e_in, g_ref, save, out, u_ref, k_ref, e_ref, f_ref, s_ref):
    fine = Fine(u_ref, k_ref, e_ref, f_ref)
    fine.stage(low, 0, turn=True)
    fine.stage(high, 5 * HALF, turn=True)

    once = one_trip()

    def wedges(t, _):
        fine.begin(t, u_ref.at[t - 1], k_ref.at[t - 1])

        def low_side(_, carry):
            for q in range(HALF - 1):
                fine.plane(t + q, fine.keep)
            fine.plane(t + HALF - 1, fine.keep, save.at[0, t], save.at[1, t])
            return carry

        lax.fori_loop(0, once, low_side, 0)
        fine.begin(5 * HALF - t, save.at[2, t], save.at[3, t])
        fine.stretches(5 * HALF - t, once, HALF, fine.keep)
        return 0

    lax.fori_loop(1, HALF + 1, wedges, 0)
    for t in range(HALF + 1, STEPS):
        fine.step(t, 2, 3 * HALF - t, fine.keep)

    def keep_last(x, r, u0, total):
        u_ref[x - BX, r] = (u0 + total) - g_ref[x - HALF, r]

    fine.step(BX, 2, HALF, keep_last)

    def natural(n, _):
        for q in range(HALF):
            to_rows(u_ref.at[HALF * n + q], s_ref.at[HALF * n + q])
        return 0

    lax.fori_loop(0, 2, natural, 0)

    row = lax.broadcasted_iota(jnp.int32, (ROWS, NZ), 0)
    for j in range(SLICES):

        def tile(x, c, j=j):
            strip = ORDER[j] + c - 1
            if 0 <= strip < SLICES:
                return s_ref[x, strip * ROWS : (strip + 1) * ROWS, :]
            return jnp.zeros((ROWS, NZ), jnp.float32)

        low_end, high_end = tile(BX - 1, 0), tile(BX - 1, 2)
        for x in range(BX):
            out[j, x] = tile(x, 1)
        for x in range(BX - 1):
            shift = BX - 1 - x
            low = pltpu.roll(low_end, shift, 0) if shift else low_end
            high = pltpu.roll(high_end, shift, 0) if shift else high_end
            out[j, BX + x] = jnp.where(row == 0, low, tile(x, 0))
            out[j, 2 * BX - 1 + x] = jnp.where(row == ROWS - 1, high, tile(x, 2))


GRID = jax.ShapeDtypeStruct((3 * BX + 1, PARTS, 8, NZ), jnp.float32)


def inner(low, own_a, own_b, high):
    f32 = jnp.float32
    return pl.pallas_call(
        inner_kernel,
        out_shape=(
            GRID,
            GRID,
            GRID,
            jax.ShapeDtypeStruct((4 * HALF, PARTS, 8, NZ), f32),
            jax.ShapeDtypeStruct((4, HALF + 1, PARTS, 8, NZ), f32),
        ),
        in_specs=[VMEM] * 4,
        out_specs=(VMEM,) * 5,
        scratch_shapes=[pltpu.VMEM((PARTS, 8, NZ), f32)],
        compiler_params=pltpu.CompilerParams(vmem_limit_bytes=16 << 20),
        cost_estimate=pl.CostEstimate(flops=10**8, bytes_accessed=10**7, transcendentals=0),
        name="inner",
    )(low, own_a, own_b, high)


def outer(low, high, u, k, e, g, save):
    f32 = jnp.float32
    return pl.pallas_call(
        outer_kernel,
        out_shape=(jax.ShapeDtypeStruct((SLICES, LOAD, ROWS, NZ), f32), GRID, GRID, GRID),
        in_specs=[VMEM] * 7,
        out_specs=(VMEM,) * 4,
        scratch_shapes=[pltpu.VMEM((PARTS, 8, NZ), f32), pltpu.VMEM((BX, NY, NZ), f32)],
        input_output_aliases={2: 1, 3: 2, 4: 3},
        compiler_params=pltpu.CompilerParams(vmem_limit_bytes=16 << 20),
        name="outer",
    )(low, high, u, k, e, g, save)[0]


def own_tile(sent, ends, i, x, c):
    if c == 1:
        return sent[i, x]
    if x == BX - 1:
        return ends[i, c // 2]
    return sent[i, (BX if c == 0 else 2 * BX - 1) + x]


def pack_kernel(sent, down, up, ends):
    row = lax.broadcasted_iota(jnp.int32, (ROWS, NZ), 0)

    def rebuild(i, _):
        low, high = sent[i, 2 * BX - 2], sent[i, 3 * BX - 3]
        low = pltpu.roll(low, BX - 1, 0)
        for x in range(BX - 1):
            low = jnp.where(row == x + 1, pltpu.roll(sent[i, BX + x], x + 1, 0), low)
            high = jnp.where(row == x, pltpu.roll(sent[i, 2 * BX - 1 + x], (x + 1) % 8, 0), high)
        ends[i, 0] = low
        ends[i, 1] = high
        return 0

    lax.fori_loop(0, SLICES, rebuild, 0, unroll=4)
    for n, tile in enumerate(TILES):
        for ref, near in ((down, True), (up, False)):
            value = None
            for i, d, part, rows, start in tile:
                part_of = own_tile(sent, ends, i, d - 1 if near else BX - d, part)
                shift = PLACE[i, d, part][1]
                if shift:
                    part_of = pltpu.roll(part_of, shift, 0)
                value = part_of if value is None else jnp.where(row >= start, part_of, value)
            ref[n] = value


def pack(sent):
    shape = jax.ShapeDtypeStruct((len(TILES), ROWS, NZ), jnp.float32)
    return pl.pallas_call(
        pack_kernel,
        out_shape=(shape, shape, jax.ShapeDtypeStruct((SLICES, 2, ROWS, NZ), jnp.float32)),
        in_specs=[VMEM],
        out_specs=(VMEM,) * 3,
        compiler_params=pltpu.CompilerParams(vmem_limit_bytes=8 << 20),
        name="pack",
    )(sent)


def strip_kernel(*refs):
    own = strip_of(lax.axis_index("tm"))
    parts, out = refs[:-1], refs[-1]
    lane, _ = iotas()
    for c in range(3):
        strip = own + (c - 1)
        scale = jnp.where((strip >= 0) & (strip < SLICES), float(STEPS), 0.0).astype(jnp.float32)
        strip = jnp.clip(strip, 0, SLICES - 1)
        h, s0 = lax.div(strip, Q), 2 * lax.rem(strip, Q)
        source = CHUNK * h + (lane >> 2)
        for n, ref in enumerate(parts):
            for x in range(HALF):
                turned = []
                for rz in range(Q):
                    halves = [
                        ref[HALF + x, pl.ds(8 * rz + s0 + ds, Q, stride=8 * Q), :]
                        for ds in range(2)
                    ]
                    both = jnp.concatenate(halves, axis=0)
                    turned.append(jnp.take_along_axis(both, source, axis=1))
                low = jnp.where((lane & 3) == 0, turned[0], turned[1])
                high = jnp.where((lane & 3) == 2, turned[2], turned[3])
                value = jnp.where((lane & 3) < 2, low, high)
                to = HALF - 1 - x if n in (0, 1, 4, 5) else x
                out[n * HALF + to, c] = scale * value


def strip_part(*parts):
    flat = [a.reshape(2 * HALF, NY, NZ) for a in parts]
    return pl.pallas_call(
        strip_kernel,
        out_shape=jax.ShapeDtypeStruct((3 * BX, 3, 8, NZ), jnp.float32),
        in_specs=[VMEM] * len(parts),
        out_specs=VMEM,
        compiler_params=pltpu.CompilerParams(vmem_limit_bytes=8 << 20),
        cost_estimate=pl.CostEstimate(flops=10**6, bytes_accessed=10**6, transcendentals=0),
        name="strip",
    )(*flat)


def sent_tile(refs, i, x, c):
    sent, ends, below, above = refs
    if x < BX or x >= 2 * BX:
        ref, d = (below, BX - x) if x < BX else (above, x - 2 * BX + 1)
        n, shift = PLACE[i, d, c]
        return pltpu.roll(ref[n], ROWS - shift, 0) if shift else ref[n]
    return own_tile(sent, ends, i, x - BX, c)


def coarse_steps(count, base, eta, refs, u_ref, k_ref, f_ref, out):
    lane, row = iotas()
    x_below = next_chip_exists()
    y_below, y_above = has_neighbours(strip_of(lax.axis_index("tm")), SLICES)
    once = one_trip()

    def mask(x, c):
        factors = []
        if x < BX:
            factors.append(x_below)
        if c != 1:
            factors.append(y_below if c == 0 else y_above)
        return factors[0] * factors[1] if len(factors) == 2 else (factors or [None])[0]

    def begin(x, _):
        for c in range(3):
            k_ref[x, c] = coeff(eta[x, c], u_ref[x, c])
        return 0

    lax.fori_loop(BX - count, 2 * BX + count, begin, 0, unroll=4)

    def stretch(n, left, planes):
        def body(_, carry):
            flux = [None] * 3
            for x in planes:
                far = max(BX - x, x - (2 * BX - 1), 0)
                tiles = (0, 1, 2) if left - far >= 1 else (1,)
                us = [u_ref[x, c] for c in range(3)]
                ks = [k_ref[x, c] for c in range(3)]
                ru = [pltpu.roll(u, 7, 0) for u in us]
                rk = [pltpu.roll(k, 7, 0) for k in ks]
                ups = []
                for c in range(max(tiles) + 1):
                    un, kn = ru[c], rk[c]
                    if c < 2:
                        un = jnp.where(row == 7, ru[c + 1], un)
                        kn = jnp.where(row == 7, rk[c + 1], kn)
                    ups.append((ks[c] + kn) * (un - us[c]))
                rolled = [pltpu.roll(v, 1, 0) for v in ups]
                for c in tiles:
                    low = rolled[c]
                    if c > 0:
                        low = jnp.where(row == 0, rolled[c - 1], low)
                    u0, k0 = us[c], ks[c]
                    x_up = (k0 + k_ref[x + 1, c]) * (u_ref[x + 1, c] - u0)
                    x_low = flux[c]
                    if x_low is None:
                        if x == BX - (left if c == 1 else left - 1):
                            x_low = (k0 + k_ref[x - 1, c]) * (u0 - u_ref[x - 1, c])
                        else:
                            x_low = f_ref[c]
                    flux[c] = x_up
                    new = (u0 + (x_up - x_low) + (ups[c] - low) + z_flux(u0, k0, lane)) + (
                        sent_tile(refs, base + n, x, c)
                    )
                    m = mask(x, c)
                    if m is not None:
                        new = m * new
                    if left > 0:
                        u_ref[x, c] = new
                        k_ref[x, c] = coeff(eta[x, c], new)
                    if c == 1 and far == 0:
                        out(n, x - BX, new)
            for c in range(3):
                if flux[c] is not None:
                    f_ref[c] = flux[c]
            return carry

        lax.fori_loop(0, once, body, 0)

    for n in range(1, count + 1):
        left = count - n
        planes = list(range(BX - left, 2 * BX + left))
        parts = -(-len(planes) * (3 if left else 1) // GROUP)
        size = -(-len(planes) // parts)
        for a in range(0, len(planes), size):
            stretch(n, left, planes[a : a + size])


def first_kernel(eta, sent, ends, below, above, out, u_ref, k_ref, f_ref):
    refs = (sent, ends, below, above)
    for x in range(BX - FIRST, 2 * BX + FIRST):
        for c in range(3):
            if BX <= x < 2 * BX or c == 1 or max(BX - x, x - 2 * BX + 1) < FIRST:
                u_ref[x, c] = sent_tile(refs, 0, x, c)
            else:
                u_ref[x, c] = jnp.zeros((8, NZ), jnp.float32)
    for x in range(BX):
        out[0, x] = sent[0, x]

    def put(n, x, value):
        out[n, x] = value

    coarse_steps(FIRST, 0, eta, refs, u_ref, k_ref, f_ref, put)


def second_kernel(
    eta, sent, ends, below, above, low_u, own_u, high_u, done, out, u_ref, k_ref, f_ref
):
    odd = is_mirrored()

    def true_plane(x):
        return jnp.where(odd, BX - 1 - x, x)

    for b, ref in enumerate((low_u, own_u, high_u)):
        for x in range(BX):
            for c in range(3):
                to = b * BX + (x if b == 1 else BX - 1 - x)
                u_ref[to, c] = ref[x, c * ROWS : (c + 1) * ROWS, :]
    for i in range(FIRST + 1):
        for x in range(BX):
            out[i, true_plane(x)] = done[i, x]
    refs = (sent, ends, below, above)

    def put(n, x, value):
        out[FIRST + n, true_plane(x)] = value

    coarse_steps(SLICES - 1 - FIRST, FIRST, eta, refs, u_ref, k_ref, f_ref, put)


def coarse_call(kernel, count, *operands):
    f32 = jnp.float32
    return pl.pallas_call(
        kernel,
        out_shape=jax.ShapeDtypeStruct((count, BX, ROWS, NZ), f32),
        in_specs=[VMEM] * len(operands),
        out_specs=VMEM,
        scratch_shapes=[
            pltpu.VMEM((3 * BX, 3, 8, NZ), f32),
            pltpu.VMEM((3 * BX, 3, 8, NZ), f32),
            pltpu.VMEM((3, 8, NZ), f32),
        ],
        compiler_params=pltpu.CompilerParams(vmem_limit_bytes=8 << 20),
    )(*operands)


def place_kernel(strips, out, sems):
    copies = [
        pltpu.make_async_copy(
            strips.at[j], out.at[:, pl.ds(ORDER[j] * ROWS, ROWS), :], sems.at[j]
        )
        for j in range(SLICES)
    ]
    for copy in copies:
        copy.start()
    for copy in copies:
        copy.wait()


def place(strips):
    return pl.pallas_call(
        place_kernel,
        out_shape=jax.ShapeDtypeStruct((BX, NY, NZ), jnp.float32),
        in_specs=[VMEM],
        out_specs=pl.BlockSpec(memory_space=HBM),
        scratch_shapes=[pltpu.SemaphoreType.DMA((SLICES,))],
        compiler_params=pltpu.CompilerParams(vmem_limit_bytes=4 << 20),
        name="place",
    )(strips)


def across(value):
    count = lax.axis_size("space")
    pairs = [(i, i + 1) for i in range(1, count - 1, 2)]
    return lax.ppermute(value, "space", pairs + [(b, a) for a, b in pairs])


def beside(value):
    pairs = [(i, i + 1) for i in range(0, lax.axis_size("space"), 2)]
    return lax.ppermute(value, "space", pairs + [(b, a) for a, b in pairs])


def with_strips(state):
    sides = []
    for first in (0, 1):
        pairs = [(ORDER[q], ORDER[q + 1]) for q in range(first, SLICES - 1, 2)]
        sides.append(lax.ppermute(state, "tm", pairs + [(b, a) for a, b in pairs]))
    even = lax.rem(strip_of(lax.axis_index("tm")), 2) == 0
    low = jnp.where(even, sides[1], sides[0])
    high = jnp.where(even, sides[0], sides[1])
    return jnp.concatenate([low, state, high], axis=1)


def per_device(start_values, regions, resistivity):
    own_a, own_b = own_part(start_values[0], regions, resistivity)
    low_near = across(own_a)
    low_far = across(own_b)
    high_near = beside(own_b)
    high_far = beside(own_a)
    sent = outer(low_far, high_far, *inner(low_near, own_a, own_b, high_near))
    sent = lax.all_to_all(sent, "tm", 0, 0)
    down, up, ends = pack(sent)
    below, above = across(down), beside(up)
    eta = strip_part(low_far, low_near, own_a, own_b, high_near, high_far)
    done = coarse_call(first_kernel, FIRST + 1, eta, sent, ends, below, above)
    strip = with_strips(done[FIRST])
    x_low, x_high = across(strip), beside(strip)
    ends = coarse_call(
        second_kernel, SLICES, eta, sent, ends, below, above, x_low, strip, x_high, done
    )
    result = lax.all_to_all(ends, "tm", 0, 0)
    return place(result)[None]


def solution(mesh):
    in_specs = (P("tm", "space", None, None), P("space", None, None), P())
    out_specs = P("tm", "space", None, None)
    return jax.shard_map(
        per_device, mesh=mesh, in_specs=in_specs, out_specs=out_specs, check_vma=False
    )
```

```python
import functools

import jax
import jax.numpy as jnp
from jax import lax
from jax.experimental import pallas as pl
from jax.experimental.pallas import tpu as pltpu
from jax.sharding import PartitionSpec as P

STEPS = 8
fine_step = 0.008

SIDE = 4
ORDER = [a * SIDE + (b if a % 2 == 0 else SIDE - 1 - b) for a in range(SIDE) for b in range(SIDE)]
BX = 8
HALF = BX // 2
NY = 128
NZ = 128
SLICES = 16
REGIONS = 4
ROWS = 8
SMEM = pl.BlockSpec(memory_space=pltpu.SMEM)
FIRST = 7
VMEM = pl.BlockSpec(memory_space=pltpu.VMEM)
HBM = pltpu.MemorySpace.HBM


def halo_depth(i):
    return FIRST - i if i <= FIRST else SLICES - 1 - i


def packed_tiles():
    tiles, groups = [], []
    for i in range(SLICES):
        depth = halo_depth(i)
        for d in range(1, depth + 1):
            tiles.append([(i, d, 1, ROWS, 0)])
            if depth > d:
                groups += [(depth - d, i, d, 0), (depth - d, i, d, 2)]
    used = []
    for rows, i, d, part in sorted(groups, reverse=True):
        for tile in used:
            start = sum(entry[3] for entry in tile)
            if start + rows <= ROWS:
                break
        else:
            tile, start = [], 0
            used.append(tile)
        tile.append((i, d, part, rows, start))
    return tiles + used


TILES = packed_tiles()
PLACE = {
    (i, d, part): (n, (start if part else start + rows) % ROWS)
    for n, tile in enumerate(TILES)
    for i, d, part, rows, start in tile
}
PARTS = NY // 8
LOAD = 3 * BX - 2
GROUP = 40


def coeff(eta, u):
    return eta * (2.0 - 1.0 / (1.0 + u * u))


def z_flux(u0, k0, lane):
    up = pltpu.roll(u0, NZ - 1, 1)
    kp = pltpu.roll(k0, NZ - 1, 1)
    edge = k0 * u0
    upper = jnp.where(lane == NZ - 1, -edge, (k0 + kp) * (up - u0))
    lower = jnp.where(lane == 0, edge, pltpu.roll(upper, 1, 1))
    return upper - lower


Q = 4
CHUNK = NZ // Q


def by_chunk(lane, values):
    low = jnp.where(lane < CHUNK, values[0], values[1])
    return jnp.where(lane < 2 * CHUNK, low, jnp.where(lane < 3 * CHUNK, values[2], values[3]))


def turn(h, rows):
    lane, _ = iotas()
    source = Q * (lane & (CHUNK - 1)) + (((lane >> 5) - h) & (Q - 1))
    return jnp.take_along_axis(rows, source, axis=1)


def gather_tiles(turned):
    lane, _ = iotas()
    tiles = []
    for rz in range(Q):
        tile = by_chunk(lane, [turned[(c - rz) % Q] for c in range(Q)])
        tiles.append(pltpu.roll(tile, NZ - CHUNK * rz, 1) if rz else tile)
    return tiles


def separate(tiles):
    lane, _ = iotas()
    turned = [pltpu.roll(t, CHUNK * rz, 1) if rz else t for rz, t in enumerate(tiles)]
    rows = []
    for h in range(Q):
        mixed = by_chunk(lane, [turned[(c - h) % Q] for c in range(Q)])
        source = CHUNK * (((lane & (Q - 1)) + h) & (Q - 1)) + (lane >> 2)
        rows.append(jnp.take_along_axis(mixed, source, axis=1))
    return rows


def rows_at(h, ry):
    return pl.ds(CHUNK * h + ry, 8, stride=Q)


def strip_of(tm):
    across, along = lax.div(tm, SIDE), lax.rem(tm, SIDE)
    return across * SIDE + jnp.where(lax.rem(across, 2) == 0, along, SIDE - 1 - along)


def iotas():
    shape = (8, NZ)
    return lax.broadcasted_iota(jnp.int32, shape, 1), lax.broadcasted_iota(jnp.int32, shape, 0)


def has_neighbours(index, count):
    below = jnp.where(index == 0, 0.0, 1.0).astype(jnp.float32)
    above = jnp.where(index == count - 1, 0.0, 1.0).astype(jnp.float32)
    return below, above


def is_mirrored():
    return lax.rem(lax.axis_index("space"), 2) == 1


def next_chip_exists():
    index = lax.axis_index("space")
    at_end = (index == 0) | (index == lax.axis_size("space") - 1)
    return jnp.where(at_end, 0.0, 1.0).astype(jnp.float32)


def one_trip():
    return jnp.where(lax.axis_index("space") < 0, 2, 1)


def own_kernel(h, start, regions, resistivity, out, *refs):
    start_v, regions_v, half_v, resistivity_s, sems = refs
    odd = is_mirrored()
    part = pl.ds(jnp.where(odd, 1 - h, h) * HALF, HALF)
    copies = (
        pltpu.make_async_copy(resistivity, resistivity_s, sems.at[0]),
        pltpu.make_async_copy(start.at[part], start_v, sems.at[1]),
        pltpu.make_async_copy(regions.at[part], regions_v, sems.at[2]),
    )
    for copy in copies:
        copy.start()
    for copy in copies:
        copy.wait()
    scaled = [resistivity_s[i] * jnp.float32(0.5 * fine_step) for i in range(REGIONS)]

    def first_pass(_, carry):
        for x in range(HALF):
            source = jnp.where(odd, HALF - 1 - x, x)
            for ry in range(Q):
                for g in range(Q):
                    where = rows_at(g, ry)
                    region = regions_v[source, where, :]
                    value = jnp.zeros((8, NZ), jnp.float32)
                    for i in range(REGIONS):
                        value = jnp.where(region == i, scaled[i], value)
                    half_v[x, Q * ry + g] = turn(g, start_v[source, where, :])
                    half_v[HALF + x, Q * ry + g] = turn(g, value)
        return carry

    def second_pass(n, _):
        for x in [HALF * n + q for q in range(HALF)]:
            for ry in range(Q):
                tiles = gather_tiles([half_v[x, Q * ry + g] for g in range(Q)])
                for rz in range(Q):
                    out[x, Q * ry + rz] = tiles[rz]
        return 0

    lax.fori_loop(0, one_trip(), first_pass, 0)
    lax.fori_loop(0, 2, second_pass, 0)


def own_part(h, start, regions, resistivity):
    hbm = pl.BlockSpec(memory_space=HBM)
    return pl.pallas_call(
        functools.partial(own_kernel, h),
        out_shape=jax.ShapeDtypeStruct((2 * HALF, PARTS, 8, NZ), jnp.float32),
        in_specs=[hbm] * 3,
        out_specs=VMEM,
        scratch_shapes=[
            pltpu.VMEM((HALF, NY, NZ), jnp.float32),
            pltpu.VMEM((HALF, NY, NZ), jnp.int32),
            pltpu.VMEM((2 * HALF, PARTS, 8, NZ), jnp.float32),
            pltpu.SMEM((REGIONS,), jnp.float32),
            pltpu.SemaphoreType.DMA((3,)),
        ],
        compiler_params=pltpu.CompilerParams(vmem_limit_bytes=8 << 20),
        cost_estimate=pl.CostEstimate(flops=10**6, bytes_accessed=10**6, transcendentals=0),
    )(*(pltpu.with_memory_space_constraint(a, HBM) for a in (start, regions, resistivity)))


class Fine:
    def __init__(self, u_ref, k_ref, e_ref, f_ref):
        self.u, self.k, self.e, self.f = u_ref, k_ref, e_ref, f_ref
        self.below = next_chip_exists()
        lane, sub = iotas()
        self.z_high, self.z_low = [(lane & (CHUNK - 1)) == v for v in (CHUNK - 1, 0)]
        self.y_high, self.y_low = sub == 7, sub == 0
        self.y_end = (sub == 7) & (lane >= NZ - CHUNK)
        self.y_start = (sub == 0) & (lane < CHUNK)

    def stage(self, ref, base, turn=False):
        def two(n, _):
            for x in (2 * n, 2 * n + 1):
                to = base + (HALF - 1 - x if turn else x)
                for r in range(PARTS):
                    u, e = ref[x, r], ref[HALF + x, r]
                    self.u[to, r] = u
                    self.e[to, r] = e
                    self.k[to, r] = coeff(e, u)
            return 0

        lax.fori_loop(0, HALF // 2, two, 0)

    def above_y(self, v):
        turned = pltpu.roll(pltpu.roll(v, NZ - CHUNK, 1), 7, 0)
        v = jnp.where(self.y_high, turned, pltpu.roll(v, 7, 0))
        return jnp.where(self.y_end, 0.0, v)

    def plane(self, x, emit, next_u=None, next_k=None):
        f_ref = self.f
        if next_u is None:
            next_u, next_k = self.u.at[x + 1], self.k.at[x + 1]

        def at(ry, rz):
            return self.u[x, Q * ry + rz], self.k[x, Q * ry + rz]

        z_ends, y_tops, y_lows = [], [], []
        for ry in range(Q):
            (u0, k0), (u3, k3) = at(ry, 0), at(ry, Q - 1)
            un, kn = pltpu.roll(u0, NZ - 1, 1), pltpu.roll(k0, NZ - 1, 1)
            top = jnp.where(self.z_high, -(k3 * u3), (k3 + kn) * (un - u3))
            low = jnp.where(self.z_low, k0 * u0, pltpu.roll(top, 1, 1))
            z_ends.append((low, top))
        for rz in range(Q):
            (u0, k0), (u3, k3) = at(0, rz), at(Q - 1, rz)
            top = (k3 + self.above_y(k0)) * (self.above_y(u0) - u3)
            turned = pltpu.roll(pltpu.roll(top, CHUNK, 1), 1, 0)
            low = jnp.where(self.y_low, turned, pltpu.roll(top, 1, 0))
            y_tops.append(top)
            y_lows.append(jnp.where(self.y_start, k0 * u0, low))
        for ry in range(Q):
            z_low, z_top = z_ends[ry]
            u0, k0 = at(ry, 0)
            for rz in range(Q):
                r = Q * ry + rz
                if rz < Q - 1:
                    u1, k1 = at(ry, rz + 1)
                    z_up = (k0 + k1) * (u1 - u0)
                else:
                    u1 = k1 = None
                    z_up = z_top
                if ry < Q - 1:
                    un, kn = at(ry + 1, rz)
                    y_up = (k0 + kn) * (un - u0)
                else:
                    y_up = y_tops[rz]
                x_up = (k0 + next_k[r]) * (next_u[r] - u0)
                x_low = f_ref[r]
                f_ref[r] = x_up
                total = (x_up - x_low) + (y_up - y_lows[rz]) + (z_up - z_low)
                emit(x, r, u0, total)
                y_lows[rz], z_low = y_up, z_up
                u0, k0 = u1, k1

    def begin(self, x, low_u, low_k):
        for r in range(PARTS):
            self.f[r] = (low_k[r] + self.k[x, r]) * (self.u[x, r] - low_u[r])

    def stretches(self, first, count, size, emit):
        def stretch(n, _):
            for q in range(size):
                self.plane(first + size * n + q, emit)
            return 0

        lax.fori_loop(0, count, stretch, 0)

    def step(self, first, count, size, emit):
        self.begin(first, self.u.at[first - 1], self.k.at[first - 1])
        self.stretches(first, count, size, emit)

    def keep(self, x, r, u0, total):
        inside = jnp.where(x < BX, self.below, jnp.float32(1.0))
        new = inside * (u0 + total)
        self.u[x, r] = new
        self.k[x, r] = coeff(self.e[x, r], new)


def to_rows(tiles, rows):
    for ry in range(Q):
        parts = separate([tiles[Q * ry + rz] for rz in range(Q)])
        for h in range(Q):
            rows[rows_at(h, ry), :] = parts[h]


def inner_kernel(low, own_a, own_b, high, u_ref, k_ref, e_ref, g_ref, save, f_ref):
    later = jnp.where(lax.axis_index("tm") == 0, 0.0, 1.0).astype(jnp.float32)
    fine = Fine(u_ref, k_ref, e_ref, f_ref)
    for n, ref in enumerate((low, own_a, own_b, high)):
        fine.stage(ref, (n + 1) * HALF, turn=n in (0, 3))

    def keep_first(x, r, u0, total):
        g_ref[x - HALF, r] = later * (u0 + STEPS * total)
        fine.keep(x, r, u0, total)

    def stow(t):
        for r in range(PARTS):
            save[0, t, r] = u_ref[HALF + t, r]
            save[1, t, r] = k_ref[HALF + t, r]
            save[2, t, r] = u_ref[5 * HALF - 1 - t, r]
            save[3, t, r] = k_ref[5 * HALF - 1 - t, r]

    for t in range(1, HALF + 1):
        stow(t)
        fine.step(HALF + t, 2, BX - t, keep_first if t == 1 else fine.keep)


def outer_kernel(low, high, u_in, k_in, e_in, g_ref, save, out, u_ref, k_ref, e_ref, f_ref, s_ref):
    fine = Fine(u_ref, k_ref, e_ref, f_ref)
    fine.stage(low, 0, turn=True)
    fine.stage(high, 5 * HALF, turn=True)

    once = one_trip()

    def wedges(t, _):
        fine.begin(t, u_ref.at[t - 1], k_ref.at[t - 1])

        def low_side(_, carry):
            for q in range(HALF - 1):
                fine.plane(t + q, fine.keep)
            fine.plane(t + HALF - 1, fine.keep, save.at[0, t], save.at[1, t])
            return carry

        lax.fori_loop(0, once, low_side, 0)
        fine.begin(5 * HALF - t, save.at[2, t], save.at[3, t])
        fine.stretches(5 * HALF - t, once, HALF, fine.keep)
        return 0

    lax.fori_loop(1, HALF + 1, wedges, 0)
    for t in range(HALF + 1, STEPS):
        fine.step(t, 2, 3 * HALF - t, fine.keep)

    def keep_last(x, r, u0, total):
        u_ref[x - BX, r] = (u0 + total) - g_ref[x - HALF, r]

    fine.step(BX, 2, HALF, keep_last)

    def natural(n, _):
        for q in range(HALF):
            to_rows(u_ref.at[HALF * n + q], s_ref.at[HALF * n + q])
        return 0

    lax.fori_loop(0, 2, natural, 0)

    row = lax.broadcasted_iota(jnp.int32, (ROWS, NZ), 0)
    for j in range(SLICES):

        def tile(x, c, j=j):
            strip = ORDER[j] + c - 1
            if 0 <= strip < SLICES:
                return s_ref[x, strip * ROWS : (strip + 1) * ROWS, :]
            return jnp.zeros((ROWS, NZ), jnp.float32)

        low_end, high_end = tile(BX - 1, 0), tile(BX - 1, 2)
        for x in range(BX):
            out[j, x] = tile(x, 1)
        for x in range(BX - 1):
            shift = BX - 1 - x
            low = pltpu.roll(low_end, shift, 0) if shift else low_end
            high = pltpu.roll(high_end, shift, 0) if shift else high_end
            out[j, BX + x] = jnp.where(row == 0, low, tile(x, 0))
            out[j, 2 * BX - 1 + x] = jnp.where(row == ROWS - 1, high, tile(x, 2))


GRID = jax.ShapeDtypeStruct((3 * BX + 1, PARTS, 8, NZ), jnp.float32)


def inner(low, own_a, own_b, high):
    f32 = jnp.float32
    return pl.pallas_call(
        inner_kernel,
        out_shape=(
            GRID,
            GRID,
            GRID,
            jax.ShapeDtypeStruct((4 * HALF, PARTS, 8, NZ), f32),
            jax.ShapeDtypeStruct((4, HALF + 1, PARTS, 8, NZ), f32),
        ),
        in_specs=[VMEM] * 4,
        out_specs=(VMEM,) * 5,
        scratch_shapes=[pltpu.VMEM((PARTS, 8, NZ), f32)],
        compiler_params=pltpu.CompilerParams(vmem_limit_bytes=16 << 20),
        cost_estimate=pl.CostEstimate(flops=10**8, bytes_accessed=10**7, transcendentals=0),
        name="inner",
    )(low, own_a, own_b, high)


def outer(low, high, u, k, e, g, save):
    f32 = jnp.float32
    return pl.pallas_call(
        outer_kernel,
        out_shape=(jax.ShapeDtypeStruct((SLICES, LOAD, ROWS, NZ), f32), GRID, GRID, GRID),
        in_specs=[VMEM] * 7,
        out_specs=(VMEM,) * 4,
        scratch_shapes=[pltpu.VMEM((PARTS, 8, NZ), f32), pltpu.VMEM((BX, NY, NZ), f32)],
        input_output_aliases={2: 1, 3: 2, 4: 3},
        compiler_params=pltpu.CompilerParams(vmem_limit_bytes=16 << 20),
        name="outer",
    )(low, high, u, k, e, g, save)[0]


def own_tile(sent, ends, i, x, c):
    if c == 1:
        return sent[i, x]
    if x == BX - 1:
        return ends[i, c // 2]
    return sent[i, (BX if c == 0 else 2 * BX - 1) + x]


def pack_kernel(sent, down, up, ends):
    row = lax.broadcasted_iota(jnp.int32, (ROWS, NZ), 0)

    def rebuild(i, _):
        low, high = sent[i, 2 * BX - 2], sent[i, 3 * BX - 3]
        low = pltpu.roll(low, BX - 1, 0)
        for x in range(BX - 1):
            low = jnp.where(row == x + 1, pltpu.roll(sent[i, BX + x], x + 1, 0), low)
            high = jnp.where(row == x, pltpu.roll(sent[i, 2 * BX - 1 + x], (x + 1) % 8, 0), high)
        ends[i, 0] = low
        ends[i, 1] = high
        return 0

    lax.fori_loop(0, SLICES, rebuild, 0, unroll=4)
    for n, tile in enumerate(TILES):
        for ref, near in ((down, True), (up, False)):
            value = None
            for i, d, part, rows, start in tile:
                part_of = own_tile(sent, ends, i, d - 1 if near else BX - d, part)
                shift = PLACE[i, d, part][1]
                if shift:
                    part_of = pltpu.roll(part_of, shift, 0)
                value = part_of if value is None else jnp.where(row >= start, part_of, value)
            ref[n] = value


def pack(sent):
    shape = jax.ShapeDtypeStruct((len(TILES), ROWS, NZ), jnp.float32)
    return pl.pallas_call(
        pack_kernel,
        out_shape=(shape, shape, jax.ShapeDtypeStruct((SLICES, 2, ROWS, NZ), jnp.float32)),
        in_specs=[VMEM],
        out_specs=(VMEM,) * 3,
        compiler_params=pltpu.CompilerParams(vmem_limit_bytes=8 << 20),
        name="pack",
    )(sent)


def strip_kernel(*refs):
    own = strip_of(lax.axis_index("tm"))
    parts, out = refs[:-1], refs[-1]
    lane, _ = iotas()
    for c in range(3):
        strip = own + (c - 1)
        scale = jnp.where((strip >= 0) & (strip < SLICES), float(STEPS), 0.0).astype(jnp.float32)
        strip = jnp.clip(strip, 0, SLICES - 1)
        h, s0 = lax.div(strip, Q), 2 * lax.rem(strip, Q)
        source = CHUNK * h + (lane >> 2)
        for n, ref in enumerate(parts):
            for x in range(HALF):
                turned = []
                for rz in range(Q):
                    halves = [
                        ref[HALF + x, pl.ds(8 * rz + s0 + ds, Q, stride=8 * Q), :]
                        for ds in range(2)
                    ]
                    both = jnp.concatenate(halves, axis=0)
                    turned.append(jnp.take_along_axis(both, source, axis=1))
                low = jnp.where((lane & 3) == 0, turned[0], turned[1])
                high = jnp.where((lane & 3) == 2, turned[2], turned[3])
                value = jnp.where((lane & 3) < 2, low, high)
                to = HALF - 1 - x if n in (0, 1, 4, 5) else x
                out[n * HALF + to, c] = scale * value


def strip_part(*parts):
    flat = [a.reshape(2 * HALF, NY, NZ) for a in parts]
    return pl.pallas_call(
        strip_kernel,
        out_shape=jax.ShapeDtypeStruct((3 * BX, 3, 8, NZ), jnp.float32),
        in_specs=[VMEM] * len(parts),
        out_specs=VMEM,
        compiler_params=pltpu.CompilerParams(vmem_limit_bytes=8 << 20),
        cost_estimate=pl.CostEstimate(flops=10**6, bytes_accessed=10**6, transcendentals=0),
        name="strip",
    )(*flat)


def sent_tile(refs, i, x, c):
    sent, ends, below, above = refs
    if x < BX or x >= 2 * BX:
        ref, d = (below, BX - x) if x < BX else (above, x - 2 * BX + 1)
        n, shift = PLACE[i, d, c]
        return pltpu.roll(ref[n], ROWS - shift, 0) if shift else ref[n]
    return own_tile(sent, ends, i, x - BX, c)


def coarse_steps(count, base, eta, refs, u_ref, k_ref, f_ref, out):
    lane, row = iotas()
    x_below = next_chip_exists()
    y_below, y_above = has_neighbours(strip_of(lax.axis_index("tm")), SLICES)
    once = one_trip()

    def mask(x, c):
        factors = []
        if x < BX:
            factors.append(x_below)
        if c != 1:
            factors.append(y_below if c == 0 else y_above)
        return factors[0] * factors[1] if len(factors) == 2 else (factors or [None])[0]

    def begin(x, _):
        for c in range(3):
            k_ref[x, c] = coeff(eta[x, c], u_ref[x, c])
        return 0

    lax.fori_loop(BX - count, 2 * BX + count, begin, 0, unroll=BX // 2 + count)

    def stretch(n, left, planes):
        def body(_, carry):
            flux = [None] * 3
            for x in planes:
                far = max(BX - x, x - (2 * BX - 1), 0)
                tiles = (0, 1, 2) if left - far >= 1 else (1,)
                us = [u_ref[x, c] for c in range(3)]
                ks = [k_ref[x, c] for c in range(3)]
                ru = [pltpu.roll(u, 7, 0) for u in us]
                rk = [pltpu.roll(k, 7, 0) for k in ks]
                ups = []
                for c in range(max(tiles) + 1):
                    un, kn = ru[c], rk[c]
                    if c < 2:
                        un = jnp.where(row == 7, ru[c + 1], un)
                        kn = jnp.where(row == 7, rk[c + 1], kn)
                    ups.append((ks[c] + kn) * (un - us[c]))
                rolled = [pltpu.roll(v, 1, 0) for v in ups]
                for c in tiles:
                    low = rolled[c]
                    if c > 0:
                        low = jnp.where(row == 0, rolled[c - 1], low)
                    u0, k0 = us[c], ks[c]
                    x_up = (k0 + k_ref[x + 1, c]) * (u_ref[x + 1, c] - u0)
                    x_low = flux[c]
                    if x_low is None:
                        if x == BX - (left if c == 1 else left - 1):
                            x_low = (k0 + k_ref[x - 1, c]) * (u0 - u_ref[x - 1, c])
                        else:
                            x_low = f_ref[c]
                    flux[c] = x_up
                    new = (u0 + (x_up - x_low) + (ups[c] - low) + z_flux(u0, k0, lane)) + (
                        sent_tile(refs, base + n, x, c)
                    )
                    m = mask(x, c)
                    if m is not None:
                        new = m * new
                    if left > 0:
                        u_ref[x, c] = new
                        k_ref[x, c] = coeff(eta[x, c], new)
                    if c == 1 and far == 0:
                        out(n, x - BX, new)
            for c in range(3):
                if flux[c] is not None:
                    f_ref[c] = flux[c]
            return carry

        lax.fori_loop(0, once, body, 0)

    for n in range(1, count + 1):
        left = count - n
        planes = list(range(BX - left, 2 * BX + left))
        parts = -(-len(planes) * (3 if left else 1) // GROUP)
        size = -(-len(planes) // parts)
        for a in range(0, len(planes), size):
            stretch(n, left, planes[a : a + size])


def first_kernel(eta, sent, ends, below, above, out, u_ref, k_ref, f_ref):
    refs = (sent, ends, below, above)
    for x in range(BX - FIRST, 2 * BX + FIRST):
        for c in range(3):
            if BX <= x < 2 * BX or c == 1 or max(BX - x, x - 2 * BX + 1) < FIRST:
                u_ref[x, c] = sent_tile(refs, 0, x, c)
            else:
                u_ref[x, c] = jnp.zeros((8, NZ), jnp.float32)
    for x in range(BX):
        out[0, x] = sent[0, x]

    def put(n, x, value):
        out[n, x] = value

    coarse_steps(FIRST, 0, eta, refs, u_ref, k_ref, f_ref, put)


def second_kernel(
    eta, sent, ends, below, above, low_u, own_u, high_u, done, out, u_ref, k_ref, f_ref
):
    odd = is_mirrored()

    def true_plane(x):
        return jnp.where(odd, BX - 1 - x, x)

    for b, ref in enumerate((low_u, own_u, high_u)):
        for x in range(BX):
            for c in range(3):
                to = b * BX + (x if b == 1 else BX - 1 - x)
                u_ref[to, c] = ref[x, c * ROWS : (c + 1) * ROWS, :]
    for i in range(FIRST + 1):
        for x in range(BX):
            out[i, true_plane(x)] = done[i, x]
    refs = (sent, ends, below, above)

    def put(n, x, value):
        out[FIRST + n, true_plane(x)] = value

    coarse_steps(SLICES - 1 - FIRST, FIRST, eta, refs, u_ref, k_ref, f_ref, put)


def coarse_call(kernel, count, *operands):
    f32 = jnp.float32
    return pl.pallas_call(
        kernel,
        out_shape=jax.ShapeDtypeStruct((count, BX, ROWS, NZ), f32),
        in_specs=[VMEM] * len(operands),
        out_specs=VMEM,
        scratch_shapes=[
            pltpu.VMEM((3 * BX, 3, 8, NZ), f32),
            pltpu.VMEM((3 * BX, 3, 8, NZ), f32),
            pltpu.VMEM((3, 8, NZ), f32),
        ],
        compiler_params=pltpu.CompilerParams(vmem_limit_bytes=8 << 20),
    )(*operands)


def place_kernel(strips, out, sems):
    copies = [
        pltpu.make_async_copy(
            strips.at[j], out.at[:, pl.ds(ORDER[j] * ROWS, ROWS), :], sems.at[j]
        )
        for j in range(SLICES)
    ]
    for copy in copies:
        copy.start()
    for copy in copies:
        copy.wait()


def place(strips):
    return pl.pallas_call(
        place_kernel,
        out_shape=jax.ShapeDtypeStruct((BX, NY, NZ), jnp.float32),
        in_specs=[VMEM],
        out_specs=pl.BlockSpec(memory_space=HBM),
        scratch_shapes=[pltpu.SemaphoreType.DMA((SLICES,))],
        compiler_params=pltpu.CompilerParams(vmem_limit_bytes=4 << 20),
        name="place",
    )(strips)


def across(value):
    count = lax.axis_size("space")
    pairs = [(i, i + 1) for i in range(1, count - 1, 2)]
    return lax.ppermute(value, "space", pairs + [(b, a) for a, b in pairs])


def beside(value):
    pairs = [(i, i + 1) for i in range(0, lax.axis_size("space"), 2)]
    return lax.ppermute(value, "space", pairs + [(b, a) for a, b in pairs])


def with_strips(state):
    sides = []
    for first in (0, 1):
        pairs = [(ORDER[q], ORDER[q + 1]) for q in range(first, SLICES - 1, 2)]
        sides.append(lax.ppermute(state, "tm", pairs + [(b, a) for a, b in pairs]))
    even = lax.rem(strip_of(lax.axis_index("tm")), 2) == 0
    low = jnp.where(even, sides[1], sides[0])
    high = jnp.where(even, sides[0], sides[1])
    return jnp.concatenate([low, state, high], axis=1)


def per_device(start_values, regions, resistivity):
    args = (start_values[0], regions, resistivity)
    own_a = own_part(0, *args)
    low_near = across(own_a)
    own_b = own_part(1, *args)
    low_far = across(own_b)
    high_near = beside(own_b)
    high_far = beside(own_a)
    sent = outer(low_far, high_far, *inner(low_near, own_a, own_b, high_near))
    sent = lax.all_to_all(sent, "tm", 0, 0)
    down, up, ends = pack(sent)
    below, above = across(down), beside(up)
    eta = strip_part(low_far, low_near, own_a, own_b, high_near, high_far)
    done = coarse_call(first_kernel, FIRST + 1, eta, sent, ends, below, above)
    strip = with_strips(done[FIRST])
    x_low, x_high = across(strip), beside(strip)
    ends = coarse_call(
        second_kernel, SLICES, eta, sent, ends, below, above, x_low, strip, x_high, done
    )
    result = lax.all_to_all(ends, "tm", 0, 0)
    return place(result)[None]


def solution(mesh):
    in_specs = (P("tm", "space", None, None), P("space", None, None), P())
    out_specs = P("tm", "space", None, None)
    return jax.shard_map(
        per_device, mesh=mesh, in_specs=in_specs, out_specs=out_specs, check_vma=False
    )
```

```python
import jax
import jax.numpy as jnp
from jax import lax
from jax.experimental import pallas as pl
from jax.experimental.pallas import tpu as pltpu
from jax.sharding import PartitionSpec as P

STEPS = 8
fine_step = 0.008

SIDE = 4
ORDER = [a * SIDE + (b if a % 2 == 0 else SIDE - 1 - b) for a in range(SIDE) for b in range(SIDE)]
BX = 8
HALF = BX // 2
NY = 128
NZ = 128
SLICES = 16
REGIONS = 4
ROWS = 8
SMEM = pl.BlockSpec(memory_space=pltpu.SMEM)
FIRST = 7
VMEM = pl.BlockSpec(memory_space=pltpu.VMEM)
HBM = pltpu.MemorySpace.HBM


def halo_depth(i):
    return FIRST - i if i <= FIRST else SLICES - 1 - i


def packed_tiles():
    tiles, groups = [], []
    for i in range(SLICES):
        depth = halo_depth(i)
        for d in range(1, depth + 1):
            tiles.append([(i, d, 1, ROWS, 0)])
            if depth > d:
                groups += [(depth - d, i, d, 0), (depth - d, i, d, 2)]
    used = []
    for rows, i, d, part in sorted(groups, reverse=True):
        for tile in used:
            start = sum(entry[3] for entry in tile)
            if start + rows <= ROWS:
                break
        else:
            tile, start = [], 0
            used.append(tile)
        tile.append((i, d, part, rows, start))
    return tiles + used


TILES = packed_tiles()
PLACE = {
    (i, d, part): (n, (start if part else start + rows) % ROWS)
    for n, tile in enumerate(TILES)
    for i, d, part, rows, start in tile
}
PARTS = NY // 8
LOAD = 3 * BX - 2
GROUP = 40


def coeff(eta, u):
    return eta * (2.0 - 1.0 / (1.0 + u * u))


def z_flux(u0, k0, lane):
    up = pltpu.roll(u0, NZ - 1, 1)
    kp = pltpu.roll(k0, NZ - 1, 1)
    edge = k0 * u0
    upper = jnp.where(lane == NZ - 1, -edge, (k0 + kp) * (up - u0))
    lower = jnp.where(lane == 0, edge, pltpu.roll(upper, 1, 1))
    return upper - lower


Q = 4
CHUNK = NZ // Q


def by_chunk(lane, values):
    low = jnp.where(lane < CHUNK, values[0], values[1])
    return jnp.where(lane < 2 * CHUNK, low, jnp.where(lane < 3 * CHUNK, values[2], values[3]))


def turn(h, rows):
    lane, _ = iotas()
    source = Q * (lane & (CHUNK - 1)) + (((lane >> 5) - h) & (Q - 1))
    return jnp.take_along_axis(rows, source, axis=1)


def gather_tiles(turned):
    lane, _ = iotas()
    tiles = []
    for rz in range(Q):
        tile = by_chunk(lane, [turned[(c - rz) % Q] for c in range(Q)])
        tiles.append(pltpu.roll(tile, NZ - CHUNK * rz, 1) if rz else tile)
    return tiles


def separate(tiles):
    lane, _ = iotas()
    turned = [pltpu.roll(t, CHUNK * rz, 1) if rz else t for rz, t in enumerate(tiles)]
    rows = []
    for h in range(Q):
        mixed = by_chunk(lane, [turned[(c - h) % Q] for c in range(Q)])
        source = CHUNK * (((lane & (Q - 1)) + h) & (Q - 1)) + (lane >> 2)
        rows.append(jnp.take_along_axis(mixed, source, axis=1))
    return rows


def rows_at(h, ry):
    return pl.ds(CHUNK * h + ry, 8, stride=Q)


def strip_of(tm):
    across, along = lax.div(tm, SIDE), lax.rem(tm, SIDE)
    return across * SIDE + jnp.where(lax.rem(across, 2) == 0, along, SIDE - 1 - along)


def iotas():
    shape = (8, NZ)
    return lax.broadcasted_iota(jnp.int32, shape, 1), lax.broadcasted_iota(jnp.int32, shape, 0)


def has_neighbours(index, count):
    below = jnp.where(index == 0, 0.0, 1.0).astype(jnp.float32)
    above = jnp.where(index == count - 1, 0.0, 1.0).astype(jnp.float32)
    return below, above


def is_mirrored():
    return lax.rem(lax.axis_index("space"), 2) == 1


def next_chip_exists():
    index = lax.axis_index("space")
    at_end = (index == 0) | (index == lax.axis_size("space") - 1)
    return jnp.where(at_end, 0.0, 1.0).astype(jnp.float32)


def one_trip():
    return jnp.where(lax.axis_index("space") < 0, 2, 1)


def convert(start_v, regions_v, scaled, half_v, out):
    odd = is_mirrored()

    def first_pass(_, carry):
        for x in range(HALF):
            source = jnp.where(odd, HALF - 1 - x, x)
            for ry in range(Q):
                for g in range(Q):
                    where = rows_at(g, ry)
                    region = regions_v[source, where, :]
                    value = jnp.zeros((8, NZ), jnp.float32)
                    for i in range(REGIONS):
                        value = jnp.where(region == i, scaled[i], value)
                    half_v[x, Q * ry + g] = turn(g, start_v[source, where, :])
                    half_v[HALF + x, Q * ry + g] = turn(g, value)
        return carry

    def second_pass(n, _):
        for x in [HALF * n + q for q in range(HALF)]:
            for ry in range(Q):
                tiles = gather_tiles([half_v[x, Q * ry + g] for g in range(Q)])
                for rz in range(Q):
                    out[x, Q * ry + rz] = tiles[rz]
        return 0

    lax.fori_loop(0, one_trip(), first_pass, 0)
    lax.fori_loop(0, 2, second_pass, 0)


def near_kernel(
    start, regions, resistivity, out, start_far, regions_far, table,
    start_v, regions_v, half_v, resistivity_s, sems,
):
    odd = is_mirrored()
    near, far = [pl.ds(jnp.where(odd, 1 - h, h) * HALF, HALF) for h in range(2)]
    copies = (
        pltpu.make_async_copy(resistivity, resistivity_s, sems.at[0]),
        pltpu.make_async_copy(start.at[near], start_v, sems.at[1]),
        pltpu.make_async_copy(regions.at[near], regions_v, sems.at[2]),
        pltpu.make_async_copy(start.at[far], start_far, sems.at[3]),
        pltpu.make_async_copy(regions.at[far], regions_far, sems.at[4]),
    )
    for copy in copies:
        copy.start()
    for copy in copies[:3]:
        copy.wait()
    scaled = [resistivity_s[i] * jnp.float32(0.5 * fine_step) for i in range(REGIONS)]
    for i in range(REGIONS):
        table[i] = jnp.full((8, NZ), scaled[i], jnp.float32)
    convert(start_v, regions_v, scaled, half_v, out)
    for copy in copies[3:]:
        copy.wait()


def far_kernel(start_v, regions_v, table, out, half_v):
    convert(start_v, regions_v, [table[i] for i in range(REGIONS)], half_v, out)


TILED = jax.ShapeDtypeStruct((2 * HALF, PARTS, 8, NZ), jnp.float32)


def near_half(start, regions, resistivity):
    f32 = jnp.float32
    shape = (HALF, NY, NZ)
    return pl.pallas_call(
        near_kernel,
        out_shape=(
            TILED,
            jax.ShapeDtypeStruct(shape, f32),
            jax.ShapeDtypeStruct(shape, jnp.int32),
            jax.ShapeDtypeStruct((REGIONS, 8, NZ), f32),
        ),
        in_specs=[pl.BlockSpec(memory_space=HBM)] * 3,
        out_specs=(VMEM,) * 4,
        scratch_shapes=[
            pltpu.VMEM(shape, f32),
            pltpu.VMEM(shape, jnp.int32),
            pltpu.VMEM(TILED.shape, f32),
            pltpu.SMEM((REGIONS,), f32),
            pltpu.SemaphoreType.DMA((5,)),
        ],
        compiler_params=pltpu.CompilerParams(vmem_limit_bytes=8 << 20),
        name="near",
    )(*(pltpu.with_memory_space_constraint(a, HBM) for a in (start, regions, resistivity)))


def far_half(start, regions, table):
    return pl.pallas_call(
        far_kernel,
        out_shape=TILED,
        in_specs=[VMEM] * 3,
        out_specs=VMEM,
        scratch_shapes=[pltpu.VMEM(TILED.shape, jnp.float32)],
        compiler_params=pltpu.CompilerParams(vmem_limit_bytes=8 << 20),
        cost_estimate=pl.CostEstimate(flops=10**6, bytes_accessed=10**6, transcendentals=0),
        name="far",
    )(start, regions, table)


class Fine:
    def __init__(self, u_ref, k_ref, e_ref, f_ref):
        self.u, self.k, self.e, self.f = u_ref, k_ref, e_ref, f_ref
        self.below = next_chip_exists()
        lane, sub = iotas()
        self.z_high, self.z_low = [(lane & (CHUNK - 1)) == v for v in (CHUNK - 1, 0)]
        self.y_high, self.y_low = sub == 7, sub == 0
        self.y_end = (sub == 7) & (lane >= NZ - CHUNK)
        self.y_start = (sub == 0) & (lane < CHUNK)

    def stage(self, ref, base, turn=False):
        def two(n, _):
            for x in (2 * n, 2 * n + 1):
                to = base + (HALF - 1 - x if turn else x)
                for r in range(PARTS):
                    u, e = ref[x, r], ref[HALF + x, r]
                    self.u[to, r] = u
                    self.e[to, r] = e
                    self.k[to, r] = coeff(e, u)
            return 0

        lax.fori_loop(0, HALF // 2, two, 0)

    def above_y(self, v):
        turned = pltpu.roll(pltpu.roll(v, NZ - CHUNK, 1), 7, 0)
        v = jnp.where(self.y_high, turned, pltpu.roll(v, 7, 0))
        return jnp.where(self.y_end, 0.0, v)

    def plane(self, x, emit, next_u=None, next_k=None):
        f_ref = self.f
        if next_u is None:
            next_u, next_k = self.u.at[x + 1], self.k.at[x + 1]

        def at(ry, rz):
            return self.u[x, Q * ry + rz], self.k[x, Q * ry + rz]

        z_ends, y_tops, y_lows = [], [], []
        for ry in range(Q):
            (u0, k0), (u3, k3) = at(ry, 0), at(ry, Q - 1)
            un, kn = pltpu.roll(u0, NZ - 1, 1), pltpu.roll(k0, NZ - 1, 1)
            top = jnp.where(self.z_high, -(k3 * u3), (k3 + kn) * (un - u3))
            low = jnp.where(self.z_low, k0 * u0, pltpu.roll(top, 1, 1))
            z_ends.append((low, top))
        for rz in range(Q):
            (u0, k0), (u3, k3) = at(0, rz), at(Q - 1, rz)
            top = (k3 + self.above_y(k0)) * (self.above_y(u0) - u3)
            turned = pltpu.roll(pltpu.roll(top, CHUNK, 1), 1, 0)
            low = jnp.where(self.y_low, turned, pltpu.roll(top, 1, 0))
            y_tops.append(top)
            y_lows.append(jnp.where(self.y_start, k0 * u0, low))
        for ry in range(Q):
            z_low, z_top = z_ends[ry]
            u0, k0 = at(ry, 0)
            for rz in range(Q):
                r = Q * ry + rz
                if rz < Q - 1:
                    u1, k1 = at(ry, rz + 1)
                    z_up = (k0 + k1) * (u1 - u0)
                else:
                    u1 = k1 = None
                    z_up = z_top
                if ry < Q - 1:
                    un, kn = at(ry + 1, rz)
                    y_up = (k0 + kn) * (un - u0)
                else:
                    y_up = y_tops[rz]
                x_up = (k0 + next_k[r]) * (next_u[r] - u0)
                x_low = f_ref[r]
                f_ref[r] = x_up
                total = (x_up - x_low) + (y_up - y_lows[rz]) + (z_up - z_low)
                emit(x, r, u0, total)
                y_lows[rz], z_low = y_up, z_up
                u0, k0 = u1, k1

    def begin(self, x, low_u, low_k):
        for r in range(PARTS):
            self.f[r] = (low_k[r] + self.k[x, r]) * (self.u[x, r] - low_u[r])

    def stretches(self, first, count, size, emit):
        def stretch(n, _):
            for q in range(size):
                self.plane(first + size * n + q, emit)
            return 0

        lax.fori_loop(0, count, stretch, 0)

    def step(self, first, count, size, emit):
        self.begin(first, self.u.at[first - 1], self.k.at[first - 1])
        self.stretches(first, count, size, emit)

    def keep(self, x, r, u0, total):
        inside = jnp.where(x < BX, self.below, jnp.float32(1.0))
        new = inside * (u0 + total)
        self.u[x, r] = new
        self.k[x, r] = coeff(self.e[x, r], new)


def to_rows(tiles, rows):
    for ry in range(Q):
        parts = separate([tiles[Q * ry + rz] for rz in range(Q)])
        for h in range(Q):
            rows[rows_at(h, ry), :] = parts[h]


def inner_kernel(low, own_a, own_b, high, u_ref, k_ref, e_ref, g_ref, save, f_ref):
    later = jnp.where(lax.axis_index("tm") == 0, 0.0, 1.0).astype(jnp.float32)
    fine = Fine(u_ref, k_ref, e_ref, f_ref)
    for n, ref in enumerate((low, own_a, own_b, high)):
        fine.stage(ref, (n + 1) * HALF, turn=n in (0, 3))

    def keep_first(x, r, u0, total):
        g_ref[x - HALF, r] = later * (u0 + STEPS * total)
        fine.keep(x, r, u0, total)

    def stow(t):
        for r in range(PARTS):
            save[0, t, r] = u_ref[HALF + t, r]
            save[1, t, r] = k_ref[HALF + t, r]
            save[2, t, r] = u_ref[5 * HALF - 1 - t, r]
            save[3, t, r] = k_ref[5 * HALF - 1 - t, r]

    for t in range(1, HALF + 1):
        stow(t)
        fine.step(HALF + t, 2, BX - t, keep_first if t == 1 else fine.keep)


def outer_kernel(low, high, u_in, k_in, e_in, g_ref, save, out, u_ref, k_ref, e_ref, f_ref, s_ref):
    fine = Fine(u_ref, k_ref, e_ref, f_ref)
    fine.stage(low, 0, turn=True)
    fine.stage(high, 5 * HALF, turn=True)

    once = one_trip()

    def wedges(t, _):
        fine.begin(t, u_ref.at[t - 1], k_ref.at[t - 1])

        def low_side(_, carry):
            for q in range(HALF - 1):
                fine.plane(t + q, fine.keep)
            fine.plane(t + HALF - 1, fine.keep, save.at[0, t], save.at[1, t])
            return carry

        lax.fori_loop(0, once, low_side, 0)
        fine.begin(5 * HALF - t, save.at[2, t], save.at[3, t])
        fine.stretches(5 * HALF - t, once, HALF, fine.keep)
        return 0

    lax.fori_loop(1, HALF + 1, wedges, 0)
    for t in range(HALF + 1, STEPS):
        fine.step(t, 2, 3 * HALF - t, fine.keep)

    def keep_last(x, r, u0, total):
        u_ref[x - BX, r] = (u0 + total) - g_ref[x - HALF, r]

    fine.step(BX, 2, HALF, keep_last)

    def natural(n, _):
        for q in range(HALF):
            to_rows(u_ref.at[HALF * n + q], s_ref.at[HALF * n + q])
        return 0

    lax.fori_loop(0, 2, natural, 0)

    row = lax.broadcasted_iota(jnp.int32, (ROWS, NZ), 0)
    for j in range(SLICES):

        def tile(x, c, j=j):
            strip = ORDER[j] + c - 1
            if 0 <= strip < SLICES:
                return s_ref[x, strip * ROWS : (strip + 1) * ROWS, :]
            return jnp.zeros((ROWS, NZ), jnp.float32)

        low_end, high_end = tile(BX - 1, 0), tile(BX - 1, 2)
        for x in range(BX):
            out[j, x] = tile(x, 1)
        for x in range(BX - 1):
            shift = BX - 1 - x
            low = pltpu.roll(low_end, shift, 0) if shift else low_end
            high = pltpu.roll(high_end, shift, 0) if shift else high_end
            out[j, BX + x] = jnp.where(row == 0, low, tile(x, 0))
            out[j, 2 * BX - 1 + x] = jnp.where(row == ROWS - 1, high, tile(x, 2))


GRID = jax.ShapeDtypeStruct((3 * BX + 1, PARTS, 8, NZ), jnp.float32)


def inner(low, own_a, own_b, high):
    f32 = jnp.float32
    return pl.pallas_call(
        inner_kernel,
        out_shape=(
            GRID,
            GRID,
            GRID,
            jax.ShapeDtypeStruct((4 * HALF, PARTS, 8, NZ), f32),
            jax.ShapeDtypeStruct((4, HALF + 1, PARTS, 8, NZ), f32),
        ),
        in_specs=[VMEM] * 4,
        out_specs=(VMEM,) * 5,
        scratch_shapes=[pltpu.VMEM((PARTS, 8, NZ), f32)],
        compiler_params=pltpu.CompilerParams(vmem_limit_bytes=16 << 20),
        cost_estimate=pl.CostEstimate(flops=10**8, bytes_accessed=10**7, transcendentals=0),
        name="inner",
    )(low, own_a, own_b, high)


def outer(low, high, u, k, e, g, save):
    f32 = jnp.float32
    return pl.pallas_call(
        outer_kernel,
        out_shape=(jax.ShapeDtypeStruct((SLICES, LOAD, ROWS, NZ), f32), GRID, GRID, GRID),
        in_specs=[VMEM] * 7,
        out_specs=(VMEM,) * 4,
        scratch_shapes=[pltpu.VMEM((PARTS, 8, NZ), f32), pltpu.VMEM((BX, NY, NZ), f32)],
        input_output_aliases={2: 1, 3: 2, 4: 3},
        compiler_params=pltpu.CompilerParams(vmem_limit_bytes=16 << 20),
        name="outer",
    )(low, high, u, k, e, g, save)[0]


def own_tile(sent, ends, i, x, c):
    if c == 1:
        return sent[i, x]
    if x == BX - 1:
        return ends[i, c // 2]
    return sent[i, (BX if c == 0 else 2 * BX - 1) + x]


def pack_kernel(sent, down, up, ends):
    row = lax.broadcasted_iota(jnp.int32, (ROWS, NZ), 0)

    def rebuild(i, _):
        low, high = sent[i, 2 * BX - 2], sent[i, 3 * BX - 3]
        low = pltpu.roll(low, BX - 1, 0)
        for x in range(BX - 1):
            low = jnp.where(row == x + 1, pltpu.roll(sent[i, BX + x], x + 1, 0), low)
            high = jnp.where(row == x, pltpu.roll(sent[i, 2 * BX - 1 + x], (x + 1) % 8, 0), high)
        ends[i, 0] = low
        ends[i, 1] = high
        return 0

    lax.fori_loop(0, SLICES, rebuild, 0, unroll=4)
    for n, tile in enumerate(TILES):
        for ref, near in ((down, True), (up, False)):
            value = None
            for i, d, part, rows, start in tile:
                part_of = own_tile(sent, ends, i, d - 1 if near else BX - d, part)
                shift = PLACE[i, d, part][1]
                if shift:
                    part_of = pltpu.roll(part_of, shift, 0)
                value = part_of if value is None else jnp.where(row >= start, part_of, value)
            ref[n] = value


def pack(sent):
    shape = jax.ShapeDtypeStruct((len(TILES), ROWS, NZ), jnp.float32)
    return pl.pallas_call(
        pack_kernel,
        out_shape=(shape, shape, jax.ShapeDtypeStruct((SLICES, 2, ROWS, NZ), jnp.float32)),
        in_specs=[VMEM],
        out_specs=(VMEM,) * 3,
        compiler_params=pltpu.CompilerParams(vmem_limit_bytes=8 << 20),
        name="pack",
    )(sent)


def strip_kernel(*refs):
    own = strip_of(lax.axis_index("tm"))
    parts, out = refs[:-1], refs[-1]
    lane, _ = iotas()
    for c in range(3):
        strip = own + (c - 1)
        scale = jnp.where((strip >= 0) & (strip < SLICES), float(STEPS), 0.0).astype(jnp.float32)
        strip = jnp.clip(strip, 0, SLICES - 1)
        h, s0 = lax.div(strip, Q), 2 * lax.rem(strip, Q)
        source = CHUNK * h + (lane >> 2)
        for n, ref in enumerate(parts):
            for x in range(HALF):
                turned = []
                for rz in range(Q):
                    halves = [
                        ref[HALF + x, pl.ds(8 * rz + s0 + ds, Q, stride=8 * Q), :]
                        for ds in range(2)
                    ]
                    both = jnp.concatenate(halves, axis=0)
                    turned.append(jnp.take_along_axis(both, source, axis=1))
                low = jnp.where((lane & 3) == 0, turned[0], turned[1])
                high = jnp.where((lane & 3) == 2, turned[2], turned[3])
                value = jnp.where((lane & 3) < 2, low, high)
                to = HALF - 1 - x if n in (0, 1, 4, 5) else x
                out[n * HALF + to, c] = scale * value


def strip_part(*parts):
    flat = [a.reshape(2 * HALF, NY, NZ) for a in parts]
    return pl.pallas_call(
        strip_kernel,
        out_shape=jax.ShapeDtypeStruct((3 * BX, 3, 8, NZ), jnp.float32),
        in_specs=[VMEM] * len(parts),
        out_specs=VMEM,
        compiler_params=pltpu.CompilerParams(vmem_limit_bytes=8 << 20),
        cost_estimate=pl.CostEstimate(flops=10**6, bytes_accessed=10**6, transcendentals=0),
        name="strip",
    )(*flat)


def sent_tile(refs, i, x, c):
    sent, ends, below, above = refs
    if x < BX or x >= 2 * BX:
        ref, d = (below, BX - x) if x < BX else (above, x - 2 * BX + 1)
        n, shift = PLACE[i, d, c]
        return pltpu.roll(ref[n], ROWS - shift, 0) if shift else ref[n]
    return own_tile(sent, ends, i, x - BX, c)


def coarse_steps(count, base, eta, refs, u_ref, k_ref, f_ref, out):
    lane, row = iotas()
    x_below = next_chip_exists()
    y_below, y_above = has_neighbours(strip_of(lax.axis_index("tm")), SLICES)
    once = one_trip()

    def mask(x, c):
        factors = []
        if x < BX:
            factors.append(x_below)
        if c != 1:
            factors.append(y_below if c == 0 else y_above)
        return factors[0] * factors[1] if len(factors) == 2 else (factors or [None])[0]

    def begin(x, _):
        for c in range(3):
            k_ref[x, c] = coeff(eta[x, c], u_ref[x, c])
        return 0

    lax.fori_loop(BX - count, 2 * BX + count, begin, 0, unroll=BX // 2 + count)

    def stretch(n, left, planes):
        def body(_, carry):
            flux = [None] * 3
            for x in planes:
                far = max(BX - x, x - (2 * BX - 1), 0)
                tiles = (0, 1, 2) if left - far >= 1 else (1,)
                us = [u_ref[x, c] for c in range(3)]
                ks = [k_ref[x, c] for c in range(3)]
                ru = [pltpu.roll(u, 7, 0) for u in us]
                rk = [pltpu.roll(k, 7, 0) for k in ks]
                ups = []
                for c in range(max(tiles) + 1):
                    un, kn = ru[c], rk[c]
                    if c < 2:
                        un = jnp.where(row == 7, ru[c + 1], un)
                        kn = jnp.where(row == 7, rk[c + 1], kn)
                    ups.append((ks[c] + kn) * (un - us[c]))
                rolled = [pltpu.roll(v, 1, 0) for v in ups]
                for c in tiles:
                    low = rolled[c]
                    if c > 0:
                        low = jnp.where(row == 0, rolled[c - 1], low)
                    u0, k0 = us[c], ks[c]
                    x_up = (k0 + k_ref[x + 1, c]) * (u_ref[x + 1, c] - u0)
                    x_low = flux[c]
                    if x_low is None:
                        if x == BX - (left if c == 1 else left - 1):
                            x_low = (k0 + k_ref[x - 1, c]) * (u0 - u_ref[x - 1, c])
                        else:
                            x_low = f_ref[c]
                    flux[c] = x_up
                    new = (u0 + (x_up - x_low) + (ups[c] - low) + z_flux(u0, k0, lane)) + (
                        sent_tile(refs, base + n, x, c)
                    )
                    m = mask(x, c)
                    if m is not None:
                        new = m * new
                    if left > 0:
                        u_ref[x, c] = new
                        k_ref[x, c] = coeff(eta[x, c], new)
                    if c == 1 and far == 0:
                        out(n, x - BX, new)
            for c in range(3):
                if flux[c] is not None:
                    f_ref[c] = flux[c]
            return carry

        lax.fori_loop(0, once, body, 0)

    for n in range(1, count + 1):
        left = count - n
        planes = list(range(BX - left, 2 * BX + left))
        parts = -(-len(planes) * (3 if left else 1) // GROUP)
        size = -(-len(planes) // parts)
        for a in range(0, len(planes), size):
            stretch(n, left, planes[a : a + size])


def first_kernel(eta, sent, ends, below, above, out, u_ref, k_ref, f_ref):
    refs = (sent, ends, below, above)
    for x in range(BX - FIRST, 2 * BX + FIRST):
        for c in range(3):
            if BX <= x < 2 * BX or c == 1 or max(BX - x, x - 2 * BX + 1) < FIRST:
                u_ref[x, c] = sent_tile(refs, 0, x, c)
            else:
                u_ref[x, c] = jnp.zeros((8, NZ), jnp.float32)
    for x in range(BX):
        out[0, x] = sent[0, x]

    def put(n, x, value):
        out[n, x] = value

    coarse_steps(FIRST, 0, eta, refs, u_ref, k_ref, f_ref, put)


def second_kernel(
    eta, sent, ends, below, above, low_u, own_u, high_u, done, out, u_ref, k_ref, f_ref
):
    odd = is_mirrored()

    def true_plane(x):
        return jnp.where(odd, BX - 1 - x, x)

    for b, ref in enumerate((low_u, own_u, high_u)):
        for x in range(BX):
            for c in range(3):
                to = b * BX + (x if b == 1 else BX - 1 - x)
                u_ref[to, c] = ref[x, c * ROWS : (c + 1) * ROWS, :]
    for i in range(FIRST + 1):
        for x in range(BX):
            out[i, true_plane(x)] = done[i, x]
    refs = (sent, ends, below, above)

    def put(n, x, value):
        out[FIRST + n, true_plane(x)] = value

    coarse_steps(SLICES - 1 - FIRST, FIRST, eta, refs, u_ref, k_ref, f_ref, put)


def coarse_call(kernel, count, *operands):
    f32 = jnp.float32
    return pl.pallas_call(
        kernel,
        out_shape=jax.ShapeDtypeStruct((count, BX, ROWS, NZ), f32),
        in_specs=[VMEM] * len(operands),
        out_specs=VMEM,
        scratch_shapes=[
            pltpu.VMEM((3 * BX, 3, 8, NZ), f32),
            pltpu.VMEM((3 * BX, 3, 8, NZ), f32),
            pltpu.VMEM((3, 8, NZ), f32),
        ],
        compiler_params=pltpu.CompilerParams(vmem_limit_bytes=8 << 20),
    )(*operands)


def place_kernel(strips, out, sems):
    copies = [
        pltpu.make_async_copy(
            strips.at[j], out.at[:, pl.ds(ORDER[j] * ROWS, ROWS), :], sems.at[j]
        )
        for j in range(SLICES)
    ]
    for copy in copies:
        copy.start()
    for copy in copies:
        copy.wait()


def place(strips):
    return pl.pallas_call(
        place_kernel,
        out_shape=jax.ShapeDtypeStruct((BX, NY, NZ), jnp.float32),
        in_specs=[VMEM],
        out_specs=pl.BlockSpec(memory_space=HBM),
        scratch_shapes=[pltpu.SemaphoreType.DMA((SLICES,))],
        compiler_params=pltpu.CompilerParams(vmem_limit_bytes=4 << 20),
        name="place",
    )(strips)


def across(value):
    count = lax.axis_size("space")
    pairs = [(i, i + 1) for i in range(1, count - 1, 2)]
    return lax.ppermute(value, "space", pairs + [(b, a) for a, b in pairs])


def beside(value):
    pairs = [(i, i + 1) for i in range(0, lax.axis_size("space"), 2)]
    return lax.ppermute(value, "space", pairs + [(b, a) for a, b in pairs])


def with_strips(state):
    sides = []
    for first in (0, 1):
        pairs = [(ORDER[q], ORDER[q + 1]) for q in range(first, SLICES - 1, 2)]
        sides.append(lax.ppermute(state, "tm", pairs + [(b, a) for a, b in pairs]))
    even = lax.rem(strip_of(lax.axis_index("tm")), 2) == 0
    low = jnp.where(even, sides[1], sides[0])
    high = jnp.where(even, sides[0], sides[1])
    return jnp.concatenate([low, state, high], axis=1)


def per_device(start_values, regions, resistivity):
    own_a, *rest = near_half(start_values[0], regions, resistivity)
    low_near = across(own_a)
    own_b = far_half(*rest)
    low_far = across(own_b)
    high_near = beside(own_b)
    high_far = beside(own_a)
    sent = outer(low_far, high_far, *inner(low_near, own_a, own_b, high_near))
    sent = lax.all_to_all(sent, "tm", 0, 0)
    down, up, ends = pack(sent)
    below, above = across(down), beside(up)
    eta = strip_part(low_far, low_near, own_a, own_b, high_near, high_far)
    done = coarse_call(first_kernel, FIRST + 1, eta, sent, ends, below, above)
    strip = with_strips(done[FIRST])
    x_low, x_high = across(strip), beside(strip)
    ends = coarse_call(
        second_kernel, SLICES, eta, sent, ends, below, above, x_low, strip, x_high, done
    )
    result = lax.all_to_all(ends, "tm", 0, 0)
    return place(result)[None]


def solution(mesh):
    in_specs = (P("tm", "space", None, None), P("space", None, None), P())
    out_specs = P("tm", "space", None, None)
    return jax.shard_map(
        per_device, mesh=mesh, in_specs=in_specs, out_specs=out_specs, check_vma=False
    )
```
